128 devices in a mesh: patch: 32 (over y, z, core), visit: 4 (over x).
Axes of the slice: x: 4, y: 4, z: 4, core: 2. Of those that a mesh axis runs over, the one named last changes fastest.
Arguments:
- ccd_rows: float32 [32, 1024, 4096], P('visit', 'patch'), may hold values from -6 to 6
- tract_row: int32 [32, 1024], P('visit', 'patch'), may hold values from 0 to 1023, as said below
- warp_taps: float32 [32, 32, 8, 4096], P('visit', 'patch'), may hold values from -0.25 to 0.5
- warp_shift: int32 [32, 32, 4096], P('visit', 'patch'), may hold values from -64 to 56
- basis_rows: float32 [9, 21], replicated, may hold values from -1 to 1
- basis_cols: float32 [9, 21], replicated, may hold values from -1 to 1
- coef_table: float32 [32, 32, 9, 32], P('visit', 'patch'), may hold values from -2 to 2
- grid_index: int32 [32, 4096], P('patch'), may hold values from 0 to 31
- template: float32 [1024, 4096], P('patch'), may hold values from -6 to 6
- visit_weight: float32 [32], replicated, may hold values from 0.2 to 5
Outputs:
- difference: float32 [32, 1024, 4096], P('visit', 'patch')
- coadd: float32 [1024, 4096], P(('patch', 'visit'))
The draws below stay inside these ranges and needn't reach their ends.
Inputs may be any that keep to these rules, and one draw needn't show every extreme that they name: In each visit, tract_row is a permutation of the tract rows. For visit q with group g = q // 8 and l = q % 8, a value v among the rows held by patch index s (rows s * 32 to s * 32 + 31) lies in patch v // 32 = s + o_g - l + (v % 32) // 2 modulo the patch axis's size, with o_g one integer for all visits of group g. So the rows of one visit held on one device reach a patch either 2 times or never, with distinct v % 2, and the rows of one device reach one patch at most min(8, 16) * 2 times, exactly that often for one patch.
All inputs are finite; a program needn't handle non-finite values.
Results may differ from the reference program's by a relative error of at most 0.0003.
Values sent between devices are 32-bit elements; how exact they have to be, the bound alone decides.
A program may use at most 128 MiB of HBM per device.

```python
import math
import jax
import jax.numpy as jnp
from jax import lax

W = 4096
PROWS = 32
VIS_DEV = 8
TAPS = 8
KSIZE = 21
NBASIS = 9
GRID = 32
HALF = 10
RUN = 2
VISITS = 32
TROWS = 1024
N_PATCH = 32


def shuffle_rows(sub_key):
    return jax.random.permutation(sub_key, PROWS)


def draw_tract_row(key, part):
    base_key, order_key = jax.random.split(key)
    offsets = jax.random.randint(base_key, (VISITS // VIS_DEV,), 0, N_PATCH)
    row_keys = jax.random.split(order_key, VISITS * N_PATCH)
    orders = jax.vmap(shuffle_rows)(row_keys).reshape(VISITS, N_PATCH, PROWS)
    visit_ids = jnp.arange(VISITS)[:, None, None]
    local_visit = visit_ids % VIS_DEV
    group_of = visit_ids // VIS_DEV
    sources = jnp.arange(N_PATCH)[None, :, None]
    run_index = orders // RUN
    patch_of = (sources + offsets[group_of] - local_visit + run_index) % N_PATCH
    return (patch_of * PROWS + orders).reshape(VISITS, TROWS).astype(jnp.int32)


def place_ends(entries, rng, low, high):
    longest = entries.shape.index(max(entries.shape))
    spots = []
    for shift in (0, 1):
        where = [jax.random.randint(jax.random.fold_in(rng, axis), (), 0, length) for axis, length in enumerate(entries.shape)]
        where[longest] = (where[longest] + shift) % entries.shape[longest]
        spots.append(tuple(where))
    return entries.at[spots[0]].set(low).at[spots[1]].set(high)


def steps_of(rng, extent, shards, least, top_value):
    level, own = 1.0, jax.random.fold_in(rng, 6)
    for dim, shards_of in shards:
        heights = jnp.exp(jax.random.uniform(jax.random.fold_in(own, dim), (shards_of,), jnp.float32, least / len(shards), top_value / len(shards)))
        level = level * jnp.repeat(heights, extent[dim] // shards_of).reshape([-1 if axis == dim else 1 for axis in range(len(extent))])
    return level


def scatter_about(stream_key, extent, deviation, most, shards=(), kind=jnp.bfloat16):
    factor_of = steps_of(stream_key, extent, shards, -0.22, 0.18) if shards else 1.0
    array = jax.random.normal(stream_key, extent, jnp.float32) * deviation * factor_of
    return jnp.minimum(jnp.maximum(array, -most), most).astype(kind)


def setup_inputs(seed: int = 0) -> dict:
    splits = jax.random.split(jax.random.key(seed), 11)
    ccd_rows = scatter_about(splits[0], (VISITS, TROWS, W), 1.0, 6.0, ((0, 4), (1, 32)), jnp.float32)
    tract_row = draw_tract_row(jax.random.fold_in(splits[10], 71), 0)
    warp_taps = jnp.clip(-0.25 + 0.75 * jax.random.uniform(splits[2], (VISITS, N_PATCH, TAPS, W), jnp.float32) ** steps_of(splits[2], (VISITS, N_PATCH, TAPS, W), ((0, 4), (1, 32)), -0.2, 0.2), -0.25, 0.5)
    warp_shift = place_ends(jax.random.randint(splits[3], (VISITS, N_PATCH, W), -64, 57), jax.random.fold_in(splits[3], 1), -64, 56).astype(jnp.int32)
    basis_rows = scatter_about(splits[4], (NBASIS, KSIZE), 0.2, 1.0, (), jnp.float32)
    basis_cols = scatter_about(splits[5], (NBASIS, KSIZE), 0.2, 1.0, (), jnp.float32)
    coef_table = scatter_about(splits[6], (VISITS, N_PATCH, NBASIS, GRID), 0.35, 2.0, ((0, 4), (1, 32)), jnp.float32)
    grid_index = place_ends(jax.random.randint(splits[7], (N_PATCH, W), 0, GRID), jax.random.fold_in(splits[7], 1), 0, GRID - 1).astype(jnp.int32)
    template = scatter_about(splits[8], (TROWS, W), 1.0, 6.0, ((0, 32),), jnp.float32)
    visit_weight = jnp.clip(jnp.exp(jax.random.uniform(splits[9], (VISITS,), jnp.float32, math.log(0.2), math.log(5.0))), 0.2, 5.0)
    return {"ccd_rows": ccd_rows, "tract_row": tract_row, "warp_taps": warp_taps, "warp_shift": warp_shift, "basis_rows": basis_rows, "basis_cols": basis_cols, "coef_table": coef_table, "grid_index": grid_index, "template": template, "visit_weight": visit_weight}


def warp_patches(image, taps, shift):
    columns = jnp.arange(W)[None, :]
    result = jnp.zeros(image.shape, jnp.float32)
    for lag in range(TAPS):
        source = columns + shift + lag
        inside = (source >= 0) & (source < W)
        index = jnp.broadcast_to(jnp.clip(source, 0, W - 1).astype(jnp.int32)[:, None, :], image.shape)
        picked = jnp.take_along_axis(image, index, axis=2)
        result = result + taps[:, lag][:, None, :] * jnp.where(inside[:, None, :], picked, 0.0)
    return result


def reference(ccd_rows, tract_row, warp_taps, warp_shift, basis_rows, basis_cols, coef_table, grid_index, template, visit_weight):
    row_kernel = basis_rows[:, None, :, None]
    col_kernel = basis_cols[:, None, None, :]

    def one_visit(total, items):
        row_data, places, taps, shift, coefs, weight = items
        image = jnp.zeros((TROWS, W), jnp.float32).at[places.astype(jnp.int32)].set(row_data)
        warped = warp_patches(image.reshape(N_PATCH, PROWS, W), taps, shift).reshape(1, 1, TROWS, W)
        vertical = lax.conv_general_dilated(warped, row_kernel, (1, 1), ((HALF, HALF), (0, 0)), precision=lax.Precision.HIGHEST)
        smoothed = lax.conv_general_dilated(vertical, col_kernel, (1, 1), ((0, 0), (HALF, HALF)), feature_group_count=NBASIS, precision=lax.Precision.HIGHEST)
        index = jnp.broadcast_to(grid_index.astype(jnp.int32)[:, None, :], (N_PATCH, NBASIS, W))
        coefficient = jnp.take_along_axis(coefs, index, axis=2)
        matched = jnp.einsum("bpyx,pbx->pyx", smoothed.reshape(NBASIS, N_PATCH, PROWS, W), coefficient, precision=lax.Precision.HIGHEST).reshape(TROWS, W)
        return total + weight * matched, matched - template

    total, difference = lax.scan(one_visit, jnp.zeros((TROWS, W), jnp.float32), (ccd_rows, tract_row, warp_taps, warp_shift, coef_table, visit_weight))
    coadd = total / jnp.sum(visit_weight)
    return difference, coadd
```

```python
import functools

import jax
import jax.numpy as jnp
from jax import lax
from jax.experimental import pallas as pl
from jax.experimental.pallas import tpu as pltpu
from jax.sharding import PartitionSpec as P

lane = 128
half_lane = 64
group = 1024
chunks = (2, 2, 2, 2)
bf16 = jnp.bfloat16


def pack_kernel(first, places_ref, rows_ref, sent_ref, sem):
    count = sent_ref.shape[1]
    patch_rows = places_ref.shape[1]

    def step(item, carry):
        local = item // patch_rows
        row = item % patch_rows
        place = places_ref[first + local, row]
        pltpu.make_async_copy(
            rows_ref.at[first + local, row // 8, :, row % 8, :],
            sent_ref.at[place // patch_rows, local, :, place % 2, :],
            sem,
        ).start()
        return carry

    lax.fori_loop(0, count * patch_rows, step, 0)
    everything = rows_ref.at[pl.ds(first, count)]
    pltpu.make_async_copy(everything, everything, sem).wait()


def pack_rows(first, count, tract_row, tiled_rows, patches):
    return pl.pallas_call(
        functools.partial(pack_kernel, first),
        out_shape=jax.ShapeDtypeStruct(
            (patches, count, tiled_rows.shape[2], 2, lane), jnp.float32
        ),
        in_specs=[
            pl.BlockSpec(memory_space=pltpu.SMEM),
            pl.BlockSpec(memory_space=pl.ANY),
        ],
        out_specs=pl.BlockSpec(memory_space=pl.ANY),
        scratch_shapes=[pltpu.SemaphoreType.DMA],
        cost_estimate=pl.CostEstimate(flops=0, bytes_accessed=8 * count << 20, transcendentals=0),
        name="pack_rows",
    )(tract_row, tiled_rows)


def pick_lanes(cells, index):
    return jnp.take_along_axis(cells, index, axis=1, mode="promise_in_bounds")


def warp_kernel(
    first, turn_ref, got_ref, taps_ref, shift_ref, warped_ref, head_ref, tail_ref, image, sems
):
    patches, count, tiles = got_ref.shape[:3]
    pairs = warped_ref.shape[1] // 2
    for local in range(count):

        def fetch(pair, carry):
            source = (turn_ref[0] + first + local - pair + 2 * patches) % patches
            pltpu.make_async_copy(
                got_ref.at[source, local],
                image.at[local, pair // 4, pl.ds(1, tiles), pl.ds(2 * (pair % 4), 2), :],
                sems.at[local],
            ).start()
            return carry

        lax.fori_loop(0, pairs, fetch, 0)
    blank = jnp.zeros((8, lane), jnp.float32)
    groups = image.shape[1]
    for local in range(count):
        for g in range(groups):
            image[local, g, 0] = blank
            image[local, g, tiles + 1] = blank
    columns = lax.broadcasted_iota(jnp.int32, (8, lane), 1) + half_lane
    for local in range(count):
        whole = image.at[local, :, pl.ds(1, tiles)]
        pltpu.make_async_copy(whole, whole, sems.at[local]).wait()

        def tile_step(u, carry):
            window = pl.ds(pl.multiple_of(u * lane, lane), lane)
            base = columns + jnp.broadcast_to(shift_ref[local, :, window], (8, lane))
            totals = [blank] * groups
            lows = [image[local, g, u] for g in range(groups)]
            highs = [image[local, g, u + 1] for g in range(groups)]
            for k in range(taps_ref.shape[1]):
                spot = base + k
                index = spot & (lane - 1)
                upper = spot >= lane
                tap = jnp.broadcast_to(taps_ref[local, k : k + 1, window], (8, lane))
                for g in range(groups):
                    picked = jnp.where(
                        upper, pick_lanes(highs[g], index), pick_lanes(lows[g], index)
                    )
                    totals[g] = totals[g] + tap * picked
            for g in range(groups):
                warped_ref[local, 8 * g : 8 * g + 8, window] = totals[g]
            return carry

        lax.fori_loop(0, tiles + 1, tile_step, 0)
        edge = head_ref.shape[1]
        last = warped_ref.shape[1] - 2 * edge
        for i in range(edge):
            head_ref[local, i] = warped_ref[local, 2 * i : 2 * i + 2, :]
            tail_ref[local, i] = warped_ref[local, last + 2 * i : last + 2 * i + 2, :]


def warp_rows(first, turn, got, taps, shift, patch_rows, edge):
    patches, count, tiles = got.shape[:3]
    width = (tiles + 1) * lane
    shapes = (
        jax.ShapeDtypeStruct((count, patch_rows, width), jnp.float32),
        jax.ShapeDtypeStruct((count, edge, 2, width), jnp.float32),
        jax.ShapeDtypeStruct((count, edge, 2, width), jnp.float32),
    )
    part = first // count
    return pl.pallas_call(
        functools.partial(warp_kernel, first),
        out_shape=shapes,
        grid=(1,),
        in_specs=[
            pl.BlockSpec(memory_space=pltpu.SMEM),
            pl.BlockSpec(memory_space=pl.ANY),
            pl.BlockSpec((count,) + taps.shape[1:], lambda i: (part, 0, 0)),
            pl.BlockSpec((count,) + shift.shape[1:], lambda i: (part, 0, 0)),
        ],
        out_specs=[
            pl.BlockSpec(shapes[0].shape, lambda i: (0, 0, 0)),
            pl.BlockSpec(shapes[1].shape, lambda i: (0, 0, 0, 0)),
            pl.BlockSpec(shapes[2].shape, lambda i: (0, 0, 0, 0)),
        ],
        scratch_shapes=[
            pltpu.VMEM((count, patch_rows // 8, tiles + 2, 8, lane), jnp.float32),
            pltpu.SemaphoreType.DMA((count,)),
        ],
        compiler_params=pltpu.CompilerParams(vmem_limit_bytes=32 << 20),
        cost_estimate=pl.CostEstimate(flops=0, bytes_accessed=5 * count << 20, transcendentals=0),
        name="warp_rows",
    )(turn, got, taps, shift)


def two_parts(values):
    high = values.astype(bf16)
    low = (values - high.astype(jnp.float32)).astype(bf16)
    return high, low


def match_kernel(
    first,
    fresh,
    weight_ref,
    warped_ref,
    above_ref,
    below_ref,
    down_ref,
    across_ref,
    coef_ref,
    template_ref,
    before_ref,
    _,
    difference_ref,
    total_ref,
    stack,
    high_ref,
    low_ref,
):
    patch_rows = warped_ref.shape[1]
    edge = above_ref.shape[1]
    bases = coef_ref.shape[1]
    tiles = group // lane

    @pl.when(pl.program_id(1) == 0)
    def _():
        stack[:patch_rows, :] = warped_ref[0]
        for i in range(edge):
            at = patch_rows + 2 * i
            stack[at : at + 2, :] = above_ref[0, i]
            at = at + 2 * edge
            stack[at : at + 2, :] = below_ref[0, i]
        used = patch_rows + 4 * edge
        stack[used:, :] = jnp.zeros((stack.shape[0] - used, stack.shape[1]), jnp.float32)

    start = pl.multiple_of(pl.program_id(1) * group, group)
    high, low = two_parts(stack[:, pl.ds(start, group + lane)])
    vertical = jnp.dot(
        down_ref[...],
        jnp.concatenate([high, low, high], axis=0),
        preferred_element_type=jnp.float32,
    )
    high_ref[...], low_ref[...] = two_parts(vertical)

    def windows(ref, b):
        rows = slice(b * patch_rows, (b + 1) * patch_rows)
        return jnp.concatenate(
            [ref[rows, lane * i : lane * (i + 2)] for i in range(tiles)], axis=0
        )

    matched = jnp.zeros((tiles * patch_rows, lane), jnp.float32)
    for b in range(bases):
        both = jnp.dot(windows(high_ref, b), across_ref[b], preferred_element_type=jnp.float32)
        rest = jnp.dot(
            windows(low_ref, b), across_ref[b, :, :lane], preferred_element_type=jnp.float32
        )
        smoothed = both[:, :lane] + both[:, lane:] + rest
        scale = jnp.concatenate(
            [
                jnp.broadcast_to(
                    coef_ref[0, b : b + 1, lane * i : lane * (i + 1)], (patch_rows, lane)
                )
                for i in range(tiles)
            ],
            axis=0,
        )
        matched = matched + scale * smoothed
    weight = weight_ref[first + pl.program_id(0)]
    for i in range(tiles):
        piece = matched[i * patch_rows : (i + 1) * patch_rows]
        here = slice(lane * i, lane * (i + 1))
        columns = pl.ds(pl.multiple_of(start + lane * i, lane), lane)
        difference_ref[0, :, here] = piece - template_ref[:, columns]
        if fresh:

            @pl.when(pl.program_id(0) == 0)
            def _():
                total_ref[:, columns] = weight * piece

        else:

            @pl.when(pl.program_id(0) == 0)
            def _():
                total_ref[:, columns] = before_ref[:, columns] + weight * piece

        @pl.when(pl.program_id(0) > 0)
        def _():
            total_ref[:, columns] = total_ref[:, columns] + weight * piece


def match_rows(
    first, weights, warped, above, below, down, across, coefs, template, before, difference
):
    count, patch_rows, width = warped.shape
    edge = above.shape[1]
    visits, bases, row_width = coefs.shape
    fresh = before is None
    if fresh:
        before = template
    extra, aliases = [], {}
    if difference is not None:
        extra, aliases = [difference], {9: 0}
    kernel = functools.partial(match_kernel, first, fresh)
    if difference is None:

        def body(*refs):
            kernel(*refs[:9], None, *refs[9:])

    else:
        body = kernel
    rows_spec = pl.BlockSpec(template.shape, lambda q, c: (0, 0))
    return pl.pallas_call(
        body,
        out_shape=(
            jax.ShapeDtypeStruct((visits, patch_rows, row_width), jnp.float32),
            jax.ShapeDtypeStruct(template.shape, jnp.float32),
        ),
        grid=(count, row_width // group),
        in_specs=[
            pl.BlockSpec(memory_space=pltpu.SMEM),
            pl.BlockSpec((1, patch_rows, width), lambda q, c: (q, 0, 0)),
            pl.BlockSpec((1, edge, 2, width), lambda q, c: (q, 0, 0, 0)),
            pl.BlockSpec((1, edge, 2, width), lambda q, c: (q, 0, 0, 0)),
            pl.BlockSpec(down.shape, lambda q, c: (0, 0)),
            pl.BlockSpec(across.shape, lambda q, c: (0, 0, 0)),
            pl.BlockSpec((1, bases, group), lambda q, c: (q + first, 0, c)),
            rows_spec,
            rows_spec,
        ]
        + [pl.BlockSpec(memory_space=pl.ANY)] * len(extra),
        out_specs=[
            pl.BlockSpec((1, patch_rows, group), lambda q, c: (q + first, 0, c)),
            rows_spec,
        ],
        scratch_shapes=[
            pltpu.VMEM((down.shape[1] // 3, width), jnp.float32),
            pltpu.VMEM((down.shape[0], group + lane), bf16),
            pltpu.VMEM((down.shape[0], group + lane), bf16),
        ],
        input_output_aliases=aliases,
        compiler_params=pltpu.CompilerParams(vmem_limit_bytes=48 << 20),
        cost_estimate=pl.CostEstimate(flops=0, bytes_accessed=14 * count << 20, transcendentals=0),
        name="match_rows",
    )(weights, warped, above, below, down, across, coefs, template, before, *extra)


def split_table(values):
    high = lax.reduce_precision(values, 8, 7)
    return high.astype(bf16), (values - high).astype(bf16)


def taken(values, index):
    table = jnp.zeros((values.shape[0],) + index.shape, jnp.float32)
    for lag in range(values.shape[1]):
        table = jnp.where((index == lag)[None], values[:, lag].reshape(-1, 1, 1), table)
    return table


def on_device(
    ccd_rows,
    tract_row,
    warp_taps,
    warp_shift,
    basis_rows,
    basis_cols,
    coef_table,
    grid_index,
    template,
    visit_weight,
):
    visits, patch_rows, row_width = ccd_rows.shape
    patches = lax.axis_size("patch")
    here = lax.axis_index("patch")
    half = basis_rows.shape[1] // 2
    edge = half // 2
    tiles = row_width // lane

    tiled_rows = ccd_rows.reshape(visits, patch_rows // 8, 8, tiles, lane).transpose(0, 1, 3, 2, 4)
    place = tract_row[0, 0]
    offset = place // patch_rows - here - (place % patch_rows) // 2
    turn = ((here - offset) % patches).astype(jnp.int32).reshape(1)
    taps = jnp.pad(warp_taps[:, 0], ((0, 0), (0, 0), (half_lane, half_lane)))
    shift = jnp.pad(warp_shift, ((0, 0), (0, 0), (half_lane, half_lane)))

    one_hot = (grid_index[0][None, :] == jnp.arange(coef_table.shape[3])[:, None]).astype(
        jnp.float32
    )
    coefs = jnp.einsum(
        "qbg,gx->qbx", coef_table[:, 0], one_hot, precision=lax.Precision.HIGHEST
    )

    rows = jnp.arange(patch_rows)
    ends = jnp.arange(half)
    blank = jnp.full((64 - patch_rows - 2 * half,), 4 * patch_rows)
    inner = jnp.concatenate([rows, ends - half, ends + patch_rows, blank])
    down = taken(basis_rows, inner[None, :] - rows[:, None] + half).reshape(-1, inner.shape[0])
    down_high, down_low = split_table(down)
    down = jnp.concatenate([down_high, down_high, down_low], axis=1)
    across = taken(
        basis_cols, jnp.arange(2 * lane)[:, None] - half_lane - jnp.arange(lane)[None, :] + half
    )
    across = jnp.concatenate(split_table(across), axis=2)
    weights = lax.dynamic_slice_in_dim(
        visit_weight, lax.axis_index("visit") * visits, visits
    )

    starts = [sum(chunks[:i]) for i in range(len(chunks))]
    sent = [
        pack_rows(first, count, tract_row, tiled_rows, patches)
        for first, count in zip(starts, chunks)
    ]
    got = [lax.all_to_all(block, "patch", split_axis=0, concat_axis=0, tiled=True) for block in sent]
    total, difference = None, None
    down_pairs = [(i, i + 1) for i in range(patches - 1)]
    up_pairs = [(i + 1, i) for i in range(patches - 1)]
    for first, block in zip(starts, got):
        warped, head, tail = warp_rows(first, turn, block, taps, shift, patch_rows, edge)
        above = lax.ppermute(tail, "patch", down_pairs)
        below = lax.ppermute(head, "patch", up_pairs)
        difference, total = match_rows(
            first, weights, warped, above, below, down, across, coefs, template, total, difference
        )
    parts = lax.axis_size("visit")
    slices = lax.all_to_all(
        total.reshape(parts, patch_rows // parts, row_width),
        "visit",
        split_axis=0,
        concat_axis=0,
        tiled=True,
    )
    return difference, jnp.sum(slices, axis=0) / jnp.sum(visit_weight)


def solution(mesh):
    placed = (
        P("visit", "patch", None),
        P("visit", "patch"),
        P("visit", "patch", None, None),
        P("visit", "patch", None),
        P(),
        P(),
        P("visit", "patch", None, None),
        P("patch", None),
        P("patch", None),
        P(),
    )
    return jax.shard_map(
        on_device,
        mesh=mesh,
        in_specs=placed,
        out_specs=(P("visit", "patch", None), P(("patch", "visit"), None)),
        check_vma=False,
    )
```

```python
import functools

import jax
import jax.numpy as jnp
from jax import lax
from jax.experimental import pallas as pl
from jax.experimental.pallas import tpu as pltpu
from jax.sharding import PartitionSpec as P

lane = 128
half_lane = 64
group = 1024
chunks = (4, 3, 1)
bf16 = jnp.bfloat16


def pack_kernel(first, places_ref, rows_ref, sent_ref):
    tiles = sent_ref.shape[2] // 2
    patch_rows = places_ref.shape[1]
    visit = first + pl.program_id(0)

    def step(row, carry):
        place = places_ref[visit, row]
        start = (row // 8) * (8 * tiles) + row % 8
        cells = rows_ref[0, pl.ds(start, tiles, stride=8), :]
        at = pl.multiple_of((place % 2) * tiles, tiles)
        sent_ref[place // patch_rows, pl.program_id(0), pl.ds(at, tiles), :] = cells
        return carry

    lax.fori_loop(0, patch_rows, step, 0, unroll=4)


def pack_rows(first, count, tract_row, tiled_rows, patches):
    visits, cells, _ = tiled_rows.shape
    tiles = cells // tract_row.shape[1]
    shape = (patches, count, 2 * tiles, lane)
    return pl.pallas_call(
        functools.partial(pack_kernel, first),
        out_shape=jax.ShapeDtypeStruct(shape, jnp.float32),
        grid=(count,),
        in_specs=[
            pl.BlockSpec(memory_space=pltpu.SMEM),
            pl.BlockSpec((1, cells, lane), lambda q: (q + first, 0, 0)),
        ],
        out_specs=pl.BlockSpec(shape, lambda q: (0, 0, 0, 0)),
        compiler_params=pltpu.CompilerParams(vmem_limit_bytes=32 << 20),
        cost_estimate=pl.CostEstimate(flops=0, bytes_accessed=3 * count << 20, transcendentals=0),
        name="pack_rows",
    )(tract_row, tiled_rows)


def pick_lanes(cells, index):
    return jnp.take_along_axis(cells, index, axis=1, mode="promise_in_bounds")


def warp_kernel(
    first, turn_ref, got_ref, taps_ref, shift_ref, warped_ref, head_ref, tail_ref, rows, sems
):
    patches, count, depth = got_ref.shape[:3]
    tiles = depth // 2
    patch_rows = warped_ref.shape[1]
    groups = patch_rows // 8
    visit = pl.program_id(0)

    @pl.when(visit == 0)
    def _():
        def fetch(item, carry):
            local = item // (patch_rows // 2)
            pair = item % (patch_rows // 2)
            source = (turn_ref[0] + first + local - pair + 2 * patches) % patches
            pltpu.make_async_copy(
                got_ref.at[source, local],
                rows.at[local, pl.ds(pl.multiple_of(pair * depth, depth), depth), :],
                sems.at[local],
            ).start()
            return carry

        lax.fori_loop(0, count * patch_rows // 2, fetch, 0)

    pltpu.make_async_copy(rows.at[visit], rows.at[visit], sems.at[visit]).wait()
    blank = jnp.zeros((8, lane), jnp.float32)
    columns = lax.broadcasted_iota(jnp.int32, (8, lane), 1) + half_lane

    def tile_step(u, carry):
        window = pl.ds(pl.multiple_of(u * lane, lane), lane)
        base = columns + jnp.broadcast_to(shift_ref[0, :, window], (8, lane))
        totals = [blank] * groups
        left, right = jnp.maximum(u - 1, 0), jnp.minimum(u, tiles - 1)
        lows, highs = [], []
        for g in range(groups):
            low = rows[visit, pl.ds(8 * g * tiles + left, 8, stride=tiles), :]
            high = rows[visit, pl.ds(8 * g * tiles + right, 8, stride=tiles), :]
            lows.append(jnp.where(u > 0, low, 0.0))
            highs.append(jnp.where(u < tiles, high, 0.0))
        for k in range(taps_ref.shape[1]):
            spot = base + k
            index = spot & (lane - 1)
            upper = spot >= lane
            tap = jnp.broadcast_to(taps_ref[0, k : k + 1, window], (8, lane))
            for g in range(groups):
                picked = jnp.where(upper, pick_lanes(highs[g], index), pick_lanes(lows[g], index))
                totals[g] = totals[g] + tap * picked
        for g in range(groups):
            warped_ref[0, 8 * g : 8 * g + 8, window] = totals[g]
        return carry

    lax.fori_loop(0, tiles + 1, tile_step, 0)
    edge = head_ref.shape[1]
    last = patch_rows - 2 * edge
    for i in range(edge):
        head_ref[0, i] = warped_ref[0, 2 * i : 2 * i + 2, :]
        tail_ref[0, i] = warped_ref[0, last + 2 * i : last + 2 * i + 2, :]


def warp_rows(first, turn, got, taps, shift, patch_rows, edge):
    patches, count, depth = got.shape[:3]
    width = (depth // 2 + 1) * lane
    edges = jax.ShapeDtypeStruct((count, edge, 2, width), jnp.float32)
    return pl.pallas_call(
        functools.partial(warp_kernel, first),
        out_shape=(
            jax.ShapeDtypeStruct((count, patch_rows, width), jnp.float32),
            edges,
            edges,
        ),
        grid=(count,),
        in_specs=[
            pl.BlockSpec(memory_space=pltpu.SMEM),
            pl.BlockSpec(memory_space=pl.ANY),
            pl.BlockSpec((1,) + taps.shape[1:], lambda q: (q + first, 0, 0)),
            pl.BlockSpec((1,) + shift.shape[1:], lambda q: (q + first, 0, 0)),
        ],
        out_specs=[
            pl.BlockSpec((1, patch_rows, width), lambda q: (q, 0, 0)),
            pl.BlockSpec((1, edge, 2, width), lambda q: (q, 0, 0, 0)),
            pl.BlockSpec((1, edge, 2, width), lambda q: (q, 0, 0, 0)),
        ],
        scratch_shapes=[
            pltpu.VMEM((count, patch_rows // 2 * depth, lane), jnp.float32),
            pltpu.SemaphoreType.DMA((count,)),
        ],
        compiler_params=pltpu.CompilerParams(vmem_limit_bytes=32 << 20),
        cost_estimate=pl.CostEstimate(flops=0, bytes_accessed=12 * count << 20, transcendentals=0),
        name="warp_rows",
    )(turn, got, taps, shift)


def two_parts(values):
    high = values.astype(bf16)
    low = (values - high.astype(jnp.float32)).astype(bf16)
    return high, low


def match_kernel(
    first,
    fresh,
    weight_ref,
    warped_ref,
    above_ref,
    below_ref,
    down_ref,
    across_ref,
    coef_ref,
    template_ref,
    before_ref,
    _,
    difference_ref,
    total_ref,
    stack,
    high_ref,
    low_ref,
):
    patch_rows = warped_ref.shape[1]
    edge = above_ref.shape[1]
    bases = coef_ref.shape[1]
    tiles = group // lane

    @pl.when(pl.program_id(1) == 0)
    def _():
        stack[:patch_rows, :] = warped_ref[0]
        for i in range(edge):
            at = patch_rows + 2 * i
            stack[at : at + 2, :] = above_ref[0, i]
            at = at + 2 * edge
            stack[at : at + 2, :] = below_ref[0, i]
        used = patch_rows + 4 * edge
        stack[used:, :] = jnp.zeros((stack.shape[0] - used, stack.shape[1]), jnp.float32)

    start = pl.multiple_of(pl.program_id(1) * group, group)
    high, low = two_parts(stack[:, pl.ds(start, group + lane)])
    vertical = jnp.dot(
        down_ref[...],
        jnp.concatenate([high, low, high], axis=0),
        preferred_element_type=jnp.float32,
    )
    high_ref[...], low_ref[...] = two_parts(vertical)

    def windows(ref, b):
        rows = slice(b * patch_rows, (b + 1) * patch_rows)
        return jnp.concatenate(
            [ref[rows, lane * i : lane * (i + 2)] for i in range(tiles)], axis=0
        )

    matched = jnp.zeros((tiles * patch_rows, lane), jnp.float32)
    for b in range(bases):
        both = jnp.dot(windows(high_ref, b), across_ref[b], preferred_element_type=jnp.float32)
        rest = jnp.dot(
            windows(low_ref, b), across_ref[b, :, :lane], preferred_element_type=jnp.float32
        )
        smoothed = both[:, :lane] + both[:, lane:] + rest
        scale = jnp.concatenate(
            [
                jnp.broadcast_to(
                    coef_ref[0, b : b + 1, lane * i : lane * (i + 1)], (patch_rows, lane)
                )
                for i in range(tiles)
            ],
            axis=0,
        )
        matched = matched + scale * smoothed
    weight = weight_ref[first + pl.program_id(0)]
    for i in range(tiles):
        piece = matched[i * patch_rows : (i + 1) * patch_rows]
        here = slice(lane * i, lane * (i + 1))
        columns = pl.ds(pl.multiple_of(start + lane * i, lane), lane)
        difference_ref[0, :, here] = piece - template_ref[:, columns]
        if fresh:

            @pl.when(pl.program_id(0) == 0)
            def _():
                total_ref[:, columns] = weight * piece

        else:

            @pl.when(pl.program_id(0) == 0)
            def _():
                total_ref[:, columns] = before_ref[:, columns] + weight * piece

        @pl.when(pl.program_id(0) > 0)
        def _():
            total_ref[:, columns] = total_ref[:, columns] + weight * piece


def match_rows(
    first, weights, warped, above, below, down, across, coefs, template, before, difference
):
    count, patch_rows, width = warped.shape
    edge = above.shape[1]
    visits, bases, row_width = coefs.shape
    fresh = before is None
    if fresh:
        before = template
    extra, aliases = [], {}
    if difference is not None:
        extra, aliases = [difference], {9: 0}
    kernel = functools.partial(match_kernel, first, fresh)
    if difference is None:

        def body(*refs):
            kernel(*refs[:9], None, *refs[9:])

    else:
        body = kernel
    rows_spec = pl.BlockSpec(template.shape, lambda q, c: (0, 0))
    return pl.pallas_call(
        body,
        out_shape=(
            jax.ShapeDtypeStruct((visits, patch_rows, row_width), jnp.float32),
            jax.ShapeDtypeStruct(template.shape, jnp.float32),
        ),
        grid=(count, row_width // group),
        in_specs=[
            pl.BlockSpec(memory_space=pltpu.SMEM),
            pl.BlockSpec((1, patch_rows, width), lambda q, c: (q, 0, 0)),
            pl.BlockSpec((1, edge, 2, width), lambda q, c: (q, 0, 0, 0)),
            pl.BlockSpec((1, edge, 2, width), lambda q, c: (q, 0, 0, 0)),
            pl.BlockSpec(down.shape, lambda q, c: (0, 0)),
            pl.BlockSpec(across.shape, lambda q, c: (0, 0, 0)),
            pl.BlockSpec((1, bases, group), lambda q, c: (q + first, 0, c)),
            rows_spec,
            rows_spec,
        ]
        + [pl.BlockSpec(memory_space=pl.ANY)] * len(extra),
        out_specs=[
            pl.BlockSpec((1, patch_rows, group), lambda q, c: (q + first, 0, c)),
            rows_spec,
        ],
        scratch_shapes=[
            pltpu.VMEM((down.shape[1] // 3, width), jnp.float32),
            pltpu.VMEM((down.shape[0], group + lane), bf16),
            pltpu.VMEM((down.shape[0], group + lane), bf16),
        ],
        input_output_aliases=aliases,
        compiler_params=pltpu.CompilerParams(vmem_limit_bytes=48 << 20),
        cost_estimate=pl.CostEstimate(flops=0, bytes_accessed=20 * count << 20, transcendentals=0),
        name="match_rows",
    )(weights, warped, above, below, down, across, coefs, template, before, *extra)


def split_table(values):
    high = lax.reduce_precision(values, 8, 7)
    return high.astype(bf16), (values - high).astype(bf16)


def taken(values, index):
    table = jnp.zeros((values.shape[0],) + index.shape, jnp.float32)
    for lag in range(values.shape[1]):
        table = jnp.where((index == lag)[None], values[:, lag].reshape(-1, 1, 1), table)
    return table


def on_device(
    ccd_rows,
    tract_row,
    warp_taps,
    warp_shift,
    basis_rows,
    basis_cols,
    coef_table,
    grid_index,
    template,
    visit_weight,
):
    visits, patch_rows, row_width = ccd_rows.shape
    patches = lax.axis_size("patch")
    here = lax.axis_index("patch")
    half = basis_rows.shape[1] // 2
    edge = half // 2
    tiles = row_width // lane

    tiled_rows = ccd_rows.reshape(visits, patch_rows // 8, 8, tiles, lane).transpose(0, 1, 3, 2, 4)
    tiled_rows = tiled_rows.reshape(visits, patch_rows * tiles, lane)
    place = tract_row[0, 0]
    offset = place // patch_rows - here - (place % patch_rows) // 2
    turn = ((here - offset) % patches).astype(jnp.int32).reshape(1)
    taps = jnp.pad(warp_taps[:, 0], ((0, 0), (0, 0), (half_lane, half_lane)))
    shift = jnp.pad(warp_shift, ((0, 0), (0, 0), (half_lane, half_lane)))

    one_hot = (grid_index[0][None, :] == jnp.arange(coef_table.shape[3])[:, None]).astype(
        jnp.float32
    )
    coefs = jnp.einsum(
        "qbg,gx->qbx", coef_table[:, 0], one_hot, precision=lax.Precision.HIGHEST
    )

    rows = jnp.arange(patch_rows)
    ends = jnp.arange(half)
    blank = jnp.full((64 - patch_rows - 2 * half,), 4 * patch_rows)
    inner = jnp.concatenate([rows, ends - half, ends + patch_rows, blank])
    down = taken(basis_rows, inner[None, :] - rows[:, None] + half).reshape(-1, inner.shape[0])
    down_high, down_low = split_table(down)
    down = jnp.concatenate([down_high, down_high, down_low], axis=1)
    across = taken(
        basis_cols, jnp.arange(2 * lane)[:, None] - half_lane - jnp.arange(lane)[None, :] + half
    )
    across = jnp.concatenate(split_table(across), axis=2)
    weights = lax.dynamic_slice_in_dim(
        visit_weight, lax.axis_index("visit") * visits, visits
    )

    starts = [sum(chunks[:i]) for i in range(len(chunks))]
    sent = [
        pack_rows(first, count, tract_row, tiled_rows, patches)
        for first, count in zip(starts, chunks)
    ]
    got = [lax.all_to_all(block, "patch", split_axis=0, concat_axis=0, tiled=True) for block in sent]
    total, difference = None, None
    down_pairs = [(i, i + 1) for i in range(patches - 1)]
    up_pairs = [(i + 1, i) for i in range(patches - 1)]
    for first, block in zip(starts, got):
        if total is not None:
            turn, total = lax.optimization_barrier((turn, total))
        warped, head, tail = warp_rows(first, turn, block, taps, shift, patch_rows, edge)
        above = lax.ppermute(tail, "patch", down_pairs)
        below = lax.ppermute(head, "patch", up_pairs)
        difference, total = match_rows(
            first, weights, warped, above, below, down, across, coefs, template, total, difference
        )
    parts = lax.axis_size("visit")
    slices = lax.all_to_all(
        total.reshape(parts, patch_rows // parts, row_width),
        "visit",
        split_axis=0,
        concat_axis=0,
        tiled=True,
    )
    return difference, jnp.sum(slices, axis=0) / jnp.sum(visit_weight)


def solution(mesh):
    placed = (
        P("visit", "patch", None),
        P("visit", "patch"),
        P("visit", "patch", None, None),
        P("visit", "patch", None),
        P(),
        P(),
        P("visit", "patch", None, None),
        P("patch", None),
        P("patch", None),
        P(),
    )
    return jax.shard_map(
        on_device,
        mesh=mesh,
        in_specs=placed,
        out_specs=(P("visit", "patch", None), P(("patch", "visit"), None)),
        check_vma=False,
    )
```

```python
import functools

import jax
import jax.numpy as jnp
from jax import lax
from jax.experimental import pallas as pl
from jax.experimental.pallas import tpu as pltpu
from jax.sharding import PartitionSpec as P

lane = 128
half_lane = 64
step = 108
parts = 2
room = 58 << 20
chunks = (4, 3, 1)
bf16 = jnp.bfloat16


def pack_kernel(first, places_ref, rows_ref, sent_ref):
    tiles = sent_ref.shape[2] // 2
    patch_rows = places_ref.shape[1]
    visit = first + pl.program_id(0)

    def step(row, carry):
        place = places_ref[visit, row]
        start = (row // 8) * (8 * tiles) + row % 8
        cells = rows_ref[0, pl.ds(start, tiles, stride=8), :]
        at = pl.multiple_of((place % 2) * tiles, tiles)
        sent_ref[place // patch_rows, pl.program_id(0), pl.ds(at, tiles), :] = cells
        return carry

    lax.fori_loop(0, patch_rows, step, 0, unroll=4)


def pack_rows(first, count, tract_row, tiled_rows, patches):
    visits, cells, _ = tiled_rows.shape
    tiles = cells // tract_row.shape[1]
    shape = (patches, count, 2 * tiles, lane)
    return pl.pallas_call(
        functools.partial(pack_kernel, first),
        out_shape=jax.ShapeDtypeStruct(shape, jnp.float32),
        grid=(count,),
        in_specs=[
            pl.BlockSpec(memory_space=pltpu.SMEM),
            pl.BlockSpec((1, cells, lane), lambda q: (q + first, 0, 0)),
        ],
        out_specs=pl.BlockSpec(shape, lambda q: (0, 0, 0, 0)),
        compiler_params=pltpu.CompilerParams(vmem_limit_bytes=room),
        cost_estimate=pl.CostEstimate(flops=0, bytes_accessed=3 * count << 20, transcendentals=0),
        name="pack_rows",
    )(tract_row, tiled_rows)


def split(values):
    high = values.astype(bf16)
    low = (values - high.astype(jnp.float32)).astype(bf16)
    return high, low


def warp_kernel(
    first, turn_ref, got_ref, taps_ref, shift_ref, upper_ref, lower_ref, rows, image, sems
):
    patches, count, depth = got_ref.shape[:3]
    tiles = depth // 2
    half_rows = upper_ref.shape[1]
    patch_rows = 2 * half_rows
    groups = patch_rows // 8
    visit = pl.program_id(0)

    @pl.when(visit == 0)
    def _():
        def fetch(item, carry):
            local = item // (patch_rows // 2)
            pair = item % (patch_rows // 2)
            source = (turn_ref[0] + first + local - pair + 2 * patches) % patches
            pltpu.make_async_copy(
                got_ref.at[source, local],
                rows.at[local, pl.ds(pl.multiple_of(pair * depth, depth), depth), :],
                sems.at[local],
            ).start()
            return carry

        lax.fori_loop(0, count * patch_rows // 2, fetch, 0)
        blank = jnp.zeros((2 * patch_rows, lane), bf16)
        image[:, :lane] = blank
        image[:, (tiles + 1) * lane :] = blank

    pltpu.make_async_copy(rows.at[visit], rows.at[visit], sems.at[visit]).wait()

    def split_step(tile, carry):
        values = jnp.concatenate(
            [
                rows[visit, pl.ds(8 * g * tiles + tile, 8, stride=tiles), :]
                for g in range(groups)
            ],
            axis=0,
        )
        window = pl.ds(pl.multiple_of((tile + 1) * lane, lane), lane)
        image[:, window] = jnp.concatenate(split(values), axis=0)
        return carry

    lax.fori_loop(0, tiles, split_step, 0, unroll=4)
    columns = lax.broadcasted_iota(jnp.int32, (8, lane), 1) + half_lane
    sublanes = lax.broadcasted_iota(jnp.int32, (8, lane), 0)

    def tile_step(u, carry):
        window = pl.ds(pl.multiple_of(u * lane, lane), lane)
        spot = columns + jnp.broadcast_to(shift_ref[0, :, window], (8, lane))
        taps = taps_ref[0, :, window]
        turned = jnp.take_along_axis(
            taps, (sublanes - spot) & 7, axis=0, mode="promise_in_bounds"
        )
        block = (spot >> 3) + jnp.where(sublanes < (spot & 7), 1, 0)
        high = turned.astype(bf16).astype(jnp.float32)
        low = turned - high
        here = [block == i for i in range(2 * lane // 8)]
        matrix = jnp.concatenate(
            [
                jnp.concatenate([jnp.where(m, high, 0.0) for m in here], axis=0).astype(bf16),
                jnp.concatenate([jnp.where(m, low, 0.0) for m in here], axis=0).astype(bf16),
            ],
            axis=1,
        )
        both = pl.ds(pl.multiple_of(u * lane, lane), 2 * lane)
        out = jnp.dot(image[:, both], matrix, preferred_element_type=jnp.float32)
        cells = out[:patch_rows, :lane] + out[:patch_rows, lane:] + out[patch_rows:, :lane]
        upper_ref[0, :, window] = cells[:half_rows]
        lower_ref[0, :, window] = cells[half_rows:]
        return carry

    lax.fori_loop(0, tiles + 1, tile_step, 0, unroll=3)


def warp_rows(first, turn, got, taps, shift, patch_rows):
    patches, count, depth = got.shape[:3]
    width = (depth // 2 + 1) * lane
    half_rows = patch_rows // 2
    shape = jax.ShapeDtypeStruct((count, half_rows, width), jnp.float32)
    return pl.pallas_call(
        functools.partial(warp_kernel, first),
        out_shape=(shape, shape),
        grid=(count,),
        in_specs=[
            pl.BlockSpec(memory_space=pltpu.SMEM),
            pl.BlockSpec(memory_space=pl.ANY),
            pl.BlockSpec((1,) + taps.shape[1:], lambda q: (q + first, 0, 0)),
            pl.BlockSpec((1,) + shift.shape[1:], lambda q: (q + first, 0, 0)),
        ],
        out_specs=[pl.BlockSpec((1, half_rows, width), lambda q: (q, 0, 0))] * 2,
        scratch_shapes=[
            pltpu.VMEM((count, patch_rows // 2 * depth, lane), jnp.float32),
            pltpu.VMEM((2 * patch_rows, width + lane), bf16),
            pltpu.SemaphoreType.DMA((count,)),
        ],
        compiler_params=pltpu.CompilerParams(vmem_limit_bytes=room),
        cost_estimate=pl.CostEstimate(flops=0, bytes_accessed=12 * count << 20, transcendentals=0),
        name="warp_rows",
    )(turn, got, taps, shift)


def match_kernel(
    first,
    fresh,
    weight_ref,
    upper_ref,
    lower_ref,
    above_ref,
    below_ref,
    down_ref,
    across_ref,
    coef_ref,
    template_ref,
    before_ref,
    _,
    difference_ref,
    total_ref,
    pieces,
    high_ref,
    low_ref,
    found,
):
    patch_rows, row_width = template_ref.shape
    bases = across_ref.shape[0]
    windows = pieces.shape[1] // lane
    part = high_ref.shape[1] // lane
    blocks = (upper_ref, lower_ref, above_ref, below_ref)
    half_rows = upper_ref.shape[1]
    inside = lax.broadcasted_iota(jnp.int32, (half_rows, lane), 1)

    @pl.when(pl.program_id(0) == 0)
    def _():
        total_ref[...] = jnp.zeros_like(total_ref) if fresh else before_ref[...]

    for w in range(windows):
        start = step * w + half_lane - (lane - step) // 2
        tile, turn = start // lane, start % lane
        here = slice(w * lane, (w + 1) * lane)
        for i, ref in enumerate(blocks):
            values = ref[0, :, tile * lane : (tile + 1) * lane]
            if turn:
                after = ref[0, :, (tile + 1) * lane : (tile + 2) * lane]
                values = jnp.where(
                    inside < lane - turn,
                    pltpu.roll(values, lane - turn, 1),
                    pltpu.roll(after, lane - turn, 1),
                )
            high, low = split(values)
            for j, value in enumerate((high, low, high)):
                at = (j * len(blocks) + i) * half_rows
                pieces[at : at + half_rows, here] = value

    def part_step(p, carry):
        wide = pl.ds(pl.multiple_of(p * part * lane, lane), part * lane)
        vertical = jnp.dot(down_ref[...], pieces[:, wide], preferred_element_type=jnp.float32)
        high_ref[...], low_ref[...] = split(vertical)

        def gathered(ref, b):
            rows = slice(b * patch_rows, (b + 1) * patch_rows)
            return jnp.concatenate(
                [ref[rows, lane * i : lane * (i + 1)] for i in range(part)], axis=0
            )

        matched = jnp.zeros((part * patch_rows, lane), jnp.float32)
        for b in range(bases):
            operand = jnp.concatenate([gathered(high_ref, b), gathered(low_ref, b)], axis=1)
            both = jnp.dot(operand, across_ref[b], preferred_element_type=jnp.float32)
            scales = coef_ref[0, b : b + 1, wide]
            scale = jnp.concatenate(
                [
                    jnp.broadcast_to(scales[:, lane * i : lane * (i + 1)], (patch_rows, lane))
                    for i in range(part)
                ],
                axis=0,
            )
            matched = matched + scale * (both[:, :lane] + both[:, lane:])
        found[pl.ds(pl.multiple_of(p * part * patch_rows, 8), part * patch_rows), :] = matched
        return carry

    lax.fori_loop(0, windows // part, part_step, 0)
    weight = weight_ref[first + pl.program_id(0)]
    inside = lax.broadcasted_iota(jnp.int32, (patch_rows, lane), 1)
    for tile in range(row_width // lane):
        piece = None
        for w in range(tile * lane // step, ((tile + 1) * lane - 1) // step + 1):
            start = step * w - tile * lane
            values = found[w * patch_rows : (w + 1) * patch_rows, :]
            if start % lane:
                values = pltpu.roll(values, start % lane, 1)
            piece = values if piece is None else jnp.where(inside < start, piece, values)
        here = slice(lane * tile, lane * (tile + 1))
        difference_ref[0, :, here] = piece - template_ref[:, here]
        total_ref[:, here] = total_ref[:, here] + weight * piece


def match_rows(
    first, weights, upper, lower, above, below, down, across, coefs, template, before, difference
):
    count, half_rows, width = upper.shape
    visits, bases, span = coefs.shape
    patch_rows, row_width = template.shape
    part = span // lane // parts
    fresh = before is None
    if fresh:
        before = template
    extra, aliases = [], {}
    if difference is not None:
        extra, aliases = [difference], {10: 0}
    kernel = functools.partial(match_kernel, first, fresh)
    if difference is None:

        def body(*refs):
            kernel(*refs[:10], None, *refs[10:])

    else:
        body = kernel
    rows_spec = pl.BlockSpec(template.shape, lambda q: (0, 0))
    return pl.pallas_call(
        body,
        out_shape=(
            jax.ShapeDtypeStruct((visits, patch_rows, row_width), jnp.float32),
            jax.ShapeDtypeStruct(template.shape, jnp.float32),
        ),
        grid=(count,),
        in_specs=[
            pl.BlockSpec(memory_space=pltpu.SMEM),
            *[pl.BlockSpec((1, half_rows, width), lambda q: (q, 0, 0))] * 4,
            pl.BlockSpec(down.shape, lambda q: (0, 0)),
            pl.BlockSpec(across.shape, lambda q: (0, 0, 0)),
            pl.BlockSpec((1, bases, span), lambda q: (q + first, 0, 0)),
            rows_spec,
            rows_spec,
        ]
        + [pl.BlockSpec(memory_space=pl.ANY)] * len(extra),
        out_specs=[
            pl.BlockSpec((1, patch_rows, row_width), lambda q: (q + first, 0, 0)),
            rows_spec,
        ],
        scratch_shapes=[
            pltpu.VMEM((down.shape[1], span), bf16),
            pltpu.VMEM((down.shape[0], part * lane), bf16),
            pltpu.VMEM((down.shape[0], part * lane), bf16),
            pltpu.VMEM((span // lane * patch_rows, lane), jnp.float32),
        ],
        input_output_aliases=aliases,
        compiler_params=pltpu.CompilerParams(vmem_limit_bytes=room),
        cost_estimate=pl.CostEstimate(flops=0, bytes_accessed=20 * count << 20, transcendentals=0),
        name="match_rows",
    )(weights, upper, lower, above, below, down, across, coefs, template, before, *extra)


def sum_kernel(total_ref, scale_ref, out_ref, slots, send_sems, recv_sems):
    me = lax.axis_index("visit")
    slabs = lax.axis_size("visit")
    rows = out_ref.shape[0]
    mesh_ids = pl.DeviceIdType.MESH
    barrier = pltpu.get_barrier_semaphore()
    for i in range(1, slabs):
        to = lax.rem(me + i, slabs)
        pl.semaphore_signal(barrier, inc=1, device_id={"visit": to}, device_id_type=mesh_ids)
    pl.semaphore_wait(barrier, slabs - 1)
    copies = []
    for i in range(1, slabs):
        to = lax.rem(me + i, slabs)
        copy = pltpu.make_async_remote_copy(
            src_ref=total_ref.at[pl.ds(pl.multiple_of(rows * to, rows), rows), :],
            dst_ref=slots.at[i - 1],
            send_sem=send_sems.at[i - 1],
            recv_sem=recv_sems.at[i - 1],
            device_id={"visit": to},
            device_id_type=mesh_ids,
        )
        copy.start()
        copies.append(copy)
    for copy in copies:
        copy.wait()
    result = total_ref[pl.ds(pl.multiple_of(rows * me, rows), rows), :]
    for i in range(slabs - 1):
        result = result + slots[i]
    out_ref[...] = result / scale_ref[0]


def sum_visits(total, scale):
    slabs = lax.axis_size("visit")
    shape = (total.shape[0] // slabs, total.shape[1])
    return pl.pallas_call(
        sum_kernel,
        out_shape=jax.ShapeDtypeStruct(shape, jnp.float32),
        in_specs=[
            pl.BlockSpec(memory_space=pltpu.VMEM),
            pl.BlockSpec(memory_space=pltpu.SMEM),
        ],
        out_specs=pl.BlockSpec(memory_space=pltpu.VMEM),
        scratch_shapes=[
            pltpu.VMEM((slabs - 1,) + shape, jnp.float32),
            pltpu.SemaphoreType.DMA((slabs - 1,)),
            pltpu.SemaphoreType.DMA((slabs - 1,)),
        ],
        compiler_params=pltpu.CompilerParams(collective_id=0, has_side_effects=True),
        name="sum_visits",
    )(total, scale)


def split_table(values):
    high = lax.reduce_precision(values, 8, 7)
    return high.astype(bf16), (values - high).astype(bf16)


def taken(values, index):
    table = jnp.zeros((values.shape[0],) + index.shape, jnp.float32)
    for lag in range(values.shape[1]):
        table = jnp.where((index == lag)[None], values[:, lag].reshape(-1, 1, 1), table)
    return table


def on_device(
    ccd_rows,
    tract_row,
    warp_taps,
    warp_shift,
    basis_rows,
    basis_cols,
    coef_table,
    grid_index,
    template,
    visit_weight,
):
    visits, patch_rows, row_width = ccd_rows.shape
    patches = lax.axis_size("patch")
    here = lax.axis_index("patch")
    half = basis_rows.shape[1] // 2
    tiles = row_width // lane

    tiled_rows = ccd_rows.reshape(visits, patch_rows // 8, 8, tiles, lane).transpose(0, 1, 3, 2, 4)
    tiled_rows = tiled_rows.reshape(visits, patch_rows * tiles, lane)
    place = tract_row[0, 0]
    offset = place // patch_rows - here - (place % patch_rows) // 2
    turn = ((here - offset) % patches).astype(jnp.int32).reshape(1)
    taps = jnp.pad(warp_taps[:, 0], ((0, 0), (0, 0), (half_lane, half_lane)))
    shift = jnp.pad(warp_shift, ((0, 0), (0, 0), (half_lane, half_lane)))

    windows = -(-row_width // step)
    cells = jnp.pad(grid_index[0], (0, windows * step - row_width)).reshape(windows, step)
    cells = jnp.pad(cells, ((0, 0), (0, lane - step))).reshape(-1)
    one_hot = (cells[None, :] == jnp.arange(coef_table.shape[3])[:, None]).astype(jnp.float32)
    coefs = jnp.einsum(
        "qbg,gx->qbx", coef_table[:, 0], one_hot, precision=lax.Precision.HIGHEST
    )

    rows = jnp.arange(patch_rows)
    inner = jnp.concatenate(
        [rows, jnp.arange(patch_rows // 2) - patch_rows // 2, jnp.arange(patch_rows // 2) + patch_rows]
    )
    down = taken(basis_rows, inner[None, :] - rows[:, None] + half).reshape(-1, inner.shape[0])
    down_high, down_low = split_table(down)
    down = jnp.concatenate([down_high, down_high, down_low], axis=1)
    out = jnp.arange(lane)[None, :]
    across = taken(
        basis_cols, jnp.where(out < step, jnp.arange(lane)[:, None] - out, basis_cols.shape[1])
    )
    high, low = split_table(across)
    across = jnp.concatenate(
        [
            jnp.concatenate([high, low], axis=2),
            jnp.concatenate([high, jnp.zeros_like(low)], axis=2),
        ],
        axis=1,
    )
    weights = lax.dynamic_slice_in_dim(
        visit_weight, lax.axis_index("visit") * visits, visits
    )

    starts = [sum(chunks[:i]) for i in range(len(chunks))]
    sent = [
        pack_rows(first, count, tract_row, tiled_rows, patches)
        for first, count in zip(starts, chunks)
    ]
    sent[1:], down, across, coefs, taps, shift, weights, turn = lax.optimization_barrier(
        (sent[1:], down, across, coefs, taps, shift, weights, turn)
    )
    got = [lax.all_to_all(block, "patch", split_axis=0, concat_axis=0, tiled=True) for block in sent]
    total, difference = None, None
    down_pairs = [(i, i + 1) for i in range(patches - 1)]
    up_pairs = [(i + 1, i) for i in range(patches - 1)]
    for first, block in zip(starts, got):
        if total is not None:
            turn, total = lax.optimization_barrier((turn, total))
        upper, lower = warp_rows(first, turn, block, taps, shift, patch_rows)
        above = lax.ppermute(lower, "patch", down_pairs)
        below = lax.ppermute(upper, "patch", up_pairs)
        difference, total = match_rows(
            first, weights, upper, lower, above, below, down, across, coefs, template, total, difference
        )
    coadd = sum_visits(total, jnp.sum(visit_weight).reshape(1))
    return difference, coadd


def solution(mesh):
    placed = (
        P("visit", "patch", None),
        P("visit", "patch"),
        P("visit", "patch", None, None),
        P("visit", "patch", None),
        P(),
        P(),
        P("visit", "patch", None, None),
        P("patch", None),
        P("patch", None),
        P(),
    )
    return jax.shard_map(
        on_device,
        mesh=mesh,
        in_specs=placed,
        out_specs=(P("visit", "patch", None), P(("patch", "visit"), None)),
        check_vma=False,
    )
```

```python
import functools

import jax
import jax.numpy as jnp
from jax import lax
from jax.experimental import pallas as pl
from jax.experimental.pallas import tpu as pltpu
from jax.sharding import PartitionSpec as P

lane = 128
half_lane = 64
step = 108
parts = 2
room = 24 << 20
chunks = (5, 3)
bf16 = jnp.bfloat16


def pack_kernel(first, places_ref, rows_ref, sent_ref):
    tiles = sent_ref.shape[2] // 2
    patch_rows = places_ref.shape[1]
    visit = first + pl.program_id(0)

    def step(row, carry):
        place = places_ref[visit, row]
        start = (row // 8) * (8 * tiles) + row % 8
        cells = rows_ref[0, pl.ds(start, tiles, stride=8), :]
        at = pl.multiple_of((place % 2) * tiles, tiles)
        sent_ref[place // patch_rows, 0, pl.ds(at, tiles), :] = cells
        return carry

    lax.fori_loop(0, patch_rows, step, 0, unroll=4)


def pack_rows(first, count, tract_row, tiled_rows, patches):
    visits, cells, _ = tiled_rows.shape
    tiles = cells // tract_row.shape[1]
    shape = (patches, count, 2 * tiles, lane)
    return pl.pallas_call(
        functools.partial(pack_kernel, first),
        out_shape=jax.ShapeDtypeStruct(shape, jnp.float32),
        grid=(count,),
        in_specs=[
            pl.BlockSpec(memory_space=pltpu.SMEM),
            pl.BlockSpec((1, cells, lane), lambda q: (q + first, 0, 0)),
        ],
        out_specs=pl.BlockSpec((patches, 1, 2 * tiles, lane), lambda q: (0, q, 0, 0)),
        compiler_params=pltpu.CompilerParams(vmem_limit_bytes=58 << 20),
        cost_estimate=pl.CostEstimate(flops=0, bytes_accessed=3 * count << 20, transcendentals=0),
        name="pack_rows",
    )(tract_row, tiled_rows)


def split(values):
    high = values.astype(bf16)
    low = (values - high.astype(jnp.float32)).astype(bf16)
    return high, low


def warp_kernel(
    first, turn_ref, got_ref, taps_ref, shift_ref, upper_ref, lower_ref, rows, image, sems
):
    patches, count, depth = got_ref.shape[:3]
    tiles = depth // 2
    half_rows = upper_ref.shape[1]
    patch_rows = 2 * half_rows
    groups = patch_rows // 8
    visit = pl.program_id(0)

    @pl.when(visit == 0)
    def _():
        def fetch(item, carry):
            local = item // (patch_rows // 2)
            pair = item % (patch_rows // 2)
            source = (turn_ref[0] + first + local - pair + 2 * patches) % patches
            pltpu.make_async_copy(
                got_ref.at[source, local],
                rows.at[local, pl.ds(pl.multiple_of(pair * depth, depth), depth), :],
                sems.at[local],
            ).start()
            return carry

        lax.fori_loop(0, count * patch_rows // 2, fetch, 0)
        blank = jnp.zeros((2 * patch_rows, lane), bf16)
        image[:, :lane] = blank
        image[:, (tiles + 1) * lane :] = blank

    pltpu.make_async_copy(rows.at[visit], rows.at[visit], sems.at[visit]).wait()

    def split_step(tile, carry):
        values = jnp.concatenate(
            [
                rows[visit, pl.ds(8 * g * tiles + tile, 8, stride=tiles), :]
                for g in range(groups)
            ],
            axis=0,
        )
        window = pl.ds(pl.multiple_of((tile + 1) * lane, lane), lane)
        image[:, window] = jnp.concatenate(split(values), axis=0)
        return carry

    lax.fori_loop(0, tiles, split_step, 0, unroll=4)
    columns = lax.broadcasted_iota(jnp.int32, (8, lane), 1) + half_lane
    sublanes = lax.broadcasted_iota(jnp.int32, (8, lane), 0)

    def tile_step(u, carry):
        window = pl.ds(pl.multiple_of(u * lane, lane), lane)
        spot = columns + jnp.broadcast_to(shift_ref[0, :, window], (8, lane))
        taps = taps_ref[0, :, window]
        turned = jnp.take_along_axis(
            taps, (sublanes - spot) & 7, axis=0, mode="promise_in_bounds"
        )
        block = (spot >> 3) + jnp.where(sublanes < (spot & 7), 1, 0)
        high = turned.astype(bf16).astype(jnp.float32)
        low = turned - high
        here = [block == i for i in range(2 * lane // 8)]
        matrix = jnp.concatenate(
            [
                jnp.concatenate([jnp.where(m, high, 0.0) for m in here], axis=0).astype(bf16),
                jnp.concatenate([jnp.where(m, low, 0.0) for m in here], axis=0).astype(bf16),
            ],
            axis=1,
        )
        both = pl.ds(pl.multiple_of(u * lane, lane), 2 * lane)
        out = jnp.dot(image[:, both], matrix, preferred_element_type=jnp.float32)
        cells = out[:patch_rows, :lane] + out[:patch_rows, lane:] + out[patch_rows:, :lane]
        upper_ref[0, :, window] = cells[:half_rows]
        lower_ref[0, :, window] = cells[half_rows:]
        return carry

    lax.fori_loop(0, tiles + 1, tile_step, 0, unroll=33)


def warp_rows(first, turn, got, taps, shift, patch_rows):
    patches, count, depth = got.shape[:3]
    width = (depth // 2 + 1) * lane
    half_rows = patch_rows // 2
    shape = jax.ShapeDtypeStruct((count, half_rows, width), jnp.float32)
    return pl.pallas_call(
        functools.partial(warp_kernel, first),
        out_shape=(shape, shape),
        grid=(count,),
        in_specs=[
            pl.BlockSpec(memory_space=pltpu.SMEM),
            pl.BlockSpec(memory_space=pl.ANY),
            pl.BlockSpec((1,) + taps.shape[1:], lambda q: (q + first, 0, 0)),
            pl.BlockSpec((1,) + shift.shape[1:], lambda q: (q + first, 0, 0)),
        ],
        out_specs=[pl.BlockSpec((1, half_rows, width), lambda q: (q, 0, 0))] * 2,
        scratch_shapes=[
            pltpu.VMEM((count, patch_rows // 2 * depth, lane), jnp.float32),
            pltpu.VMEM((2 * patch_rows, width + lane), bf16),
            pltpu.SemaphoreType.DMA((count,)),
        ],
        compiler_params=pltpu.CompilerParams(vmem_limit_bytes=room),
        cost_estimate=pl.CostEstimate(flops=0, bytes_accessed=12 * count << 20, transcendentals=0),
        name="warp_rows",
    )(turn, got, taps, shift)


def match_kernel(
    first,
    fresh,
    weight_ref,
    upper_ref,
    lower_ref,
    above_ref,
    below_ref,
    down_ref,
    across_ref,
    coef_ref,
    template_ref,
    before_ref,
    _,
    difference_ref,
    total_ref,
    pieces,
    high_refs,
    low_refs,
    found,
):
    patch_rows, row_width = template_ref.shape
    bases = across_ref.shape[0]
    windows = pieces.shape[1] // lane
    part = high_refs.shape[2] // lane
    blocks = (upper_ref, lower_ref, above_ref, below_ref)
    half_rows = upper_ref.shape[1]
    inside = lax.broadcasted_iota(jnp.int32, (half_rows, lane), 1)

    @pl.when(pl.program_id(0) == 0)
    def _():
        total_ref[...] = jnp.zeros_like(total_ref) if fresh else before_ref[...]

    def cut_window(w):
        start = step * w + half_lane - (lane - step) // 2
        tile, turn = start // lane, start % lane
        here = slice(w * lane, (w + 1) * lane)
        for i, ref in enumerate(blocks):
            values = ref[0, :, tile * lane : (tile + 1) * lane]
            if turn:
                after = ref[0, :, (tile + 1) * lane : (tile + 2) * lane]
                values = jnp.where(
                    inside < lane - turn,
                    pltpu.roll(values, lane - turn, 1),
                    pltpu.roll(after, lane - turn, 1),
                )
            high, low = split(values)
            for j, value in enumerate((high, low, high)):
                at = (j * len(blocks) + i) * half_rows
                pieces[at : at + half_rows, here] = value

    def part_step(p):
        for w in range(p * part, (p + 1) * part):
            cut_window(w)
        wide = slice(p * part * lane, (p + 1) * part * lane)
        high_ref = high_refs.at[p]
        low_ref = low_refs.at[p]
        vertical = jnp.dot(down_ref[...], pieces[:, wide], preferred_element_type=jnp.float32)
        high_ref[...], low_ref[...] = split(vertical)

        def gathered(ref, b):
            rows = slice(b * patch_rows, (b + 1) * patch_rows)
            return jnp.concatenate(
                [ref[rows, lane * i : lane * (i + 1)] for i in range(part)], axis=0
            )

        matched = jnp.zeros((part * patch_rows, lane), jnp.float32)
        for b in range(bases):
            operand = jnp.concatenate([gathered(high_ref, b), gathered(low_ref, b)], axis=1)
            both = jnp.dot(operand, across_ref[b], preferred_element_type=jnp.float32)
            scales = coef_ref[0, b : b + 1, wide]
            scale = jnp.concatenate(
                [
                    jnp.broadcast_to(scales[:, lane * i : lane * (i + 1)], (patch_rows, lane))
                    for i in range(part)
                ],
                axis=0,
            )
            matched = matched + scale * (both[:, :lane] + both[:, lane:])
        found[p * part * patch_rows : (p + 1) * part * patch_rows, :] = matched

    for p in range(windows // part):
        part_step(p)
    weight = weight_ref[first + pl.program_id(0)]
    inside = lax.broadcasted_iota(jnp.int32, (patch_rows, lane), 1)
    for tile in range(row_width // lane):
        piece = None
        for w in range(tile * lane // step, ((tile + 1) * lane - 1) // step + 1):
            start = step * w - tile * lane
            values = found[w * patch_rows : (w + 1) * patch_rows, :]
            if start % lane:
                values = pltpu.roll(values, start % lane, 1)
            piece = values if piece is None else jnp.where(inside < start, piece, values)
        here = slice(lane * tile, lane * (tile + 1))
        difference_ref[0, :, here] = piece - template_ref[:, here]
        total_ref[:, here] = total_ref[:, here] + weight * piece


def match_rows(
    first, weights, upper, lower, above, below, down, across, coefs, template, before, difference
):
    count, half_rows, width = upper.shape
    visits, bases, span = coefs.shape
    patch_rows, row_width = template.shape
    part = span // lane // parts
    fresh = before is None
    if fresh:
        before = template
    extra, aliases = [], {}
    if difference is not None:
        extra, aliases = [difference], {10: 0}
    kernel = functools.partial(match_kernel, first, fresh)
    if difference is None:

        def body(*refs):
            kernel(*refs[:10], None, *refs[10:])

    else:
        body = kernel
    rows_spec = pl.BlockSpec(template.shape, lambda q: (0, 0))
    return pl.pallas_call(
        body,
        out_shape=(
            jax.ShapeDtypeStruct((visits, patch_rows, row_width), jnp.float32),
            jax.ShapeDtypeStruct(template.shape, jnp.float32),
        ),
        grid=(count,),
        in_specs=[
            pl.BlockSpec(memory_space=pltpu.SMEM),
            *[pl.BlockSpec((1, half_rows, width), lambda q: (q, 0, 0))] * 4,
            pl.BlockSpec(down.shape, lambda q: (0, 0)),
            pl.BlockSpec(across.shape, lambda q: (0, 0, 0)),
            pl.BlockSpec((1, bases, span), lambda q: (q + first, 0, 0)),
            rows_spec,
            rows_spec,
        ]
        + [pl.BlockSpec(memory_space=pl.ANY)] * len(extra),
        out_specs=[
            pl.BlockSpec((1, patch_rows, row_width), lambda q: (q + first, 0, 0)),
            rows_spec,
        ],
        scratch_shapes=[
            pltpu.VMEM((down.shape[1], span), bf16),
            pltpu.VMEM((parts, down.shape[0], part * lane), bf16),
            pltpu.VMEM((parts, down.shape[0], part * lane), bf16),
            pltpu.VMEM((span // lane * patch_rows, lane), jnp.float32),
        ],
        input_output_aliases=aliases,
        compiler_params=pltpu.CompilerParams(vmem_limit_bytes=room),
        cost_estimate=pl.CostEstimate(flops=0, bytes_accessed=20 * count << 20, transcendentals=0),
        name="match_rows",
    )(weights, upper, lower, above, below, down, across, coefs, template, before, *extra)


def sum_kernel(total_ref, scale_ref, out_ref, own, slots, own_sem, send_sems, recv_sems):
    me = lax.axis_index("visit")
    slabs = lax.axis_size("visit")
    rows = out_ref.shape[0]
    mesh_ids = pl.DeviceIdType.MESH
    mine = pltpu.make_async_copy(
        total_ref.at[pl.ds(pl.multiple_of(rows * me, rows), rows), :], own, own_sem
    )
    mine.start()
    barrier = pltpu.get_barrier_semaphore()
    for i in range(1, slabs):
        to = lax.rem(me + i, slabs)
        pl.semaphore_signal(barrier, inc=1, device_id={"visit": to}, device_id_type=mesh_ids)
    pl.semaphore_wait(barrier, slabs - 1)
    copies = []
    for i in range(1, slabs):
        to = lax.rem(me + i, slabs)
        copy = pltpu.make_async_remote_copy(
            src_ref=total_ref.at[pl.ds(pl.multiple_of(rows * to, rows), rows), :],
            dst_ref=slots.at[i - 1],
            send_sem=send_sems.at[i - 1],
            recv_sem=recv_sems.at[i - 1],
            device_id={"visit": to},
            device_id_type=mesh_ids,
        )
        copy.start()
        copies.append(copy)
    for copy in copies:
        copy.wait()
    mine.wait()
    result = own[...]
    for i in range(slabs - 1):
        result = result + slots[i]
    out_ref[...] = result / scale_ref[0]


def sum_visits(total, scale):
    slabs = lax.axis_size("visit")
    shape = (total.shape[0] // slabs, total.shape[1])
    return pl.pallas_call(
        sum_kernel,
        out_shape=jax.ShapeDtypeStruct(shape, jnp.float32),
        in_specs=[
            pl.BlockSpec(memory_space=pl.ANY),
            pl.BlockSpec(memory_space=pltpu.SMEM),
        ],
        out_specs=pl.BlockSpec(memory_space=pltpu.VMEM),
        scratch_shapes=[
            pltpu.VMEM(shape, jnp.float32),
            pltpu.VMEM((slabs - 1,) + shape, jnp.float32),
            pltpu.SemaphoreType.DMA,
            pltpu.SemaphoreType.DMA((slabs - 1,)),
            pltpu.SemaphoreType.DMA((slabs - 1,)),
        ],
        compiler_params=pltpu.CompilerParams(collective_id=0, has_side_effects=True),
        name="sum_visits",
    )(total, scale)


def split_table(values):
    high = lax.reduce_precision(values, 8, 7)
    return high.astype(bf16), (values - high).astype(bf16)


def taken(values, index):
    table = jnp.zeros((values.shape[0],) + index.shape, jnp.float32)
    for lag in range(values.shape[1]):
        table = jnp.where((index == lag)[None], values[:, lag].reshape(-1, 1, 1), table)
    return table


def on_device(
    ccd_rows,
    tract_row,
    warp_taps,
    warp_shift,
    basis_rows,
    basis_cols,
    coef_table,
    grid_index,
    template,
    visit_weight,
):
    visits, patch_rows, row_width = ccd_rows.shape
    patches = lax.axis_size("patch")
    here = lax.axis_index("patch")
    half = basis_rows.shape[1] // 2
    tiles = row_width // lane

    tiled_rows = ccd_rows.reshape(visits, patch_rows // 8, 8, tiles, lane).transpose(0, 1, 3, 2, 4)
    tiled_rows = tiled_rows.reshape(visits, patch_rows * tiles, lane)
    place = tract_row[0, 0]
    offset = place // patch_rows - here - (place % patch_rows) // 2
    turn = ((here - offset) % patches).astype(jnp.int32).reshape(1)
    taps = jnp.pad(warp_taps[:, 0], ((0, 0), (0, 0), (half_lane, half_lane)))
    shift = jnp.pad(warp_shift, ((0, 0), (0, 0), (half_lane, half_lane)))

    windows = -(-row_width // step)
    cells = jnp.pad(grid_index[0], (0, windows * step - row_width)).reshape(windows, step)
    cells = jnp.pad(cells, ((0, 0), (0, lane - step))).reshape(-1)
    one_hot = (cells[None, :] == jnp.arange(coef_table.shape[3])[:, None]).astype(jnp.float32)
    coefs = jnp.einsum(
        "qbg,gx->qbx", coef_table[:, 0], one_hot, precision=lax.Precision.HIGHEST
    )

    rows = jnp.arange(patch_rows)
    inner = jnp.concatenate(
        [rows, jnp.arange(patch_rows // 2) - patch_rows // 2, jnp.arange(patch_rows // 2) + patch_rows]
    )
    down = taken(basis_rows, inner[None, :] - rows[:, None] + half).reshape(-1, inner.shape[0])
    down_high, down_low = split_table(down)
    down = jnp.concatenate([down_high, down_high, down_low], axis=1)
    out = jnp.arange(lane)[None, :]
    across = taken(
        basis_cols, jnp.where(out < step, jnp.arange(lane)[:, None] - out, basis_cols.shape[1])
    )
    high, low = split_table(across)
    across = jnp.concatenate(
        [
            jnp.concatenate([high, low], axis=2),
            jnp.concatenate([high, jnp.zeros_like(low)], axis=2),
        ],
        axis=1,
    )
    weights = lax.dynamic_slice_in_dim(
        visit_weight, lax.axis_index("visit") * visits, visits
    )

    starts = [sum(chunks[:i]) for i in range(len(chunks))]
    sent = [
        pack_rows(first, count, tract_row, tiled_rows, patches)
        for first, count in zip(starts, chunks)
    ]
    sent[1:], down, across, coefs, taps, shift, weights, turn = lax.optimization_barrier(
        (sent[1:], down, across, coefs, taps, shift, weights, turn)
    )
    got = [lax.all_to_all(block, "patch", split_axis=0, concat_axis=0, tiled=True) for block in sent]
    total, difference = None, None
    down_pairs = [(i, i + 1) for i in range(patches - 1)]
    up_pairs = [(i + 1, i) for i in range(patches - 1)]
    for first, block in zip(starts, got):
        if total is not None:
            turn, total = lax.optimization_barrier((turn, total))
        upper, lower = warp_rows(first, turn, block, taps, shift, patch_rows)
        above = lax.ppermute(lower, "patch", down_pairs)
        below = lax.ppermute(upper, "patch", up_pairs)
        difference, total = match_rows(
            first, weights, upper, lower, above, below, down, across, coefs, template, total, difference
        )
    coadd = sum_visits(total, jnp.sum(visit_weight).reshape(1))
    return difference, coadd


def solution(mesh):
    placed = (
        P("visit", "patch", None),
        P("visit", "patch"),
        P("visit", "patch", None, None),
        P("visit", "patch", None),
        P(),
        P(),
        P("visit", "patch", None, None),
        P("patch", None),
        P("patch", None),
        P(),
    )
    return jax.shard_map(
        on_device,
        mesh=mesh,
        in_specs=placed,
        out_specs=(P("visit", "patch", None), P(("patch", "visit"), None)),
        check_vma=False,
    )
```

```python
import functools

import jax
import jax.numpy as jnp
from jax import lax
from jax.experimental import pallas as pl
from jax.experimental.pallas import tpu as pltpu
from jax.sharding import PartitionSpec as P

lane = 128
half_lane = 64
step = 108
parts = 2
room = 24 << 20
chunks = (4, 4)
bf16 = jnp.bfloat16


def pack_kernel(first, places_ref, rows_ref, sent_ref):
    tiles = sent_ref.shape[2] // 2
    patch_rows = places_ref.shape[1]
    visit = first + pl.program_id(0)

    def step(row, carry):
        place = places_ref[visit, row]
        start = (row // 8) * (8 * tiles) + row % 8
        cells = rows_ref[0, pl.ds(start, tiles, stride=8), :]
        at = pl.multiple_of((place % 2) * tiles, tiles)
        sent_ref[place // patch_rows, 0, pl.ds(at, tiles), :] = cells
        return carry

    lax.fori_loop(0, patch_rows, step, 0, unroll=True)


def pack_rows(first, count, tract_row, tiled_rows, patches):
    visits, cells, _ = tiled_rows.shape
    tiles = cells // tract_row.shape[1]
    shape = (patches, count, 2 * tiles, lane)
    return pl.pallas_call(
        functools.partial(pack_kernel, first),
        out_shape=jax.ShapeDtypeStruct(shape, jnp.float32),
        grid=(count,),
        in_specs=[
            pl.BlockSpec(memory_space=pltpu.SMEM),
            pl.BlockSpec((1, cells, lane), lambda q: (q + first, 0, 0)),
        ],
        out_specs=pl.BlockSpec((patches, 1, 2 * tiles, lane), lambda q: (0, q, 0, 0)),
        compiler_params=pltpu.CompilerParams(vmem_limit_bytes=58 << 20),
        cost_estimate=pl.CostEstimate(flops=0, bytes_accessed=3 * count << 20, transcendentals=0),
        name="pack_rows",
    )(tract_row, tiled_rows)


def folded(tiles):
    return -(-tiles // 4)


def split(values):
    high = values.astype(bf16)
    low = (values - high.astype(jnp.float32)).astype(bf16)
    return high, low


def warp_kernel(
    first, turn_ref, got_ref, taps_ref, shift_ref, warped_ref, head_ref, tail_ref, rows, image, sems
):
    patches, _, depth = got_ref.shape[:3]
    tiles = depth // 2
    patch_rows = warped_ref.shape[1]
    groups = patch_rows // 8
    visit = pl.program_id(0)

    @pl.when(visit == 0)
    def _():
        def fetch(local, carry):
            for pair in range(patch_rows // 2):
                source = (turn_ref[0] + first + local - pair + 2 * patches) % patches
                pltpu.make_async_copy(
                    got_ref.at[source, first + local],
                    rows.at[local, pl.ds(pair * depth, depth), :],
                    sems.at[local],
                ).start()
            return carry

        lax.fori_loop(0, pl.num_programs(0), fetch, 0)
        blank = jnp.zeros((2 * patch_rows, lane), bf16)
        image[:, :lane] = blank
        image[:, (tiles + 1) * lane :] = blank

    pltpu.make_async_copy(rows.at[visit], rows.at[visit], sems.at[visit]).wait()

    def split_step(tile, carry):
        values = jnp.concatenate(
            [
                rows[visit, pl.ds(8 * g * tiles + tile, 8, stride=tiles), :]
                for g in range(groups)
            ],
            axis=0,
        )
        window = pl.ds(pl.multiple_of((tile + 1) * lane, lane), lane)
        image[:, window] = jnp.concatenate(split(values), axis=0)
        return carry

    lax.fori_loop(0, tiles, split_step, 0, unroll=4)
    columns = lax.broadcasted_iota(jnp.int32, (8, lane), 1) + half_lane
    sublanes = lax.broadcasted_iota(jnp.int32, (8, lane), 0)

    fold = folded(tiles + 1)
    for ref in (head_ref, tail_ref):
        ref[0, :, (tiles + 1) * lane :] = jnp.zeros((8, fold * lane), jnp.float32)
    for u in range(tiles + 1):
        window = slice(u * lane, (u + 1) * lane)
        spot = columns + jnp.broadcast_to(shift_ref[0, :, window], (8, lane))
        taps = taps_ref[0, :, window]
        turned = jnp.take_along_axis(
            taps, (sublanes - spot) & 7, axis=0, mode="promise_in_bounds"
        )
        block = (spot >> 3) + jnp.where(sublanes < (spot & 7), 1, 0)
        high = turned.astype(bf16).astype(jnp.float32)
        low = turned - high
        here = [block == i for i in range(2 * lane // 8)]
        matrix = jnp.concatenate(
            [
                jnp.concatenate([jnp.where(m, high, 0.0) for m in here], axis=0).astype(bf16),
                jnp.concatenate([jnp.where(m, low, 0.0) for m in here], axis=0).astype(bf16),
            ],
            axis=1,
        )
        both = slice(u * lane, (u + 2) * lane)
        out = jnp.dot(image[:, both], matrix, preferred_element_type=jnp.float32)
        cells = out[:patch_rows, :lane] + out[:patch_rows, lane:] + out[patch_rows:, :lane]
        warped_ref[0, :, window] = cells
        at = 2 * (u // fold)
        spare = slice((tiles + 1 + u % fold) * lane, (tiles + 2 + u % fold) * lane)
        head_ref[0, :, window] = cells[:8]
        head_ref[0, at : at + 2, spare] = cells[8:10]
        tail_ref[0, :, window] = cells[patch_rows - 8 :]
        tail_ref[0, at : at + 2, spare] = cells[patch_rows - 10 : patch_rows - 8]


def warp_rows(first, count, turn, got, taps, shift, patch_rows):
    depth = got.shape[2]
    width = (depth // 2 + 1) * lane
    span = width + folded(width // lane) * lane
    edge = jax.ShapeDtypeStruct((count, 8, span), jnp.float32)
    return pl.pallas_call(
        functools.partial(warp_kernel, first),
        out_shape=(jax.ShapeDtypeStruct((count, patch_rows, width), jnp.float32), edge, edge),
        grid=(count,),
        in_specs=[
            pl.BlockSpec(memory_space=pltpu.SMEM),
            pl.BlockSpec(memory_space=pl.ANY),
            pl.BlockSpec((1,) + taps.shape[1:], lambda q: (q + first, 0, 0)),
            pl.BlockSpec((1,) + shift.shape[1:], lambda q: (q + first, 0, 0)),
        ],
        out_specs=[
            pl.BlockSpec((1, patch_rows, width), lambda q: (q, 0, 0)),
            *[pl.BlockSpec((1, 8, span), lambda q: (q, 0, 0))] * 2,
        ],
        scratch_shapes=[
            pltpu.VMEM((count, patch_rows // 2 * depth, lane), jnp.float32),
            pltpu.VMEM((2 * patch_rows, width + lane), bf16),
            pltpu.SemaphoreType.DMA((count,)),
        ],
        compiler_params=pltpu.CompilerParams(vmem_limit_bytes=room),
        cost_estimate=pl.CostEstimate(flops=0, bytes_accessed=12 * count << 20, transcendentals=0),
        name="warp_rows",
    )(turn, got, taps, shift)


def match_kernel(
    first,
    fresh,
    weight_ref,
    warped_ref,
    above_ref,
    below_ref,
    down_ref,
    across_ref,
    coef_ref,
    template_ref,
    before_ref,
    _,
    difference_ref,
    total_ref,
    pieces,
    high_refs,
    low_refs,
    found,
):
    patch_rows, row_width = template_ref.shape
    bases = across_ref.shape[0]
    windows = pieces.shape[1] // lane
    part = high_refs.shape[2] // lane
    tiles = warped_ref.shape[2] // lane
    fold = folded(tiles)
    inside = lax.broadcasted_iota(jnp.int32, (16, lane), 1)
    quarter = lax.broadcasted_iota(jnp.int32, (16, lane), 0) % 8 // 2

    def columns(tile):
        own = warped_ref[0, :, tile * lane : (tile + 1) * lane]
        edges = []
        for at in (tile, tiles + tile % fold):
            here = slice(at * lane, (at + 1) * lane)
            edges.append(jnp.concatenate([above_ref[0, :, here], below_ref[0, :, here]], axis=0))
        edges[1] = jnp.where(quarter == tile // fold, edges[1], 0.0)
        return [own[:16], own[16:], *edges]


    @pl.when(pl.program_id(0) == 0)
    def _():
        total_ref[...] = jnp.zeros_like(total_ref) if fresh else before_ref[...]

    def cut_window(w):
        start = step * w + half_lane - (lane - step) // 2
        tile, turn = start // lane, start % lane
        here = slice(w * lane, (w + 1) * lane)
        blocks = columns(tile)
        if turn:
            blocks = [
                jnp.where(
                    inside < lane - turn,
                    pltpu.roll(before, lane - turn, 1),
                    pltpu.roll(after, lane - turn, 1),
                )
                for before, after in zip(blocks, columns(tile + 1))
            ]
        for i, values in enumerate(blocks):
            high, low = split(values)
            for j, value in enumerate((high, low, high)):
                at = (j * len(blocks) + i) * 16
                pieces[at : at + 16, here] = value

    def part_step(p):
        for w in range(p * part, (p + 1) * part):
            cut_window(w)
        wide = slice(p * part * lane, (p + 1) * part * lane)
        high_ref = high_refs.at[p]
        low_ref = low_refs.at[p]
        vertical = jnp.dot(down_ref[...], pieces[:, wide], preferred_element_type=jnp.float32)
        high_ref[...], low_ref[...] = split(vertical)

        def gathered(ref, b):
            rows = slice(b * patch_rows, (b + 1) * patch_rows)
            return jnp.concatenate(
                [ref[rows, lane * i : lane * (i + 1)] for i in range(part)], axis=0
            )

        matched = jnp.zeros((part * patch_rows, lane), jnp.float32)
        for b in range(bases):
            operand = jnp.concatenate([gathered(high_ref, b), gathered(low_ref, b)], axis=1)
            both = jnp.dot(operand, across_ref[b], preferred_element_type=jnp.float32)
            scales = coef_ref[0, b : b + 1, wide]
            scale = jnp.concatenate(
                [
                    jnp.broadcast_to(scales[:, lane * i : lane * (i + 1)], (patch_rows, lane))
                    for i in range(part)
                ],
                axis=0,
            )
            matched = matched + scale * (both[:, :lane] + both[:, lane:])
        found[p * part * patch_rows : (p + 1) * part * patch_rows, :] = matched

    for p in range(windows // part):
        part_step(p)
    weight = weight_ref[first + pl.program_id(0)]
    inside = lax.broadcasted_iota(jnp.int32, (patch_rows, lane), 1)
    for tile in range(row_width // lane):
        piece = None
        for w in range(tile * lane // step, ((tile + 1) * lane - 1) // step + 1):
            start = step * w - tile * lane
            values = found[w * patch_rows : (w + 1) * patch_rows, :]
            if start % lane:
                values = pltpu.roll(values, start % lane, 1)
            piece = values if piece is None else jnp.where(inside < start, piece, values)
        here = slice(lane * tile, lane * (tile + 1))
        difference_ref[0, :, here] = piece - template_ref[:, here]
        total_ref[:, here] = total_ref[:, here] + weight * piece


def match_rows(
    first, weights, warped, above, below, down, across, coefs, template, before, difference
):
    count, _, width = warped.shape
    edge = above.shape[2]
    visits, bases, span = coefs.shape
    patch_rows, row_width = template.shape
    part = span // lane // parts
    fresh = before is None
    if fresh:
        before = template
    extra, aliases = [], {}
    if difference is not None:
        extra, aliases = [difference], {9: 0}
    kernel = functools.partial(match_kernel, first, fresh)
    if difference is None:

        def body(*refs):
            kernel(*refs[:9], None, *refs[9:])

    else:
        body = kernel
    rows_spec = pl.BlockSpec(template.shape, lambda q: (0, 0))
    return pl.pallas_call(
        body,
        out_shape=(
            jax.ShapeDtypeStruct((visits, patch_rows, row_width), jnp.float32),
            jax.ShapeDtypeStruct(template.shape, jnp.float32),
        ),
        grid=(count,),
        in_specs=[
            pl.BlockSpec(memory_space=pltpu.SMEM),
            pl.BlockSpec((1, patch_rows, width), lambda q: (q, 0, 0)),
            *[pl.BlockSpec((1, 8, edge), lambda q: (q, 0, 0))] * 2,
            pl.BlockSpec(down.shape, lambda q: (0, 0)),
            pl.BlockSpec(across.shape, lambda q: (0, 0, 0)),
            pl.BlockSpec((1, bases, span), lambda q: (q + first, 0, 0)),
            rows_spec,
            rows_spec,
        ]
        + [pl.BlockSpec(memory_space=pl.ANY)] * len(extra),
        out_specs=[
            pl.BlockSpec((1, patch_rows, row_width), lambda q: (q + first, 0, 0)),
            rows_spec,
        ],
        scratch_shapes=[
            pltpu.VMEM((down.shape[1], span), bf16),
            pltpu.VMEM((parts, down.shape[0], part * lane), bf16),
            pltpu.VMEM((parts, down.shape[0], part * lane), bf16),
            pltpu.VMEM((span // lane * patch_rows, lane), jnp.float32),
        ],
        input_output_aliases=aliases,
        compiler_params=pltpu.CompilerParams(vmem_limit_bytes=room),
        cost_estimate=pl.CostEstimate(flops=0, bytes_accessed=20 * count << 20, transcendentals=0),
        name="match_rows",
    )(weights, warped, above, below, down, across, coefs, template, before, *extra)


def sum_kernel(total_ref, scale_ref, out_ref, own, slots, own_sem, send_sems, recv_sems):
    me = lax.axis_index("visit")
    slabs = lax.axis_size("visit")
    rows = out_ref.shape[0]
    mesh_ids = pl.DeviceIdType.MESH
    mine = pltpu.make_async_copy(
        total_ref.at[pl.ds(pl.multiple_of(rows * me, rows), rows), :], own, own_sem
    )
    mine.start()
    barrier = pltpu.get_barrier_semaphore()
    for i in range(1, slabs):
        to = lax.rem(me + i, slabs)
        pl.semaphore_signal(barrier, inc=1, device_id={"visit": to}, device_id_type=mesh_ids)
    pl.semaphore_wait(barrier, slabs - 1)
    copies = []
    for i in range(1, slabs):
        to = lax.rem(me + i, slabs)
        copy = pltpu.make_async_remote_copy(
            src_ref=total_ref.at[pl.ds(pl.multiple_of(rows * to, rows), rows), :],
            dst_ref=slots.at[i - 1],
            send_sem=send_sems.at[i - 1],
            recv_sem=recv_sems.at[i - 1],
            device_id={"visit": to},
            device_id_type=mesh_ids,
        )
        copy.start()
        copies.append(copy)
    for copy in copies:
        copy.wait()
    mine.wait()
    result = own[...]
    for i in range(slabs - 1):
        result = result + slots[i]
    out_ref[...] = result / scale_ref[0]


def sum_visits(total, scale):
    slabs = lax.axis_size("visit")
    shape = (total.shape[0] // slabs, total.shape[1])
    return pl.pallas_call(
        sum_kernel,
        out_shape=jax.ShapeDtypeStruct(shape, jnp.float32),
        in_specs=[
            pl.BlockSpec(memory_space=pl.ANY),
            pl.BlockSpec(memory_space=pltpu.SMEM),
        ],
        out_specs=pl.BlockSpec(memory_space=pltpu.VMEM),
        scratch_shapes=[
            pltpu.VMEM(shape, jnp.float32),
            pltpu.VMEM((slabs - 1,) + shape, jnp.float32),
            pltpu.SemaphoreType.DMA,
            pltpu.SemaphoreType.DMA((slabs - 1,)),
            pltpu.SemaphoreType.DMA((slabs - 1,)),
        ],
        compiler_params=pltpu.CompilerParams(collective_id=0, has_side_effects=True),
        name="sum_visits",
    )(total, scale)


def split_table(values):
    high = lax.reduce_precision(values, 8, 7)
    return high.astype(bf16), (values - high).astype(bf16)


def taken(values, index):
    table = jnp.zeros((values.shape[0],) + index.shape, jnp.float32)
    for lag in range(values.shape[1]):
        table = jnp.where((index == lag)[None], values[:, lag].reshape(-1, 1, 1), table)
    return table


def on_device(
    ccd_rows,
    tract_row,
    warp_taps,
    warp_shift,
    basis_rows,
    basis_cols,
    coef_table,
    grid_index,
    template,
    visit_weight,
):
    visits, patch_rows, row_width = ccd_rows.shape
    patches = lax.axis_size("patch")
    here = lax.axis_index("patch")
    half = basis_rows.shape[1] // 2
    tiles = row_width // lane

    tiled_rows = ccd_rows.reshape(visits, patch_rows // 8, 8, tiles, lane).transpose(0, 1, 3, 2, 4)
    tiled_rows = tiled_rows.reshape(visits, patch_rows * tiles, lane)
    place = tract_row[0, 0]
    offset = place // patch_rows - here - (place % patch_rows) // 2
    turn = ((here - offset) % patches).astype(jnp.int32).reshape(1)
    taps = jnp.pad(warp_taps[:, 0], ((0, 0), (0, 0), (half_lane, half_lane)))
    shift = jnp.pad(warp_shift, ((0, 0), (0, 0), (half_lane, half_lane)))

    windows = -(-row_width // step)
    cells = jnp.pad(grid_index[0], (0, windows * step - row_width)).reshape(windows, step)
    cells = jnp.pad(cells, ((0, 0), (0, lane - step))).reshape(-1)
    one_hot = (cells[None, :] == jnp.arange(coef_table.shape[3])[:, None]).astype(jnp.float32)
    coefs = jnp.einsum(
        "qbg,gx->qbx", coef_table[:, 0], one_hot, precision=lax.Precision.HIGHEST
    )

    rows = jnp.arange(patch_rows)
    pair = jnp.arange(8)
    inner = jnp.concatenate(
        [rows, pair - 8, pair + patch_rows, pair % 2 - half, pair % 2 + patch_rows + half - 2]
    )
    down = taken(basis_rows, inner[None, :] - rows[:, None] + half).reshape(-1, inner.shape[0])
    down_high, down_low = split_table(down)
    down = jnp.concatenate([down_high, down_high, down_low], axis=1)
    out = jnp.arange(lane)[None, :]
    across = taken(
        basis_cols, jnp.where(out < step, jnp.arange(lane)[:, None] - out, basis_cols.shape[1])
    )
    high, low = split_table(across)
    across = jnp.concatenate(
        [
            jnp.concatenate([high, low], axis=2),
            jnp.concatenate([high, jnp.zeros_like(low)], axis=2),
        ],
        axis=1,
    )
    weights = lax.dynamic_slice_in_dim(
        visit_weight, lax.axis_index("visit") * visits, visits
    )

    starts = [sum(chunks[:i]) for i in range(len(chunks))]
    sent = pack_rows(0, visits, tract_row, tiled_rows, patches)
    got = lax.all_to_all(sent, "patch", split_axis=0, concat_axis=0, tiled=True)
    down_pairs = [(i, i + 1) for i in range(patches - 1)]
    up_pairs = [(i + 1, i) for i in range(patches - 1)]
    fields = []
    for first, count in zip(starts, chunks):
        warped, head, tail = warp_rows(first, count, turn, got, taps, shift, patch_rows)
        if fields:
            head, tail, fields[-1] = lax.optimization_barrier((head, tail, fields[-1]))
        above = lax.ppermute(tail, "patch", down_pairs)
        below = lax.ppermute(head, "patch", up_pairs)
        fields.append((warped, above, below))
    total, difference = None, None
    for first, field in zip(starts, fields):
        difference, total = match_rows(
            first, weights, *field, down, across, coefs, template, total, difference
        )
    coadd = sum_visits(total, jnp.sum(visit_weight).reshape(1))
    return difference, coadd


def solution(mesh):
    placed = (
        P("visit", "patch", None),
        P("visit", "patch"),
        P("visit", "patch", None, None),
        P("visit", "patch", None),
        P(),
        P(),
        P("visit", "patch", None, None),
        P("patch", None),
        P("patch", None),
        P(),
    )
    return jax.shard_map(
        on_device,
        mesh=mesh,
        in_specs=placed,
        out_specs=(P("visit", "patch", None), P(("patch", "visit"), None)),
        check_vma=False,
    )
```

```python
import functools

import jax
import jax.numpy as jnp
from jax import lax
from jax.experimental import pallas as pl
from jax.experimental.pallas import tpu as pltpu
from jax.sharding import PartitionSpec as P

lane = 128
half_lane = 64
step = 108
parts = 2
room = 24 << 20
chunks = (5, 3)
bf16 = jnp.bfloat16


def pack_kernel(first, places_ref, rows_ref, sent_ref):
    tiles = sent_ref.shape[2] // 2
    patch_rows = places_ref.shape[1]
    visit = first + pl.program_id(0)

    def step(row, carry):
        place = places_ref[visit, row]
        start = (row // 8) * (8 * tiles) + row % 8
        cells = rows_ref[0, pl.ds(start, tiles, stride=8), :]
        at = pl.multiple_of((place % 2) * tiles, tiles)
        sent_ref[place // patch_rows, 0, pl.ds(at, tiles), :] = cells
        return carry

    lax.fori_loop(0, patch_rows, step, 0, unroll=True)


def pack_rows(first, count, tract_row, tiled_rows, patches):
    visits, cells, _ = tiled_rows.shape
    tiles = cells // tract_row.shape[1]
    shape = (patches, count, 2 * tiles, lane)
    return pl.pallas_call(
        functools.partial(pack_kernel, first),
        out_shape=jax.ShapeDtypeStruct(shape, jnp.float32),
        grid=(count,),
        in_specs=[
            pl.BlockSpec(memory_space=pltpu.SMEM),
            pl.BlockSpec((1, cells, lane), lambda q: (q + first, 0, 0)),
        ],
        out_specs=pl.BlockSpec((patches, 1, 2 * tiles, lane), lambda q: (0, q, 0, 0)),
        compiler_params=pltpu.CompilerParams(vmem_limit_bytes=58 << 20),
        cost_estimate=pl.CostEstimate(flops=0, bytes_accessed=3 * count << 20, transcendentals=0),
        name="pack_rows",
    )(tract_row, tiled_rows)


def folded(tiles):
    return -(-tiles // 4)


def split(values):
    high = values.astype(bf16)
    low = (values - high.astype(jnp.float32)).astype(bf16)
    return high, low


def warp_kernel(
    first, turn_ref, got_ref, taps_ref, shift_ref, warped_ref, head_ref, tail_ref, rows, image, sems
):
    patches, _, depth = got_ref.shape[:3]
    tiles = depth // 2
    patch_rows = warped_ref.shape[1]
    groups = patch_rows // 8
    visit = pl.program_id(0)

    @pl.when(visit == 0)
    def _():
        def fetch(local, carry):
            for pair in range(patch_rows // 2):
                source = (turn_ref[0] + first + local - pair + 2 * patches) % patches
                pltpu.make_async_copy(
                    got_ref.at[source, local],
                    rows.at[local, pl.ds(pair * depth, depth), :],
                    sems.at[local],
                ).start()
            return carry

        lax.fori_loop(0, pl.num_programs(0), fetch, 0)
        blank = jnp.zeros((2 * patch_rows, lane), bf16)
        image[:, :lane] = blank
        image[:, (tiles + 1) * lane :] = blank

    pltpu.make_async_copy(rows.at[visit], rows.at[visit], sems.at[visit]).wait()

    def split_step(tile, carry):
        values = jnp.concatenate(
            [
                rows[visit, pl.ds(8 * g * tiles + tile, 8, stride=tiles), :]
                for g in range(groups)
            ],
            axis=0,
        )
        window = pl.ds(pl.multiple_of((tile + 1) * lane, lane), lane)
        image[:, window] = jnp.concatenate(split(values), axis=0)
        return carry

    lax.fori_loop(0, tiles, split_step, 0, unroll=4)
    columns = lax.broadcasted_iota(jnp.int32, (8, lane), 1) + half_lane
    sublanes = lax.broadcasted_iota(jnp.int32, (8, lane), 0)

    fold = folded(tiles + 1)
    for ref in (head_ref, tail_ref):
        ref[0, :, (tiles + 1) * lane :] = jnp.zeros((8, fold * lane), jnp.float32)
    for u in range(tiles + 1):
        window = slice(u * lane, (u + 1) * lane)
        spot = columns + jnp.broadcast_to(shift_ref[0, :, window], (8, lane))
        taps = taps_ref[0, :, window]
        turned = jnp.take_along_axis(
            taps, (sublanes - spot) & 7, axis=0, mode="promise_in_bounds"
        )
        block = (spot >> 3) + jnp.where(sublanes < (spot & 7), 1, 0)
        high = turned.astype(bf16).astype(jnp.float32)
        low = turned - high
        here = [block == i for i in range(2 * lane // 8)]
        matrix = jnp.concatenate(
            [
                jnp.concatenate([jnp.where(m, high, 0.0) for m in here], axis=0).astype(bf16),
                jnp.concatenate([jnp.where(m, low, 0.0) for m in here], axis=0).astype(bf16),
            ],
            axis=1,
        )
        both = slice(u * lane, (u + 2) * lane)
        out = jnp.dot(image[:, both], matrix, preferred_element_type=jnp.float32)
        cells = out[:patch_rows, :lane] + out[:patch_rows, lane:] + out[patch_rows:, :lane]
        warped_ref[0, :, window] = cells
        at = 2 * (u // fold)
        spare = slice((tiles + 1 + u % fold) * lane, (tiles + 2 + u % fold) * lane)
        head_ref[0, :, window] = cells[:8]
        head_ref[0, at : at + 2, spare] = cells[8:10]
        tail_ref[0, :, window] = cells[patch_rows - 8 :]
        tail_ref[0, at : at + 2, spare] = cells[patch_rows - 10 : patch_rows - 8]


def warp_rows(first, count, turn, got, taps, shift, patch_rows):
    depth = got.shape[2]
    width = (depth // 2 + 1) * lane
    span = width + folded(width // lane) * lane
    edge = jax.ShapeDtypeStruct((count, 8, span), jnp.float32)
    return pl.pallas_call(
        functools.partial(warp_kernel, first),
        out_shape=(jax.ShapeDtypeStruct((count, patch_rows, width), jnp.float32), edge, edge),
        grid=(count,),
        in_specs=[
            pl.BlockSpec(memory_space=pltpu.SMEM),
            pl.BlockSpec(memory_space=pl.ANY),
            pl.BlockSpec((1,) + taps.shape[1:], lambda q: (q + first, 0, 0)),
            pl.BlockSpec((1,) + shift.shape[1:], lambda q: (q + first, 0, 0)),
        ],
        out_specs=[
            pl.BlockSpec((1, patch_rows, width), lambda q: (q, 0, 0)),
            *[pl.BlockSpec((1, 8, span), lambda q: (q, 0, 0))] * 2,
        ],
        scratch_shapes=[
            pltpu.VMEM((count, patch_rows // 2 * depth, lane), jnp.float32),
            pltpu.VMEM((2 * patch_rows, width + lane), bf16),
            pltpu.SemaphoreType.DMA((count,)),
        ],
        compiler_params=pltpu.CompilerParams(vmem_limit_bytes=room),
        cost_estimate=pl.CostEstimate(flops=0, bytes_accessed=12 * count << 20, transcendentals=0),
        name="warp_rows",
    )(turn, got, taps, shift)


def match_kernel(
    first,
    fresh,
    weight_ref,
    warped_ref,
    above_ref,
    below_ref,
    down_ref,
    across_ref,
    coef_ref,
    template_ref,
    before_ref,
    _,
    difference_ref,
    total_ref,
    pieces,
    high_refs,
    low_refs,
    found,
):
    patch_rows, row_width = template_ref.shape
    bases = across_ref.shape[0]
    windows = pieces.shape[1] // lane
    part = high_refs.shape[2] // lane
    tiles = warped_ref.shape[2] // lane
    fold = folded(tiles)
    inside = lax.broadcasted_iota(jnp.int32, (16, lane), 1)
    quarter = lax.broadcasted_iota(jnp.int32, (16, lane), 0) % 8 // 2

    def columns(tile):
        own = warped_ref[0, :, tile * lane : (tile + 1) * lane]
        edges = []
        for at in (tile, tiles + tile % fold):
            here = slice(at * lane, (at + 1) * lane)
            edges.append(jnp.concatenate([above_ref[0, :, here], below_ref[0, :, here]], axis=0))
        edges[1] = jnp.where(quarter == tile // fold, edges[1], 0.0)
        return [own[:16], own[16:], *edges]


    @pl.when(pl.program_id(0) == 0)
    def _():
        total_ref[...] = jnp.zeros_like(total_ref) if fresh else before_ref[...]

    def cut_window(w):
        start = step * w + half_lane - (lane - step) // 2
        tile, turn = start // lane, start % lane
        here = slice(w * lane, (w + 1) * lane)
        blocks = columns(tile)
        if turn:
            blocks = [
                jnp.where(
                    inside < lane - turn,
                    pltpu.roll(before, lane - turn, 1),
                    pltpu.roll(after, lane - turn, 1),
                )
                for before, after in zip(blocks, columns(tile + 1))
            ]
        for i, values in enumerate(blocks):
            high, low = split(values)
            for j, value in enumerate((high, low, high)):
                at = (j * len(blocks) + i) * 16
                pieces[at : at + 16, here] = value

    def part_step(p):
        for w in range(p * part, (p + 1) * part):
            cut_window(w)
        wide = slice(p * part * lane, (p + 1) * part * lane)
        high_ref = high_refs.at[p]
        low_ref = low_refs.at[p]
        vertical = jnp.dot(down_ref[...], pieces[:, wide], preferred_element_type=jnp.float32)
        high_ref[...], low_ref[...] = split(vertical)

        def gathered(ref, b):
            rows = slice(b * patch_rows, (b + 1) * patch_rows)
            return jnp.concatenate(
                [ref[rows, lane * i : lane * (i + 1)] for i in range(part)], axis=0
            )

        matched = jnp.zeros((part * patch_rows, lane), jnp.float32)
        for b in range(bases):
            operand = jnp.concatenate([gathered(high_ref, b), gathered(low_ref, b)], axis=1)
            both = jnp.dot(operand, across_ref[b], preferred_element_type=jnp.float32)
            scales = coef_ref[0, b : b + 1, wide]
            scale = jnp.concatenate(
                [
                    jnp.broadcast_to(scales[:, lane * i : lane * (i + 1)], (patch_rows, lane))
                    for i in range(part)
                ],
                axis=0,
            )
            matched = matched + scale * (both[:, :lane] + both[:, lane:])
        found[p * part * patch_rows : (p + 1) * part * patch_rows, :] = matched

    for p in range(windows // part):
        part_step(p)
    weight = weight_ref[first + pl.program_id(0)]
    inside = lax.broadcasted_iota(jnp.int32, (patch_rows, lane), 1)
    for tile in range(row_width // lane):
        piece = None
        for w in range(tile * lane // step, ((tile + 1) * lane - 1) // step + 1):
            start = step * w - tile * lane
            values = found[w * patch_rows : (w + 1) * patch_rows, :]
            if start % lane:
                values = pltpu.roll(values, start % lane, 1)
            piece = values if piece is None else jnp.where(inside < start, piece, values)
        here = slice(lane * tile, lane * (tile + 1))
        difference_ref[0, :, here] = piece - template_ref[:, here]
        total_ref[:, here] = total_ref[:, here] + weight * piece


def spread_kernel(
    weight_ref,
    warped_ref,
    down_ref,
    across_ref,
    coef_ref,
    coef_up_ref,
    coef_dn_ref,
    template_ref,
    difference_ref,
    total_ref,
    up_ref,
    dn_ref,
    pieces,
    high_refs,
    low_refs,
    found,
):
    patch_rows, row_width = template_ref.shape
    rows_out = patch_rows + 32
    bases = across_ref.shape[0]
    windows = pieces.shape[1] // lane
    part = high_refs.shape[2] // lane
    inside = lax.broadcasted_iota(jnp.int32, (patch_rows, lane), 1)

    @pl.when(pl.program_id(0) == 0)
    def _():
        total_ref[...] = jnp.zeros_like(total_ref)

    for p in range(windows // part):
        for w in range(p * part, (p + 1) * part):
            start = step * w + half_lane - (lane - step) // 2
            tile, turn = start // lane, start % lane
            values = warped_ref[0, :, tile * lane : (tile + 1) * lane]
            if turn:
                after = warped_ref[0, :, (tile + 1) * lane : (tile + 2) * lane]
                values = jnp.where(
                    inside < lane - turn,
                    pltpu.roll(values, lane - turn, 1),
                    pltpu.roll(after, lane - turn, 1),
                )
            high, low = split(values)
            here = slice(w * lane, (w + 1) * lane)
            for j, value in enumerate((high, low, high)):
                pieces[j * patch_rows : (j + 1) * patch_rows, here] = value
        wide = slice(p * part * lane, (p + 1) * part * lane)
        vertical = jnp.dot(down_ref[...], pieces[:, wide], preferred_element_type=jnp.float32)
        high_refs[p], low_refs[p] = split(vertical)

        def gathered(refs, b):
            rows = slice(b * rows_out, (b + 1) * rows_out)
            return jnp.concatenate(
                [refs[p, rows, lane * i : lane * (i + 1)] for i in range(part)], axis=0
            )

        matched = jnp.zeros((part * rows_out, lane), jnp.float32)
        for b in range(bases):
            operand = jnp.concatenate([gathered(high_refs, b), gathered(low_refs, b)], axis=1)
            both = jnp.dot(operand, across_ref[b], preferred_element_type=jnp.float32)
            scales = []
            for w in range(p * part, (p + 1) * part):
                here = slice(w * lane, (w + 1) * lane)
                for ref, count in ((coef_ref, patch_rows), (coef_up_ref, 16), (coef_dn_ref, 16)):
                    scales.append(jnp.broadcast_to(ref[0, b : b + 1, here], (count, lane)))
            matched = matched + jnp.concatenate(scales, axis=0) * (both[:, :lane] + both[:, lane:])
        found[p * part * rows_out : (p + 1) * part * rows_out, :] = matched
    weight = weight_ref[pl.program_id(0)]
    inside = lax.broadcasted_iota(jnp.int32, (rows_out, lane), 1)
    tiles = row_width // lane
    fold = folded(tiles)
    for tile in range(tiles):
        piece = None
        for w in range(tile * lane // step, ((tile + 1) * lane - 1) // step + 1):
            start = step * w - tile * lane
            values = found[w * rows_out : (w + 1) * rows_out, :]
            if start % lane:
                values = pltpu.roll(values, start % lane, 1)
            piece = values if piece is None else jnp.where(inside < start, piece, values)
        here = slice(lane * tile, lane * (tile + 1))
        own, above, below = piece[:patch_rows], piece[patch_rows : patch_rows + 16], piece[-16:]
        difference_ref[0, :, here] = own - template_ref[:, here]
        total_ref[:, here] = total_ref[:, here] + weight * own
        at = 2 * (tile // fold)
        spare = slice((tiles + tile % fold) * lane, (tiles + tile % fold + 1) * lane)
        up_ref[0, :, here] = above[8:]
        up_ref[0, at : at + 2, spare] = above[6:8]
        dn_ref[0, :, here] = below[:8]
        dn_ref[0, at : at + 2, spare] = below[8:10]


def spread_rows(weights, warped, down, across, coefs, coefs_up, coefs_dn, template):
    count, patch_rows, width = warped.shape
    visits, bases, span = coefs.shape
    row_width = template.shape[1]
    part = span // lane // parts
    edge = row_width + folded(row_width // lane) * lane
    coef_spec = pl.BlockSpec((1, bases, span), lambda q: (q, 0, 0))
    edge_spec = pl.BlockSpec((1, 8, edge), lambda q: (q, 0, 0))
    return pl.pallas_call(
        spread_kernel,
        out_shape=(
            jax.ShapeDtypeStruct((visits, patch_rows, row_width), jnp.float32),
            jax.ShapeDtypeStruct(template.shape, jnp.float32),
            jax.ShapeDtypeStruct((count, 8, edge), jnp.float32),
            jax.ShapeDtypeStruct((count, 8, edge), jnp.float32),
        ),
        grid=(count,),
        in_specs=[
            pl.BlockSpec(memory_space=pltpu.SMEM),
            pl.BlockSpec((1, patch_rows, width), lambda q: (q, 0, 0)),
            pl.BlockSpec(down.shape, lambda q: (0, 0)),
            pl.BlockSpec(across.shape, lambda q: (0, 0, 0)),
            coef_spec,
            coef_spec,
            coef_spec,
            pl.BlockSpec(template.shape, lambda q: (0, 0)),
        ],
        out_specs=[
            pl.BlockSpec((1, patch_rows, row_width), lambda q: (q, 0, 0)),
            pl.BlockSpec(template.shape, lambda q: (0, 0)),
            edge_spec,
            edge_spec,
        ],
        scratch_shapes=[
            pltpu.VMEM((down.shape[1], span), bf16),
            pltpu.VMEM((parts, down.shape[0], part * lane), bf16),
            pltpu.VMEM((parts, down.shape[0], part * lane), bf16),
            pltpu.VMEM((span // lane * (patch_rows + 32), lane), jnp.float32),
        ],
        compiler_params=pltpu.CompilerParams(vmem_limit_bytes=40 << 20),
        cost_estimate=pl.CostEstimate(flops=0, bytes_accessed=24 * count << 20, transcendentals=0),
        name="spread_rows",
    )(weights, warped, down, across, coefs, coefs_up, coefs_dn, template)


def add_kernel(
    weight_ref, above_ref, below_ref, before_ref, sums_ref, difference_ref, total_ref
):
    _, patch_rows, row_width = before_ref.shape
    tiles = row_width // lane
    fold = folded(tiles)
    weight = weight_ref[pl.program_id(0)]

    @pl.when(pl.program_id(0) == 0)
    def _():
        total_ref[...] = sums_ref[...]

    difference_ref[0, 10 : patch_rows - 10, :] = before_ref[0, 10 : patch_rows - 10, :]
    for tile in range(tiles):
        here = slice(lane * tile, lane * (tile + 1))
        at = 2 * (tile // fold)
        spare = slice((tiles + tile % fold) * lane, (tiles + tile % fold + 1) * lane)
        for first, ref, rows, columns in (
            (0, above_ref, slice(0, 8), here),
            (8, above_ref, slice(at, at + 2), spare),
            (patch_rows - 10, below_ref, slice(at, at + 2), spare),
            (patch_rows - 8, below_ref, slice(0, 8), here),
        ):
            values = ref[0, rows, columns]
            to = slice(first, first + rows.stop - rows.start)
            difference_ref[0, to, here] = before_ref[0, to, here] + values
            total_ref[to, here] = total_ref[to, here] + weight * values


def add_edges(weights, above, below, difference, total):
    count, _, edge = above.shape
    _, patch_rows, row_width = difference.shape
    row_spec = pl.BlockSpec((1, patch_rows, row_width), lambda q: (q, 0, 0))
    edge_spec = pl.BlockSpec((1, 8, edge), lambda q: (q, 0, 0))
    total_spec = pl.BlockSpec(total.shape, lambda q: (0, 0))
    return pl.pallas_call(
        add_kernel,
        out_shape=(
            jax.ShapeDtypeStruct(difference.shape, jnp.float32),
            jax.ShapeDtypeStruct(total.shape, jnp.float32),
        ),
        grid=(count,),
        in_specs=[
            pl.BlockSpec(memory_space=pltpu.SMEM),
            edge_spec,
            edge_spec,
            row_spec,
            total_spec,
        ],
        out_specs=[row_spec, total_spec],
        input_output_aliases={3: 0},
        compiler_params=pltpu.CompilerParams(vmem_limit_bytes=room),
        cost_estimate=pl.CostEstimate(flops=0, bytes_accessed=3 * count << 20, transcendentals=0),
        name="add_edges",
    )(weights, above, below, difference, total)


def match_rows(
    first, weights, warped, above, below, down, across, coefs, template, before, difference
):
    count, _, width = warped.shape
    edge = above.shape[2]
    visits, bases, span = coefs.shape
    patch_rows, row_width = template.shape
    part = span // lane // parts
    fresh = before is None
    if fresh:
        before = template
    extra, aliases = [], {}
    if difference is not None:
        extra, aliases = [difference], {9: 0}
    kernel = functools.partial(match_kernel, first, fresh)
    if difference is None:

        def body(*refs):
            kernel(*refs[:9], None, *refs[9:])

    else:
        body = kernel
    rows_spec = pl.BlockSpec(template.shape, lambda q: (0, 0))
    return pl.pallas_call(
        body,
        out_shape=(
            jax.ShapeDtypeStruct((visits, patch_rows, row_width), jnp.float32),
            jax.ShapeDtypeStruct(template.shape, jnp.float32),
        ),
        grid=(count,),
        in_specs=[
            pl.BlockSpec(memory_space=pltpu.SMEM),
            pl.BlockSpec((1, patch_rows, width), lambda q: (q, 0, 0)),
            *[pl.BlockSpec((1, 8, edge), lambda q: (q, 0, 0))] * 2,
            pl.BlockSpec(down.shape, lambda q: (0, 0)),
            pl.BlockSpec(across.shape, lambda q: (0, 0, 0)),
            pl.BlockSpec((1, bases, span), lambda q: (q + first, 0, 0)),
            rows_spec,
            rows_spec,
        ]
        + [pl.BlockSpec(memory_space=pl.ANY)] * len(extra),
        out_specs=[
            pl.BlockSpec((1, patch_rows, row_width), lambda q: (q + first, 0, 0)),
            rows_spec,
        ],
        scratch_shapes=[
            pltpu.VMEM((down.shape[1], span), bf16),
            pltpu.VMEM((parts, down.shape[0], part * lane), bf16),
            pltpu.VMEM((parts, down.shape[0], part * lane), bf16),
            pltpu.VMEM((span // lane * patch_rows, lane), jnp.float32),
        ],
        input_output_aliases=aliases,
        compiler_params=pltpu.CompilerParams(vmem_limit_bytes=room),
        cost_estimate=pl.CostEstimate(flops=0, bytes_accessed=20 * count << 20, transcendentals=0),
        name="match_rows",
    )(weights, warped, above, below, down, across, coefs, template, before, *extra)


def sum_kernel(total_ref, scale_ref, out_ref, own, slots, own_sem, send_sems, recv_sems):
    me = lax.axis_index("visit")
    slabs = lax.axis_size("visit")
    rows = out_ref.shape[0]
    mesh_ids = pl.DeviceIdType.MESH
    mine = pltpu.make_async_copy(
        total_ref.at[pl.ds(pl.multiple_of(rows * me, rows), rows), :], own, own_sem
    )
    mine.start()
    barrier = pltpu.get_barrier_semaphore()
    for i in range(1, slabs):
        to = lax.rem(me + i, slabs)
        pl.semaphore_signal(barrier, inc=1, device_id={"visit": to}, device_id_type=mesh_ids)
    pl.semaphore_wait(barrier, slabs - 1)
    copies = []
    for i in range(1, slabs):
        to = lax.rem(me + i, slabs)
        copy = pltpu.make_async_remote_copy(
            src_ref=total_ref.at[pl.ds(pl.multiple_of(rows * to, rows), rows), :],
            dst_ref=slots.at[i - 1],
            send_sem=send_sems.at[i - 1],
            recv_sem=recv_sems.at[i - 1],
            device_id={"visit": to},
            device_id_type=mesh_ids,
        )
        copy.start()
        copies.append(copy)
    for copy in copies:
        copy.wait()
    mine.wait()
    result = own[...]
    for i in range(slabs - 1):
        result = result + slots[i]
    out_ref[...] = result / scale_ref[0]


def sum_visits(total, scale):
    slabs = lax.axis_size("visit")
    shape = (total.shape[0] // slabs, total.shape[1])
    return pl.pallas_call(
        sum_kernel,
        out_shape=jax.ShapeDtypeStruct(shape, jnp.float32),
        in_specs=[
            pl.BlockSpec(memory_space=pl.ANY),
            pl.BlockSpec(memory_space=pltpu.SMEM),
        ],
        out_specs=pl.BlockSpec(memory_space=pltpu.VMEM),
        scratch_shapes=[
            pltpu.VMEM(shape, jnp.float32),
            pltpu.VMEM((slabs - 1,) + shape, jnp.float32),
            pltpu.SemaphoreType.DMA,
            pltpu.SemaphoreType.DMA((slabs - 1,)),
            pltpu.SemaphoreType.DMA((slabs - 1,)),
        ],
        compiler_params=pltpu.CompilerParams(collective_id=0, has_side_effects=True),
        name="sum_visits",
    )(total, scale)


def split_table(values):
    high = lax.reduce_precision(values, 8, 7)
    return high.astype(bf16), (values - high).astype(bf16)


def taken(values, index):
    table = jnp.zeros((values.shape[0],) + index.shape, jnp.float32)
    for lag in range(values.shape[1]):
        table = jnp.where((index == lag)[None], values[:, lag].reshape(-1, 1, 1), table)
    return table


def on_device(
    ccd_rows,
    tract_row,
    warp_taps,
    warp_shift,
    basis_rows,
    basis_cols,
    coef_table,
    grid_index,
    template,
    visit_weight,
):
    visits, patch_rows, row_width = ccd_rows.shape
    patches = lax.axis_size("patch")
    here = lax.axis_index("patch")
    half = basis_rows.shape[1] // 2
    tiles = row_width // lane

    tiled_rows = ccd_rows.reshape(visits, patch_rows // 8, 8, tiles, lane).transpose(0, 1, 3, 2, 4)
    tiled_rows = tiled_rows.reshape(visits, patch_rows * tiles, lane)
    place = tract_row[0, 0]
    offset = place // patch_rows - here - (place % patch_rows) // 2
    turn = ((here - offset) % patches).astype(jnp.int32).reshape(1)
    taps = jnp.pad(warp_taps[:, 0], ((0, 0), (0, 0), (half_lane, half_lane)))
    shift = jnp.pad(warp_shift, ((0, 0), (0, 0), (half_lane, half_lane)))

    def windowed_coefs(table, grid):
        windows = -(-row_width // step)
        cells = jnp.pad(grid, (0, windows * step - row_width)).reshape(windows, step)
        cells = jnp.pad(cells, ((0, 0), (0, lane - step))).reshape(-1)
        one_hot = (cells[None, :] == jnp.arange(table.shape[2])[:, None]).astype(jnp.float32)
        return jnp.einsum("qbg,gx->qbx", table, one_hot, precision=lax.Precision.HIGHEST)

    down_pairs = [(i, i + 1) for i in range(patches - 1)]
    up_pairs = [(i + 1, i) for i in range(patches - 1)]
    table = coef_table[:, 0]
    coefs = windowed_coefs(table, grid_index[0])

    rows = jnp.arange(patch_rows)
    pair = jnp.arange(8)
    inner = jnp.concatenate(
        [rows, pair - 8, pair + patch_rows, pair % 2 - half, pair % 2 + patch_rows + half - 2]
    )
    down = taken(basis_rows, inner[None, :] - rows[:, None] + half).reshape(-1, inner.shape[0])
    down_high, down_low = split_table(down)
    down = jnp.concatenate([down_high, down_high, down_low], axis=1)
    outer = jnp.concatenate([rows, jnp.arange(16) - 16, jnp.arange(16) + patch_rows])
    wide = taken(basis_rows, rows[None, :] - outer[:, None] + half).reshape(-1, patch_rows)
    wide_high, wide_low = split_table(wide)
    wide = jnp.concatenate([wide_high, wide_high, wide_low], axis=1)
    out = jnp.arange(lane)[None, :]
    across = taken(
        basis_cols, jnp.where(out < step, jnp.arange(lane)[:, None] - out, basis_cols.shape[1])
    )
    high, low = split_table(across)
    across = jnp.concatenate(
        [
            jnp.concatenate([high, low], axis=2),
            jnp.concatenate([high, jnp.zeros_like(low)], axis=2),
        ],
        axis=1,
    )
    weights = lax.dynamic_slice_in_dim(
        visit_weight, lax.axis_index("visit") * visits, visits
    )

    early, late = chunks
    sent = [
        pack_rows(first, count, tract_row, tiled_rows, patches)
        for first, count in ((0, early), (early, late))
    ]
    packed = jnp.concatenate([table.reshape(-1), grid_index[0].astype(jnp.float32)])
    nearby = [lax.ppermute(packed, "patch", pairs) for pairs in (down_pairs, up_pairs)]
    sent[1], down, wide, across, coefs, taps, shift, weights, turn, nearby = (
        lax.optimization_barrier(
            (sent[1], down, wide, across, coefs, taps, shift, weights, turn, nearby)
        )
    )
    got = [lax.all_to_all(block, "patch", split_axis=0, concat_axis=0, tiled=True) for block in sent]

    def neighbour_coefs(values):
        cells = values[table.size :].astype(jnp.int32)
        return windowed_coefs(values[: table.size].reshape(table.shape), cells)

    warped, _, _ = warp_rows(0, early, turn, got[0], taps, shift, patch_rows)
    difference, total, up, dn = spread_rows(
        weights,
        warped,
        wide,
        across,
        coefs,
        *map(neighbour_coefs, nearby),
        template,
    )
    from_above = lax.ppermute(dn, "patch", down_pairs)
    from_below = lax.ppermute(up, "patch", up_pairs)
    turn, total = lax.optimization_barrier((turn, total))
    warped, head, tail = warp_rows(early, late, turn, got[1], taps, shift, patch_rows)
    above = lax.ppermute(tail, "patch", down_pairs)
    below = lax.ppermute(head, "patch", up_pairs)
    from_above, from_below, warped = lax.optimization_barrier((from_above, from_below, warped))
    difference, total = add_edges(weights, from_above, from_below, difference, total)
    difference, total = match_rows(
        early, weights, warped, above, below, down, across, coefs, template, total, difference
    )
    coadd = sum_visits(total, jnp.sum(visit_weight).reshape(1))
    return difference, coadd


def solution(mesh):
    placed = (
        P("visit", "patch", None),
        P("visit", "patch"),
        P("visit", "patch", None, None),
        P("visit", "patch", None),
        P(),
        P(),
        P("visit", "patch", None, None),
        P("patch", None),
        P("patch", None),
        P(),
    )
    return jax.shard_map(
        on_device,
        mesh=mesh,
        in_specs=placed,
        out_specs=(P("visit", "patch", None), P(("patch", "visit"), None)),
        check_vma=False,
    )
```

```python
import functools

import jax
import jax.numpy as jnp
from jax import lax
from jax.experimental import pallas as pl
from jax.experimental.pallas import tpu as pltpu
from jax.sharding import PartitionSpec as P

lane = 128
half_lane = 64
step = 108
parts = 2
whole = 58 << 20
chunks = (5, 3)
bf16 = jnp.bfloat16


def pack_kernel(first, places_ref, rows_ref, sent_ref):
    tiles = sent_ref.shape[2] // 2
    patch_rows = places_ref.shape[1]
    visit = first + pl.program_id(0)

    def step(row, carry):
        place = places_ref[visit, row]
        start = (row // 8) * (8 * tiles) + row % 8
        cells = rows_ref[0, pl.ds(start, tiles, stride=8), :]
        at = pl.multiple_of((place % 2) * tiles, tiles)
        sent_ref[place // patch_rows, 0, pl.ds(at, tiles), :] = cells
        return carry

    lax.fori_loop(0, patch_rows, step, 0, unroll=True)


def pack_rows(first, count, tract_row, tiled_rows, patches):
    visits, cells, _ = tiled_rows.shape
    tiles = cells // tract_row.shape[1]
    shape = (patches, count, 2 * tiles, lane)
    return pl.pallas_call(
        functools.partial(pack_kernel, first),
        out_shape=jax.ShapeDtypeStruct(shape, jnp.float32),
        grid=(count,),
        in_specs=[
            pl.BlockSpec(memory_space=pltpu.SMEM),
            pl.BlockSpec((1, cells, lane), lambda q: (q + first, 0, 0)),
        ],
        out_specs=pl.BlockSpec((patches, 1, 2 * tiles, lane), lambda q: (0, q, 0, 0)),
        compiler_params=pltpu.CompilerParams(vmem_limit_bytes=whole),
        cost_estimate=pl.CostEstimate(flops=0, bytes_accessed=3 * count << 20, transcendentals=0),
        name="pack_rows",
    )(tract_row, tiled_rows)


def folded(tiles):
    return -(-tiles // 4)


def split(values):
    high = values.astype(bf16)
    low = (values - high.astype(jnp.float32)).astype(bf16)
    return high, low


def warp_kernel(
    first, turn_ref, got_ref, taps_ref, shift_ref, warped_ref, head_ref, tail_ref, rows, image, sems
):
    patches, _, depth = got_ref.shape[:3]
    tiles = depth // 2
    patch_rows = warped_ref.shape[1]
    groups = patch_rows // 8
    visit = pl.program_id(0)

    @pl.when(visit == 0)
    def _():
        def fetch(local, carry):
            for pair in range(patch_rows // 2):
                source = (turn_ref[0] + first + local - pair + 2 * patches) % patches
                pltpu.make_async_copy(
                    got_ref.at[source, local],
                    rows.at[local, pl.ds(pair * depth, depth), :],
                    sems.at[local],
                ).start()
            return carry

        lax.fori_loop(0, pl.num_programs(0), fetch, 0)
        blank = jnp.zeros((2 * patch_rows, lane), bf16)
        image[:, :lane] = blank
        image[:, (tiles + 1) * lane :] = blank

    pltpu.make_async_copy(rows.at[visit], rows.at[visit], sems.at[visit]).wait()

    def split_step(tile, carry):
        values = jnp.concatenate(
            [
                rows[visit, pl.ds(8 * g * tiles + tile, 8, stride=tiles), :]
                for g in range(groups)
            ],
            axis=0,
        )
        window = pl.ds(pl.multiple_of((tile + 1) * lane, lane), lane)
        image[:, window] = jnp.concatenate(split(values), axis=0)
        return carry

    lax.fori_loop(0, tiles, split_step, 0, unroll=4)
    columns = lax.broadcasted_iota(jnp.int32, (8, lane), 1) + half_lane
    sublanes = lax.broadcasted_iota(jnp.int32, (8, lane), 0)

    fold = folded(tiles + 1)
    for ref in (head_ref, tail_ref):
        ref[0, :, (tiles + 1) * lane :] = jnp.zeros((8, fold * lane), jnp.float32)
    for u in range(tiles + 1):
        window = slice(u * lane, (u + 1) * lane)
        spot = columns + jnp.broadcast_to(shift_ref[0, :, window], (8, lane))
        taps = taps_ref[0, :, window]
        turned = jnp.take_along_axis(
            taps, (sublanes - spot) & 7, axis=0, mode="promise_in_bounds"
        )
        block = (spot >> 3) + jnp.where(sublanes < (spot & 7), 1, 0)
        high = turned.astype(bf16).astype(jnp.float32)
        low = turned - high
        here = [block == i for i in range(2 * lane // 8)]
        matrix = jnp.concatenate(
            [
                jnp.concatenate([jnp.where(m, high, 0.0) for m in here], axis=0).astype(bf16),
                jnp.concatenate([jnp.where(m, low, 0.0) for m in here], axis=0).astype(bf16),
            ],
            axis=1,
        )
        both = slice(u * lane, (u + 2) * lane)
        out = jnp.dot(image[:, both], matrix, preferred_element_type=jnp.float32)
        cells = out[:patch_rows, :lane] + out[:patch_rows, lane:] + out[patch_rows:, :lane]
        warped_ref[0, :, window] = cells
        at = 2 * (u // fold)
        spare = slice((tiles + 1 + u % fold) * lane, (tiles + 2 + u % fold) * lane)
        head_ref[0, :, window] = cells[:8]
        head_ref[0, at : at + 2, spare] = cells[8:10]
        tail_ref[0, :, window] = cells[patch_rows - 8 :]
        tail_ref[0, at : at + 2, spare] = cells[patch_rows - 10 : patch_rows - 8]


def warp_rows(first, count, turn, got, taps, shift, patch_rows):
    depth = got.shape[2]
    width = (depth // 2 + 1) * lane
    span = width + folded(width // lane) * lane
    edge = jax.ShapeDtypeStruct((count, 8, span), jnp.float32)
    return pl.pallas_call(
        functools.partial(warp_kernel, first),
        out_shape=(jax.ShapeDtypeStruct((count, patch_rows, width), jnp.float32), edge, edge),
        grid=(count,),
        in_specs=[
            pl.BlockSpec(memory_space=pltpu.SMEM),
            pl.BlockSpec(memory_space=pl.ANY),
            pl.BlockSpec((1,) + taps.shape[1:], lambda q: (q + first, 0, 0)),
            pl.BlockSpec((1,) + shift.shape[1:], lambda q: (q + first, 0, 0)),
        ],
        out_specs=[
            pl.BlockSpec((1, patch_rows, width), lambda q: (q, 0, 0)),
            *[pl.BlockSpec((1, 8, span), lambda q: (q, 0, 0))] * 2,
        ],
        scratch_shapes=[
            pltpu.VMEM((count, patch_rows // 2 * depth, lane), jnp.float32),
            pltpu.VMEM((2 * patch_rows, width + lane), bf16),
            pltpu.SemaphoreType.DMA((count,)),
        ],
        compiler_params=pltpu.CompilerParams(vmem_limit_bytes=52 << 20),
        cost_estimate=pl.CostEstimate(flops=0, bytes_accessed=12 * count << 20, transcendentals=0),
        name="warp_rows",
    )(turn, got, taps, shift)


def match_kernel(
    first,
    fresh,
    weight_ref,
    warped_ref,
    above_ref,
    below_ref,
    down_ref,
    across_ref,
    coef_ref,
    template_ref,
    before_ref,
    _,
    difference_ref,
    total_ref,
    pieces,
    high_refs,
    low_refs,
    found,
):
    patch_rows, row_width = template_ref.shape
    bases = across_ref.shape[0]
    windows = pieces.shape[1] // lane
    part = high_refs.shape[2] // lane
    tiles = warped_ref.shape[2] // lane
    fold = folded(tiles)
    inside = lax.broadcasted_iota(jnp.int32, (16, lane), 1)
    quarter = lax.broadcasted_iota(jnp.int32, (16, lane), 0) % 8 // 2

    def columns(tile):
        own = warped_ref[0, :, tile * lane : (tile + 1) * lane]
        edges = []
        for at in (tile, tiles + tile % fold):
            here = slice(at * lane, (at + 1) * lane)
            edges.append(jnp.concatenate([above_ref[0, :, here], below_ref[0, :, here]], axis=0))
        edges[1] = jnp.where(quarter == tile // fold, edges[1], 0.0)
        return [own[:16], own[16:], *edges]


    @pl.when(pl.program_id(0) == 0)
    def _():
        total_ref[...] = jnp.zeros_like(total_ref) if fresh else before_ref[...]

    def cut_window(w):
        start = step * w + half_lane - (lane - step) // 2
        tile, turn = start // lane, start % lane
        here = slice(w * lane, (w + 1) * lane)
        blocks = columns(tile)
        if turn:
            blocks = [
                jnp.where(
                    inside < lane - turn,
                    pltpu.roll(before, lane - turn, 1),
                    pltpu.roll(after, lane - turn, 1),
                )
                for before, after in zip(blocks, columns(tile + 1))
            ]
        for i, values in enumerate(blocks):
            high, low = split(values)
            for j, value in enumerate((high, low, high)):
                at = (j * len(blocks) + i) * 16
                pieces[at : at + 16, here] = value

    def part_step(p):
        for w in range(p * part, (p + 1) * part):
            cut_window(w)
        wide = slice(p * part * lane, (p + 1) * part * lane)
        high_ref = high_refs.at[p]
        low_ref = low_refs.at[p]
        vertical = jnp.dot(down_ref[...], pieces[:, wide], preferred_element_type=jnp.float32)
        high_ref[...], low_ref[...] = split(vertical)

        def gathered(ref, b):
            rows = slice(b * patch_rows, (b + 1) * patch_rows)
            return jnp.concatenate(
                [ref[rows, lane * i : lane * (i + 1)] for i in range(part)], axis=0
            )

        matched = jnp.zeros((part * patch_rows, lane), jnp.float32)
        for b in range(bases):
            operand = jnp.concatenate([gathered(high_ref, b), gathered(low_ref, b)], axis=1)
            both = jnp.dot(operand, across_ref[b], preferred_element_type=jnp.float32)
            scales = coef_ref[0, b : b + 1, wide]
            scale = jnp.concatenate(
                [
                    jnp.broadcast_to(scales[:, lane * i : lane * (i + 1)], (patch_rows, lane))
                    for i in range(part)
                ],
                axis=0,
            )
            matched = matched + scale * (both[:, :lane] + both[:, lane:])
        found[p * part * patch_rows : (p + 1) * part * patch_rows, :] = matched

    for p in range(windows // part):
        part_step(p)
    weight = weight_ref[first + pl.program_id(0)]
    inside = lax.broadcasted_iota(jnp.int32, (patch_rows, lane), 1)
    for tile in range(row_width // lane):
        piece = None
        for w in range(tile * lane // step, ((tile + 1) * lane - 1) // step + 1):
            start = step * w - tile * lane
            values = found[w * patch_rows : (w + 1) * patch_rows, :]
            if start % lane:
                values = pltpu.roll(values, start % lane, 1)
            piece = values if piece is None else jnp.where(inside < start, piece, values)
        here = slice(lane * tile, lane * (tile + 1))
        difference_ref[0, :, here] = piece - template_ref[:, here]
        total_ref[:, here] = total_ref[:, here] + weight * piece


def spread_kernel(
    weight_ref,
    warped_ref,
    down_ref,
    across_ref,
    coef_ref,
    coef_up_ref,
    coef_dn_ref,
    template_ref,
    difference_ref,
    total_ref,
    up_ref,
    dn_ref,
    pieces,
    high_refs,
    low_refs,
    found,
):
    patch_rows, row_width = template_ref.shape
    rows_out = patch_rows + 32
    bases = across_ref.shape[0]
    windows = pieces.shape[1] // lane
    part = high_refs.shape[2] // lane
    inside = lax.broadcasted_iota(jnp.int32, (patch_rows, lane), 1)

    @pl.when(pl.program_id(0) == 0)
    def _():
        total_ref[...] = jnp.zeros_like(total_ref)

    for p in range(windows // part):
        for w in range(p * part, (p + 1) * part):
            start = step * w + half_lane - (lane - step) // 2
            tile, turn = start // lane, start % lane
            values = warped_ref[0, :, tile * lane : (tile + 1) * lane]
            if turn:
                after = warped_ref[0, :, (tile + 1) * lane : (tile + 2) * lane]
                values = jnp.where(
                    inside < lane - turn,
                    pltpu.roll(values, lane - turn, 1),
                    pltpu.roll(after, lane - turn, 1),
                )
            high, low = split(values)
            here = slice(w * lane, (w + 1) * lane)
            for j, value in enumerate((high, low, high)):
                pieces[j * patch_rows : (j + 1) * patch_rows, here] = value
        wide = slice(p * part * lane, (p + 1) * part * lane)
        vertical = jnp.dot(down_ref[...], pieces[:, wide], preferred_element_type=jnp.float32)
        high_refs[p], low_refs[p] = split(vertical)

        def gathered(refs, b):
            rows = slice(b * rows_out, (b + 1) * rows_out)
            return jnp.concatenate(
                [refs[p, rows, lane * i : lane * (i + 1)] for i in range(part)], axis=0
            )

        matched = jnp.zeros((part * rows_out, lane), jnp.float32)
        for b in range(bases):
            operand = jnp.concatenate([gathered(high_refs, b), gathered(low_refs, b)], axis=1)
            both = jnp.dot(operand, across_ref[b], preferred_element_type=jnp.float32)
            scales = []
            for w in range(p * part, (p + 1) * part):
                here = slice(w * lane, (w + 1) * lane)
                for ref, count in ((coef_ref, patch_rows), (coef_up_ref, 16), (coef_dn_ref, 16)):
                    scales.append(jnp.broadcast_to(ref[0, b : b + 1, here], (count, lane)))
            matched = matched + jnp.concatenate(scales, axis=0) * (both[:, :lane] + both[:, lane:])
        found[p * part * rows_out : (p + 1) * part * rows_out, :] = matched
    weight = weight_ref[pl.program_id(0)]
    inside = lax.broadcasted_iota(jnp.int32, (rows_out, lane), 1)
    tiles = row_width // lane
    fold = folded(tiles)
    for tile in range(tiles):
        piece = None
        for w in range(tile * lane // step, ((tile + 1) * lane - 1) // step + 1):
            start = step * w - tile * lane
            values = found[w * rows_out : (w + 1) * rows_out, :]
            if start % lane:
                values = pltpu.roll(values, start % lane, 1)
            piece = values if piece is None else jnp.where(inside < start, piece, values)
        here = slice(lane * tile, lane * (tile + 1))
        own, above, below = piece[:patch_rows], piece[patch_rows : patch_rows + 16], piece[-16:]
        difference_ref[0, :, here] = own - template_ref[:, here]
        total_ref[:, here] = total_ref[:, here] + weight * own
        at = 2 * (tile // fold)
        spare = slice((tiles + tile % fold) * lane, (tiles + tile % fold + 1) * lane)
        up_ref[0, :, here] = above[8:]
        up_ref[0, at : at + 2, spare] = above[6:8]
        dn_ref[0, :, here] = below[:8]
        dn_ref[0, at : at + 2, spare] = below[8:10]


def spread_rows(weights, warped, down, across, coefs, coefs_up, coefs_dn, template):
    count, patch_rows, width = warped.shape
    visits, bases, span = coefs.shape
    row_width = template.shape[1]
    part = span // lane // parts
    edge = row_width + folded(row_width // lane) * lane
    coef_spec = pl.BlockSpec((1, bases, span), lambda q: (q, 0, 0))
    edge_spec = pl.BlockSpec((1, 8, edge), lambda q: (q, 0, 0))
    return pl.pallas_call(
        spread_kernel,
        out_shape=(
            jax.ShapeDtypeStruct((visits, patch_rows, row_width), jnp.float32),
            jax.ShapeDtypeStruct(template.shape, jnp.float32),
            jax.ShapeDtypeStruct((count, 8, edge), jnp.float32),
            jax.ShapeDtypeStruct((count, 8, edge), jnp.float32),
        ),
        grid=(count,),
        in_specs=[
            pl.BlockSpec(memory_space=pltpu.SMEM),
            pl.BlockSpec((1, patch_rows, width), lambda q: (q, 0, 0)),
            pl.BlockSpec(down.shape, lambda q: (0, 0)),
            pl.BlockSpec(across.shape, lambda q: (0, 0, 0)),
            coef_spec,
            coef_spec,
            coef_spec,
            pl.BlockSpec(template.shape, lambda q: (0, 0)),
        ],
        out_specs=[
            pl.BlockSpec((1, patch_rows, row_width), lambda q: (q, 0, 0)),
            pl.BlockSpec(template.shape, lambda q: (0, 0)),
            edge_spec,
            edge_spec,
        ],
        scratch_shapes=[
            pltpu.VMEM((down.shape[1], span), bf16),
            pltpu.VMEM((parts, down.shape[0], part * lane), bf16),
            pltpu.VMEM((parts, down.shape[0], part * lane), bf16),
            pltpu.VMEM((span // lane * (patch_rows + 32), lane), jnp.float32),
        ],
        compiler_params=pltpu.CompilerParams(vmem_limit_bytes=58 << 20),
        cost_estimate=pl.CostEstimate(flops=0, bytes_accessed=24 * count << 20, transcendentals=0),
        name="spread_rows",
    )(weights, warped, down, across, coefs, coefs_up, coefs_dn, template)


def add_kernel(
    weight_ref, above_ref, below_ref, before_ref, sums_ref, difference_ref, total_ref
):
    _, patch_rows, row_width = before_ref.shape
    tiles = row_width // lane
    fold = folded(tiles)
    weight = weight_ref[pl.program_id(0)]

    @pl.when(pl.program_id(0) == 0)
    def _():
        total_ref[...] = sums_ref[...]

    difference_ref[0, 10 : patch_rows - 10, :] = before_ref[0, 10 : patch_rows - 10, :]
    for tile in range(tiles):
        here = slice(lane * tile, lane * (tile + 1))
        at = 2 * (tile // fold)
        spare = slice((tiles + tile % fold) * lane, (tiles + tile % fold + 1) * lane)
        for first, ref, rows, columns in (
            (0, above_ref, slice(0, 8), here),
            (8, above_ref, slice(at, at + 2), spare),
            (patch_rows - 10, below_ref, slice(at, at + 2), spare),
            (patch_rows - 8, below_ref, slice(0, 8), here),
        ):
            values = ref[0, rows, columns]
            to = slice(first, first + rows.stop - rows.start)
            difference_ref[0, to, here] = before_ref[0, to, here] + values
            total_ref[to, here] = total_ref[to, here] + weight * values


def add_edges(weights, above, below, difference, total):
    count, _, edge = above.shape
    _, patch_rows, row_width = difference.shape
    row_spec = pl.BlockSpec((1, patch_rows, row_width), lambda q: (q, 0, 0))
    edge_spec = pl.BlockSpec((1, 8, edge), lambda q: (q, 0, 0))
    total_spec = pl.BlockSpec(total.shape, lambda q: (0, 0))
    return pl.pallas_call(
        add_kernel,
        out_shape=(
            jax.ShapeDtypeStruct(difference.shape, jnp.float32),
            jax.ShapeDtypeStruct(total.shape, jnp.float32),
        ),
        grid=(count,),
        in_specs=[
            pl.BlockSpec(memory_space=pltpu.SMEM),
            edge_spec,
            edge_spec,
            row_spec,
            total_spec,
        ],
        out_specs=[row_spec, total_spec],
        input_output_aliases={3: 0},
        compiler_params=pltpu.CompilerParams(vmem_limit_bytes=52 << 20),
        cost_estimate=pl.CostEstimate(flops=0, bytes_accessed=3 * count << 20, transcendentals=0),
        name="add_edges",
    )(weights, above, below, difference, total)


def match_rows(
    first, weights, warped, above, below, down, across, coefs, template, before, difference
):
    count, _, width = warped.shape
    edge = above.shape[2]
    visits, bases, span = coefs.shape
    patch_rows, row_width = template.shape
    part = span // lane // parts
    fresh = before is None
    if fresh:
        before = template
    extra, aliases = [], {}
    if difference is not None:
        extra, aliases = [difference], {9: 0}
    kernel = functools.partial(match_kernel, first, fresh)
    if difference is None:

        def body(*refs):
            kernel(*refs[:9], None, *refs[9:])

    else:
        body = kernel
    rows_spec = pl.BlockSpec(template.shape, lambda q: (0, 0))
    return pl.pallas_call(
        body,
        out_shape=(
            jax.ShapeDtypeStruct((visits, patch_rows, row_width), jnp.float32),
            jax.ShapeDtypeStruct(template.shape, jnp.float32),
        ),
        grid=(count,),
        in_specs=[
            pl.BlockSpec(memory_space=pltpu.SMEM),
            pl.BlockSpec((1, patch_rows, width), lambda q: (q, 0, 0)),
            *[pl.BlockSpec((1, 8, edge), lambda q: (q, 0, 0))] * 2,
            pl.BlockSpec(down.shape, lambda q: (0, 0)),
            pl.BlockSpec(across.shape, lambda q: (0, 0, 0)),
            pl.BlockSpec((1, bases, span), lambda q: (q + first, 0, 0)),
            rows_spec,
            rows_spec,
        ]
        + [pl.BlockSpec(memory_space=pl.ANY)] * len(extra),
        out_specs=[
            pl.BlockSpec((1, patch_rows, row_width), lambda q: (q + first, 0, 0)),
            rows_spec,
        ],
        scratch_shapes=[
            pltpu.VMEM((down.shape[1], span), bf16),
            pltpu.VMEM((parts, down.shape[0], part * lane), bf16),
            pltpu.VMEM((parts, down.shape[0], part * lane), bf16),
            pltpu.VMEM((span // lane * patch_rows, lane), jnp.float32),
        ],
        input_output_aliases=aliases,
        compiler_params=pltpu.CompilerParams(vmem_limit_bytes=50 << 20),
        cost_estimate=pl.CostEstimate(flops=0, bytes_accessed=20 * count << 20, transcendentals=0),
        name="match_rows",
    )(weights, warped, above, below, down, across, coefs, template, before, *extra)


def sum_kernel(total_ref, scale_ref, out_ref, slots, send_sems, recv_sems):
    me = lax.axis_index("visit")
    slabs = lax.axis_size("visit")
    rows = out_ref.shape[0]
    mesh_ids = pl.DeviceIdType.MESH
    barrier = pltpu.get_barrier_semaphore()
    for i in range(1, slabs):
        to = lax.rem(me + i, slabs)
        pl.semaphore_signal(barrier, inc=1, device_id={"visit": to}, device_id_type=mesh_ids)
    pl.semaphore_wait(barrier, slabs - 1)
    copies = []
    for i in range(1, slabs):
        to = lax.rem(me + i, slabs)
        copy = pltpu.make_async_remote_copy(
            src_ref=total_ref.at[pl.ds(pl.multiple_of(rows * to, rows), rows), :],
            dst_ref=slots.at[i - 1],
            send_sem=send_sems.at[i - 1],
            recv_sem=recv_sems.at[i - 1],
            device_id={"visit": to},
            device_id_type=mesh_ids,
        )
        copy.start()
        copies.append(copy)
    for copy in copies:
        copy.wait()
    result = total_ref[pl.ds(pl.multiple_of(rows * me, rows), rows), :]
    for i in range(slabs - 1):
        result = result + slots[i]
    out_ref[...] = result / scale_ref[0]


def sum_visits(total, scale):
    slabs = lax.axis_size("visit")
    shape = (total.shape[0] // slabs, total.shape[1])
    return pl.pallas_call(
        sum_kernel,
        out_shape=jax.ShapeDtypeStruct(shape, jnp.float32),
        in_specs=[
            pl.BlockSpec(memory_space=pltpu.VMEM),
            pl.BlockSpec(memory_space=pltpu.SMEM),
        ],
        out_specs=pl.BlockSpec(memory_space=pltpu.VMEM),
        scratch_shapes=[
            pltpu.VMEM((slabs - 1,) + shape, jnp.float32),
            pltpu.SemaphoreType.DMA((slabs - 1,)),
            pltpu.SemaphoreType.DMA((slabs - 1,)),
        ],
        compiler_params=pltpu.CompilerParams(
            collective_id=0, has_side_effects=True, vmem_limit_bytes=16 << 20
        ),
        name="sum_visits",
    )(total, scale)


def split_table(values):
    high = lax.reduce_precision(values, 8, 7)
    return high.astype(bf16), (values - high).astype(bf16)


def taken(values, index):
    table = jnp.zeros((values.shape[0],) + index.shape, jnp.float32)
    for lag in range(values.shape[1]):
        table = jnp.where((index == lag)[None], values[:, lag].reshape(-1, 1, 1), table)
    return table


def on_device(
    ccd_rows,
    tract_row,
    warp_taps,
    warp_shift,
    basis_rows,
    basis_cols,
    coef_table,
    grid_index,
    template,
    visit_weight,
):
    visits, patch_rows, row_width = ccd_rows.shape
    patches = lax.axis_size("patch")
    here = lax.axis_index("patch")
    half = basis_rows.shape[1] // 2
    tiles = row_width // lane

    tiled_rows = ccd_rows.reshape(visits, patch_rows // 8, 8, tiles, lane).transpose(0, 1, 3, 2, 4)
    tiled_rows = tiled_rows.reshape(visits, patch_rows * tiles, lane)
    place = tract_row[0, 0]
    offset = place // patch_rows - here - (place % patch_rows) // 2
    turn = ((here - offset) % patches).astype(jnp.int32).reshape(1)
    taps = jnp.pad(warp_taps[:, 0], ((0, 0), (0, 0), (half_lane, half_lane)))
    shift = jnp.pad(warp_shift, ((0, 0), (0, 0), (half_lane, half_lane)))

    def windowed_coefs(table, grid):
        windows = -(-row_width // step)
        cells = jnp.pad(grid, (0, windows * step - row_width)).reshape(windows, step)
        cells = jnp.pad(cells, ((0, 0), (0, lane - step))).reshape(-1)
        one_hot = (cells[None, :] == jnp.arange(table.shape[2])[:, None]).astype(jnp.float32)
        return jnp.einsum("qbg,gx->qbx", table, one_hot, precision=lax.Precision.HIGHEST)

    down_pairs = [(i, i + 1) for i in range(patches - 1)]
    up_pairs = [(i + 1, i) for i in range(patches - 1)]
    table = coef_table[:, 0]
    coefs = windowed_coefs(table, grid_index[0])

    rows = jnp.arange(patch_rows)
    pair = jnp.arange(8)
    inner = jnp.concatenate(
        [rows, pair - 8, pair + patch_rows, pair % 2 - half, pair % 2 + patch_rows + half - 2]
    )
    down = taken(basis_rows, inner[None, :] - rows[:, None] + half).reshape(-1, inner.shape[0])
    down_high, down_low = split_table(down)
    down = jnp.concatenate([down_high, down_high, down_low], axis=1)
    outer = jnp.concatenate([rows, jnp.arange(16) - 16, jnp.arange(16) + patch_rows])
    wide = taken(basis_rows, rows[None, :] - outer[:, None] + half).reshape(-1, patch_rows)
    wide_high, wide_low = split_table(wide)
    wide = jnp.concatenate([wide_high, wide_high, wide_low], axis=1)
    out = jnp.arange(lane)[None, :]
    across = taken(
        basis_cols, jnp.where(out < step, jnp.arange(lane)[:, None] - out, basis_cols.shape[1])
    )
    high, low = split_table(across)
    across = jnp.concatenate(
        [
            jnp.concatenate([high, low], axis=2),
            jnp.concatenate([high, jnp.zeros_like(low)], axis=2),
        ],
        axis=1,
    )
    weights = lax.dynamic_slice_in_dim(
        visit_weight, lax.axis_index("visit") * visits, visits
    )

    early, late = chunks
    sent = [
        pack_rows(first, count, tract_row, tiled_rows, patches)
        for first, count in ((0, early), (early, late))
    ]
    packed = jnp.concatenate([table.reshape(-1), grid_index[0].astype(jnp.float32)])
    nearby = [lax.ppermute(packed, "patch", pairs) for pairs in (down_pairs, up_pairs)]
    sent[1], down, wide, across, coefs, taps, shift, weights, turn, nearby = (
        lax.optimization_barrier(
            (sent[1], down, wide, across, coefs, taps, shift, weights, turn, nearby)
        )
    )
    got = [lax.all_to_all(block, "patch", split_axis=0, concat_axis=0, tiled=True) for block in sent]

    def neighbour_coefs(values):
        cells = values[table.size :].astype(jnp.int32)
        return windowed_coefs(values[: table.size].reshape(table.shape), cells)

    warped, _, _ = warp_rows(0, early, turn, got[0], taps, shift, patch_rows)
    difference, total, up, dn = spread_rows(
        weights,
        warped,
        wide,
        across,
        coefs,
        *map(neighbour_coefs, nearby),
        template,
    )
    from_above = lax.ppermute(dn, "patch", down_pairs)
    from_below = lax.ppermute(up, "patch", up_pairs)
    turn, total = lax.optimization_barrier((turn, total))
    warped, head, tail = warp_rows(early, late, turn, got[1], taps, shift, patch_rows)
    above = lax.ppermute(tail, "patch", down_pairs)
    below = lax.ppermute(head, "patch", up_pairs)
    from_above, from_below, warped = lax.optimization_barrier((from_above, from_below, warped))
    difference, total = add_edges(weights, from_above, from_below, difference, total)
    difference, total = match_rows(
        early, weights, warped, above, below, down, across, coefs, template, total, difference
    )
    coadd = sum_visits(total, jnp.sum(visit_weight).reshape(1))
    return difference, coadd


def solution(mesh):
    placed = (
        P("visit", "patch", None),
        P("visit", "patch"),
        P("visit", "patch", None, None),
        P("visit", "patch", None),
        P(),
        P(),
        P("visit", "patch", None, None),
        P("patch", None),
        P("patch", None),
        P(),
    )
    return jax.shard_map(
        on_device,
        mesh=mesh,
        in_specs=placed,
        out_specs=(P("visit", "patch", None), P(("patch", "visit"), None)),
        check_vma=False,
    )
```

```python
import functools

import jax
import jax.numpy as jnp
from jax import lax
from jax.experimental import pallas as pl
from jax.experimental.pallas import tpu as pltpu
from jax.sharding import PartitionSpec as P

lane = 128
half_lane = 64
step = 108
parts = 2
whole = 58 << 20
chunks = (4, 4)
bf16 = jnp.bfloat16


def pack_kernel(first, places_ref, rows_ref, sent_ref):
    tiles = sent_ref.shape[2] // 2
    patch_rows = places_ref.shape[1]
    visit = first + pl.program_id(0)

    def step(row, carry):
        place = places_ref[visit, row]
        start = (row // 8) * (8 * tiles) + row % 8
        cells = rows_ref[0, pl.ds(start, tiles, stride=8), :]
        at = pl.multiple_of((place % 2) * tiles, tiles)
        sent_ref[place // patch_rows, 0, pl.ds(at, tiles), :] = cells
        return carry

    lax.fori_loop(0, patch_rows, step, 0, unroll=True)


def pack_rows(first, count, tract_row, tiled_rows, patches):
    visits, cells, _ = tiled_rows.shape
    tiles = cells // tract_row.shape[1]
    shape = (patches, count, 2 * tiles, lane)
    return pl.pallas_call(
        functools.partial(pack_kernel, first),
        out_shape=jax.ShapeDtypeStruct(shape, jnp.float32),
        grid=(count,),
        in_specs=[
            pl.BlockSpec(memory_space=pltpu.SMEM),
            pl.BlockSpec((1, cells, lane), lambda q: (q + first, 0, 0)),
        ],
        out_specs=pl.BlockSpec((patches, 1, 2 * tiles, lane), lambda q: (0, q, 0, 0)),
        compiler_params=pltpu.CompilerParams(vmem_limit_bytes=whole),
        cost_estimate=pl.CostEstimate(flops=0, bytes_accessed=3 * count << 20, transcendentals=0),
        name="pack_rows",
    )(tract_row, tiled_rows)


def folded(tiles):
    return -(-tiles // 4)


def split(values):
    high = values.astype(bf16)
    low = (values - high.astype(jnp.float32)).astype(bf16)
    return high, low


def warp_kernel(
    first, turn_ref, got_ref, taps_ref, shift_ref, warped_ref, head_ref, tail_ref, rows, image, sems
):
    patches, _, depth = got_ref.shape[:3]
    tiles = depth // 2
    patch_rows = warped_ref.shape[1]
    groups = patch_rows // 8
    visit = pl.program_id(0)

    @pl.when(visit == 0)
    def _():
        def fetch(local, carry):
            for pair in range(patch_rows // 2):
                source = (turn_ref[0] + first + local - pair + 2 * patches) % patches
                pltpu.make_async_copy(
                    got_ref.at[source, local],
                    rows.at[local, pl.ds(pair * depth, depth), :],
                    sems.at[local],
                ).start()
            return carry

        lax.fori_loop(0, pl.num_programs(0), fetch, 0)
        blank = jnp.zeros((2 * patch_rows, lane), bf16)
        image[:, :lane] = blank
        image[:, (tiles + 1) * lane :] = blank

    pltpu.make_async_copy(rows.at[visit], rows.at[visit], sems.at[visit]).wait()

    def split_step(tile, carry):
        values = jnp.concatenate(
            [
                rows[visit, pl.ds(8 * g * tiles + tile, 8, stride=tiles), :]
                for g in range(groups)
            ],
            axis=0,
        )
        window = pl.ds(pl.multiple_of((tile + 1) * lane, lane), lane)
        image[:, window] = jnp.concatenate(split(values), axis=0)
        return carry

    lax.fori_loop(0, tiles, split_step, 0, unroll=4)
    columns = lax.broadcasted_iota(jnp.int32, (8, lane), 1) + half_lane
    sublanes = lax.broadcasted_iota(jnp.int32, (8, lane), 0)

    fold = folded(tiles + 1)
    for ref in (head_ref, tail_ref):
        ref[0, :, (tiles + 1) * lane :] = jnp.zeros((8, fold * lane), jnp.float32)
    for u in range(tiles + 1):
        window = slice(u * lane, (u + 1) * lane)
        spot = columns + jnp.broadcast_to(shift_ref[0, :, window], (8, lane))
        taps = taps_ref[0, :, window]
        turned = jnp.take_along_axis(
            taps, (sublanes - spot) & 7, axis=0, mode="promise_in_bounds"
        )
        block = (spot >> 3) + jnp.where(sublanes < (spot & 7), 1, 0)
        high = turned.astype(bf16).astype(jnp.float32)
        low = turned - high
        here = [block == i for i in range(2 * lane // 8)]
        matrix = jnp.concatenate(
            [
                jnp.concatenate([jnp.where(m, high, 0.0) for m in here], axis=0).astype(bf16),
                jnp.concatenate([jnp.where(m, low, 0.0) for m in here], axis=0).astype(bf16),
            ],
            axis=1,
        )
        both = slice(u * lane, (u + 2) * lane)
        out = jnp.dot(image[:, both], matrix, preferred_element_type=jnp.float32)
        cells = out[:patch_rows, :lane] + out[:patch_rows, lane:] + out[patch_rows:, :lane]
        warped_ref[0, :, window] = cells
        at = 2 * (u // fold)
        spare = slice((tiles + 1 + u % fold) * lane, (tiles + 2 + u % fold) * lane)
        head_ref[0, :, window] = cells[:8]
        head_ref[0, at : at + 2, spare] = cells[8:10]
        tail_ref[0, :, window] = cells[patch_rows - 8 :]
        tail_ref[0, at : at + 2, spare] = cells[patch_rows - 10 : patch_rows - 8]


def warp_rows(first, count, turn, got, taps, shift, patch_rows):
    depth = got.shape[2]
    width = (depth // 2 + 1) * lane
    span = width + folded(width // lane) * lane
    edge = jax.ShapeDtypeStruct((count, 8, span), jnp.float32)
    return pl.pallas_call(
        functools.partial(warp_kernel, first),
        out_shape=(jax.ShapeDtypeStruct((count, patch_rows, width), jnp.float32), edge, edge),
        grid=(count,),
        in_specs=[
            pl.BlockSpec(memory_space=pltpu.SMEM),
            pl.BlockSpec(memory_space=pl.ANY),
            pl.BlockSpec((1,) + taps.shape[1:], lambda q: (q + first, 0, 0)),
            pl.BlockSpec((1,) + shift.shape[1:], lambda q: (q + first, 0, 0)),
        ],
        out_specs=[
            pl.BlockSpec((1, patch_rows, width), lambda q: (q, 0, 0)),
            *[pl.BlockSpec((1, 8, span), lambda q: (q, 0, 0))] * 2,
        ],
        scratch_shapes=[
            pltpu.VMEM((count, patch_rows // 2 * depth, lane), jnp.float32),
            pltpu.VMEM((2 * patch_rows, width + lane), bf16),
            pltpu.SemaphoreType.DMA((count,)),
        ],
        compiler_params=pltpu.CompilerParams(vmem_limit_bytes=52 << 20),
        cost_estimate=pl.CostEstimate(flops=0, bytes_accessed=12 * count << 20, transcendentals=0),
        name="warp_rows",
    )(turn, got, taps, shift)


def match_kernel(
    first,
    fresh,
    weight_ref,
    warped_ref,
    above_ref,
    below_ref,
    down_ref,
    across_ref,
    coef_ref,
    template_ref,
    before_ref,
    _,
    difference_ref,
    total_ref,
    pieces,
    high_refs,
    low_refs,
    found,
):
    patch_rows, row_width = template_ref.shape
    bases = across_ref.shape[0]
    windows = pieces.shape[1] // lane
    part = high_refs.shape[2] // lane
    tiles = warped_ref.shape[2] // lane
    fold = folded(tiles)
    inside = lax.broadcasted_iota(jnp.int32, (16, lane), 1)
    quarter = lax.broadcasted_iota(jnp.int32, (16, lane), 0) % 8 // 2

    def columns(tile):
        own = warped_ref[0, :, tile * lane : (tile + 1) * lane]
        edges = []
        for at in (tile, tiles + tile % fold):
            here = slice(at * lane, (at + 1) * lane)
            edges.append(jnp.concatenate([above_ref[0, :, here], below_ref[0, :, here]], axis=0))
        edges[1] = jnp.where(quarter == tile // fold, edges[1], 0.0)
        return [own[:16], own[16:], *edges]


    @pl.when(pl.program_id(0) == 0)
    def _():
        total_ref[...] = jnp.zeros_like(total_ref) if fresh else before_ref[...]

    def cut_window(w):
        start = step * w + half_lane - (lane - step) // 2
        tile, turn = start // lane, start % lane
        here = slice(w * lane, (w + 1) * lane)
        blocks = columns(tile)
        if turn:
            blocks = [
                jnp.where(
                    inside < lane - turn,
                    pltpu.roll(before, lane - turn, 1),
                    pltpu.roll(after, lane - turn, 1),
                )
                for before, after in zip(blocks, columns(tile + 1))
            ]
        for i, values in enumerate(blocks):
            high, low = split(values)
            for j, value in enumerate((high, low, high)):
                at = (j * len(blocks) + i) * 16
                pieces[at : at + 16, here] = value

    def part_step(p):
        for w in range(p * part, (p + 1) * part):
            cut_window(w)
        wide = slice(p * part * lane, (p + 1) * part * lane)
        high_ref = high_refs.at[p]
        low_ref = low_refs.at[p]
        vertical = jnp.dot(down_ref[...], pieces[:, wide], preferred_element_type=jnp.float32)
        high_ref[...], low_ref[...] = split(vertical)

        def gathered(ref, b):
            rows = slice(b * patch_rows, (b + 1) * patch_rows)
            return jnp.concatenate(
                [ref[rows, lane * i : lane * (i + 1)] for i in range(part)], axis=0
            )

        matched = jnp.zeros((part * patch_rows, lane), jnp.float32)
        for b in range(bases):
            operand = jnp.concatenate([gathered(high_ref, b), gathered(low_ref, b)], axis=1)
            both = jnp.dot(operand, across_ref[b], preferred_element_type=jnp.float32)
            scales = coef_ref[0, b : b + 1, wide]
            scale = jnp.concatenate(
                [
                    jnp.broadcast_to(scales[:, lane * i : lane * (i + 1)], (patch_rows, lane))
                    for i in range(part)
                ],
                axis=0,
            )
            matched = matched + scale * (both[:, :lane] + both[:, lane:])
        found[p * part * patch_rows : (p + 1) * part * patch_rows, :] = matched

    for p in range(windows // part):
        part_step(p)
    weight = weight_ref[first + pl.program_id(0)]
    inside = lax.broadcasted_iota(jnp.int32, (patch_rows, lane), 1)
    for tile in range(row_width // lane):
        piece = None
        for w in range(tile * lane // step, ((tile + 1) * lane - 1) // step + 1):
            start = step * w - tile * lane
            values = found[w * patch_rows : (w + 1) * patch_rows, :]
            if start % lane:
                values = pltpu.roll(values, start % lane, 1)
            piece = values if piece is None else jnp.where(inside < start, piece, values)
        here = slice(lane * tile, lane * (tile + 1))
        difference_ref[0, :, here] = piece - template_ref[:, here]
        total_ref[:, here] = total_ref[:, here] + weight * piece


def spread_kernel(
    weight_ref,
    warped_ref,
    down_ref,
    across_ref,
    coef_ref,
    coef_up_ref,
    coef_dn_ref,
    template_ref,
    difference_ref,
    total_ref,
    up_ref,
    dn_ref,
    pieces,
    high_refs,
    low_refs,
    found,
):
    patch_rows, row_width = template_ref.shape
    rows_out = patch_rows + 32
    bases = across_ref.shape[0]
    windows = pieces.shape[1] // lane
    part = high_refs.shape[2] // lane
    inside = lax.broadcasted_iota(jnp.int32, (patch_rows, lane), 1)

    @pl.when(pl.program_id(0) == 0)
    def _():
        total_ref[...] = jnp.zeros_like(total_ref)

    for p in range(windows // part):
        for w in range(p * part, (p + 1) * part):
            start = step * w + half_lane - (lane - step) // 2
            tile, turn = start // lane, start % lane
            values = warped_ref[0, :, tile * lane : (tile + 1) * lane]
            if turn:
                after = warped_ref[0, :, (tile + 1) * lane : (tile + 2) * lane]
                values = jnp.where(
                    inside < lane - turn,
                    pltpu.roll(values, lane - turn, 1),
                    pltpu.roll(after, lane - turn, 1),
                )
            high, low = split(values)
            here = slice(w * lane, (w + 1) * lane)
            for j, value in enumerate((high, low, high)):
                pieces[j * patch_rows : (j + 1) * patch_rows, here] = value
        wide = slice(p * part * lane, (p + 1) * part * lane)
        vertical = jnp.dot(down_ref[...], pieces[:, wide], preferred_element_type=jnp.float32)
        high_refs[p], low_refs[p] = split(vertical)

        def gathered(refs, b):
            rows = slice(b * rows_out, (b + 1) * rows_out)
            return jnp.concatenate(
                [refs[p, rows, lane * i : lane * (i + 1)] for i in range(part)], axis=0
            )

        matched = jnp.zeros((part * rows_out, lane), jnp.float32)
        for b in range(bases):
            operand = jnp.concatenate([gathered(high_refs, b), gathered(low_refs, b)], axis=1)
            both = jnp.dot(operand, across_ref[b], preferred_element_type=jnp.float32)
            scales = []
            for w in range(p * part, (p + 1) * part):
                here = slice(w * lane, (w + 1) * lane)
                for ref, count in ((coef_ref, patch_rows), (coef_up_ref, 16), (coef_dn_ref, 16)):
                    scales.append(jnp.broadcast_to(ref[0, b : b + 1, here], (count, lane)))
            matched = matched + jnp.concatenate(scales, axis=0) * (both[:, :lane] + both[:, lane:])
        found[p * part * rows_out : (p + 1) * part * rows_out, :] = matched
    weight = weight_ref[pl.program_id(0)]
    inside = lax.broadcasted_iota(jnp.int32, (rows_out, lane), 1)
    tiles = row_width // lane
    fold = folded(tiles)
    for tile in range(tiles):
        piece = None
        for w in range(tile * lane // step, ((tile + 1) * lane - 1) // step + 1):
            start = step * w - tile * lane
            values = found[w * rows_out : (w + 1) * rows_out, :]
            if start % lane:
                values = pltpu.roll(values, start % lane, 1)
            piece = values if piece is None else jnp.where(inside < start, piece, values)
        here = slice(lane * tile, lane * (tile + 1))
        own, above, below = piece[:patch_rows], piece[patch_rows : patch_rows + 16], piece[-16:]
        difference_ref[0, :, here] = own - template_ref[:, here]
        total_ref[:, here] = total_ref[:, here] + weight * own
        at = 2 * (tile // fold)
        spare = slice((tiles + tile % fold) * lane, (tiles + tile % fold + 1) * lane)
        up_ref[0, :, here] = above[8:]
        up_ref[0, at : at + 2, spare] = above[6:8]
        dn_ref[0, :, here] = below[:8]
        dn_ref[0, at : at + 2, spare] = below[8:10]


def spread_rows(weights, warped, down, across, coefs, coefs_up, coefs_dn, template):
    count, patch_rows, width = warped.shape
    visits, bases, span = coefs.shape
    row_width = template.shape[1]
    part = span // lane // parts
    edge = row_width + folded(row_width // lane) * lane
    coef_spec = pl.BlockSpec((1, bases, span), lambda q: (q, 0, 0))
    edge_spec = pl.BlockSpec((1, 8, edge), lambda q: (q, 0, 0))
    return pl.pallas_call(
        spread_kernel,
        out_shape=(
            jax.ShapeDtypeStruct((visits, patch_rows, row_width), jnp.float32),
            jax.ShapeDtypeStruct(template.shape, jnp.float32),
            jax.ShapeDtypeStruct((count, 8, edge), jnp.float32),
            jax.ShapeDtypeStruct((count, 8, edge), jnp.float32),
        ),
        grid=(count,),
        in_specs=[
            pl.BlockSpec(memory_space=pltpu.SMEM),
            pl.BlockSpec((1, patch_rows, width), lambda q: (q, 0, 0)),
            pl.BlockSpec(down.shape, lambda q: (0, 0)),
            pl.BlockSpec(across.shape, lambda q: (0, 0, 0)),
            coef_spec,
            coef_spec,
            coef_spec,
            pl.BlockSpec(template.shape, lambda q: (0, 0)),
        ],
        out_specs=[
            pl.BlockSpec((1, patch_rows, row_width), lambda q: (q, 0, 0)),
            pl.BlockSpec(template.shape, lambda q: (0, 0)),
            edge_spec,
            edge_spec,
        ],
        scratch_shapes=[
            pltpu.VMEM((down.shape[1], span), bf16),
            pltpu.VMEM((parts, down.shape[0], part * lane), bf16),
            pltpu.VMEM((parts, down.shape[0], part * lane), bf16),
            pltpu.VMEM((span // lane * (patch_rows + 32), lane), jnp.float32),
        ],
        compiler_params=pltpu.CompilerParams(vmem_limit_bytes=58 << 20),
        cost_estimate=pl.CostEstimate(flops=0, bytes_accessed=24 * count << 20, transcendentals=0),
        name="spread_rows",
    )(weights, warped, down, across, coefs, coefs_up, coefs_dn, template)


def add_kernel(
    weight_ref, above_ref, below_ref, before_ref, sums_ref, difference_ref, total_ref
):
    _, patch_rows, row_width = before_ref.shape
    tiles = row_width // lane
    fold = folded(tiles)
    weight = weight_ref[pl.program_id(0)]

    @pl.when(pl.program_id(0) == 0)
    def _():
        total_ref[...] = sums_ref[...]

    difference_ref[0, 10 : patch_rows - 10, :] = before_ref[0, 10 : patch_rows - 10, :]
    for tile in range(tiles):
        here = slice(lane * tile, lane * (tile + 1))
        at = 2 * (tile // fold)
        spare = slice((tiles + tile % fold) * lane, (tiles + tile % fold + 1) * lane)
        for first, ref, rows, columns in (
            (0, above_ref, slice(0, 8), here),
            (8, above_ref, slice(at, at + 2), spare),
            (patch_rows - 10, below_ref, slice(at, at + 2), spare),
            (patch_rows - 8, below_ref, slice(0, 8), here),
        ):
            values = ref[0, rows, columns]
            to = slice(first, first + rows.stop - rows.start)
            difference_ref[0, to, here] = before_ref[0, to, here] + values
            total_ref[to, here] = total_ref[to, here] + weight * values


def add_edges(weights, above, below, difference, total):
    count, _, edge = above.shape
    _, patch_rows, row_width = difference.shape
    row_spec = pl.BlockSpec((1, patch_rows, row_width), lambda q: (q, 0, 0))
    edge_spec = pl.BlockSpec((1, 8, edge), lambda q: (q, 0, 0))
    total_spec = pl.BlockSpec(total.shape, lambda q: (0, 0))
    return pl.pallas_call(
        add_kernel,
        out_shape=(
            jax.ShapeDtypeStruct(difference.shape, jnp.float32),
            jax.ShapeDtypeStruct(total.shape, jnp.float32),
        ),
        grid=(count,),
        in_specs=[
            pl.BlockSpec(memory_space=pltpu.SMEM),
            edge_spec,
            edge_spec,
            row_spec,
            total_spec,
        ],
        out_specs=[row_spec, total_spec],
        input_output_aliases={3: 0},
        compiler_params=pltpu.CompilerParams(vmem_limit_bytes=52 << 20),
        cost_estimate=pl.CostEstimate(flops=0, bytes_accessed=3 * count << 20, transcendentals=0),
        name="add_edges",
    )(weights, above, below, difference, total)


def match_rows(
    first, weights, warped, above, below, down, across, coefs, template, before, difference
):
    count, _, width = warped.shape
    edge = above.shape[2]
    visits, bases, span = coefs.shape
    patch_rows, row_width = template.shape
    part = span // lane // parts
    fresh = before is None
    if fresh:
        before = template
    extra, aliases = [], {}
    if difference is not None:
        extra, aliases = [difference], {9: 0}
    kernel = functools.partial(match_kernel, first, fresh)
    if difference is None:

        def body(*refs):
            kernel(*refs[:9], None, *refs[9:])

    else:
        body = kernel
    rows_spec = pl.BlockSpec(template.shape, lambda q: (0, 0))
    return pl.pallas_call(
        body,
        out_shape=(
            jax.ShapeDtypeStruct((visits, patch_rows, row_width), jnp.float32),
            jax.ShapeDtypeStruct(template.shape, jnp.float32),
        ),
        grid=(count,),
        in_specs=[
            pl.BlockSpec(memory_space=pltpu.SMEM),
            pl.BlockSpec((1, patch_rows, width), lambda q: (q, 0, 0)),
            *[pl.BlockSpec((1, 8, edge), lambda q: (q, 0, 0))] * 2,
            pl.BlockSpec(down.shape, lambda q: (0, 0)),
            pl.BlockSpec(across.shape, lambda q: (0, 0, 0)),
            pl.BlockSpec((1, bases, span), lambda q: (q + first, 0, 0)),
            rows_spec,
            rows_spec,
        ]
        + [pl.BlockSpec(memory_space=pl.ANY)] * len(extra),
        out_specs=[
            pl.BlockSpec((1, patch_rows, row_width), lambda q: (q + first, 0, 0)),
            rows_spec,
        ],
        scratch_shapes=[
            pltpu.VMEM((down.shape[1], span), bf16),
            pltpu.VMEM((parts, down.shape[0], part * lane), bf16),
            pltpu.VMEM((parts, down.shape[0], part * lane), bf16),
            pltpu.VMEM((span // lane * patch_rows, lane), jnp.float32),
        ],
        input_output_aliases=aliases,
        compiler_params=pltpu.CompilerParams(vmem_limit_bytes=50 << 20),
        cost_estimate=pl.CostEstimate(flops=0, bytes_accessed=20 * count << 20, transcendentals=0),
        name="match_rows",
    )(weights, warped, above, below, down, across, coefs, template, before, *extra)


def sum_kernel(total_ref, scale_ref, out_ref, slots, send_sems, recv_sems):
    me = lax.axis_index("visit")
    slabs = lax.axis_size("visit")
    rows = out_ref.shape[0]
    mesh_ids = pl.DeviceIdType.MESH
    barrier = pltpu.get_barrier_semaphore()
    for i in range(1, slabs):
        to = lax.rem(me + i, slabs)
        pl.semaphore_signal(barrier, inc=1, device_id={"visit": to}, device_id_type=mesh_ids)
    pl.semaphore_wait(barrier, slabs - 1)
    copies = []
    for i in range(1, slabs):
        to = lax.rem(me + i, slabs)
        copy = pltpu.make_async_remote_copy(
            src_ref=total_ref.at[pl.ds(pl.multiple_of(rows * to, rows), rows), :],
            dst_ref=slots.at[i - 1],
            send_sem=send_sems.at[i - 1],
            recv_sem=recv_sems.at[i - 1],
            device_id={"visit": to},
            device_id_type=mesh_ids,
        )
        copy.start()
        copies.append(copy)
    for copy in copies:
        copy.wait()
    result = total_ref[pl.ds(pl.multiple_of(rows * me, rows), rows), :]
    for i in range(slabs - 1):
        result = result + slots[i]
    out_ref[...] = result / scale_ref[0]


def sum_visits(total, scale):
    slabs = lax.axis_size("visit")
    shape = (total.shape[0] // slabs, total.shape[1])
    return pl.pallas_call(
        sum_kernel,
        out_shape=jax.ShapeDtypeStruct(shape, jnp.float32),
        in_specs=[
            pl.BlockSpec(memory_space=pltpu.VMEM),
            pl.BlockSpec(memory_space=pltpu.SMEM),
        ],
        out_specs=pl.BlockSpec(memory_space=pltpu.VMEM),
        scratch_shapes=[
            pltpu.VMEM((slabs - 1,) + shape, jnp.float32),
            pltpu.SemaphoreType.DMA((slabs - 1,)),
            pltpu.SemaphoreType.DMA((slabs - 1,)),
        ],
        compiler_params=pltpu.CompilerParams(
            collective_id=0, has_side_effects=True, vmem_limit_bytes=16 << 20
        ),
        name="sum_visits",
    )(total, scale)


def split_table(values):
    high = lax.reduce_precision(values, 8, 7)
    return high.astype(bf16), (values - high).astype(bf16)


def taken(values, index):
    table = jnp.zeros((values.shape[0],) + index.shape, jnp.float32)
    for lag in range(values.shape[1]):
        table = jnp.where((index == lag)[None], values[:, lag].reshape(-1, 1, 1), table)
    return table


def on_device(
    ccd_rows,
    tract_row,
    warp_taps,
    warp_shift,
    basis_rows,
    basis_cols,
    coef_table,
    grid_index,
    template,
    visit_weight,
):
    visits, patch_rows, row_width = ccd_rows.shape
    patches = lax.axis_size("patch")
    here = lax.axis_index("patch")
    half = basis_rows.shape[1] // 2
    tiles = row_width // lane

    tiled_rows = ccd_rows.reshape(visits, patch_rows // 8, 8, tiles, lane).transpose(0, 1, 3, 2, 4)
    tiled_rows = tiled_rows.reshape(visits, patch_rows * tiles, lane)
    place = tract_row[0, 0]
    offset = place // patch_rows - here - (place % patch_rows) // 2
    turn = ((here - offset) % patches).astype(jnp.int32).reshape(1)
    taps = jnp.pad(warp_taps[:, 0], ((0, 0), (0, 0), (half_lane, half_lane)))
    shift = jnp.pad(warp_shift, ((0, 0), (0, 0), (half_lane, half_lane)))

    def windowed_coefs(table, grid):
        windows = -(-row_width // step)
        cells = jnp.pad(grid, (0, windows * step - row_width)).reshape(windows, step)
        cells = jnp.pad(cells, ((0, 0), (0, lane - step))).reshape(-1)
        one_hot = (cells[None, :] == jnp.arange(table.shape[2])[:, None]).astype(jnp.float32)
        return jnp.einsum("qbg,gx->qbx", table, one_hot, precision=lax.Precision.HIGHEST)

    down_pairs = [(i, i + 1) for i in range(patches - 1)]
    up_pairs = [(i + 1, i) for i in range(patches - 1)]
    table = coef_table[:, 0]
    coefs = windowed_coefs(table, grid_index[0])

    rows = jnp.arange(patch_rows)
    pair = jnp.arange(8)
    inner = jnp.concatenate(
        [rows, pair - 8, pair + patch_rows, pair % 2 - half, pair % 2 + patch_rows + half - 2]
    )
    down = taken(basis_rows, inner[None, :] - rows[:, None] + half).reshape(-1, inner.shape[0])
    down_high, down_low = split_table(down)
    down = jnp.concatenate([down_high, down_high, down_low], axis=1)
    outer = jnp.concatenate([rows, jnp.arange(16) - 16, jnp.arange(16) + patch_rows])
    wide = taken(basis_rows, rows[None, :] - outer[:, None] + half).reshape(-1, patch_rows)
    wide_high, wide_low = split_table(wide)
    wide = jnp.concatenate([wide_high, wide_high, wide_low], axis=1)
    out = jnp.arange(lane)[None, :]
    across = taken(
        basis_cols, jnp.where(out < step, jnp.arange(lane)[:, None] - out, basis_cols.shape[1])
    )
    high, low = split_table(across)
    across = jnp.concatenate(
        [
            jnp.concatenate([high, low], axis=2),
            jnp.concatenate([high, jnp.zeros_like(low)], axis=2),
        ],
        axis=1,
    )
    weights = lax.dynamic_slice_in_dim(
        visit_weight, lax.axis_index("visit") * visits, visits
    )

    early, late = chunks
    sent = [
        pack_rows(first, count, tract_row, tiled_rows, patches)
        for first, count in ((0, early), (early, late))
    ]
    packed = jnp.concatenate([table.reshape(-1), grid_index[0].astype(jnp.float32)])
    nearby = [lax.ppermute(packed, "patch", pairs) for pairs in (down_pairs, up_pairs)]
    sent[1], down, wide, across, coefs, taps, shift, weights, turn, nearby = (
        lax.optimization_barrier(
            (sent[1], down, wide, across, coefs, taps, shift, weights, turn, nearby)
        )
    )
    got = [lax.all_to_all(block, "patch", split_axis=0, concat_axis=0, tiled=True) for block in sent]

    def neighbour_coefs(values):
        cells = values[table.size :].astype(jnp.int32)
        return windowed_coefs(values[: table.size].reshape(table.shape), cells)

    warped, _, _ = warp_rows(0, early, turn, got[0], taps, shift, patch_rows)
    difference, total, up, dn = spread_rows(
        weights,
        warped,
        wide,
        across,
        coefs,
        *map(neighbour_coefs, nearby),
        template,
    )
    from_above = lax.ppermute(dn, "patch", down_pairs)
    from_below = lax.ppermute(up, "patch", up_pairs)
    turn, total = lax.optimization_barrier((turn, total))
    warped, head, tail = warp_rows(early, late, turn, got[1], taps, shift, patch_rows)
    head, tail, from_above, from_below = lax.optimization_barrier(
        (head, tail, from_above, from_below)
    )
    above = lax.ppermute(tail, "patch", down_pairs)
    below = lax.ppermute(head, "patch", up_pairs)
    difference, total = add_edges(weights, from_above, from_below, difference, total)
    difference, total = match_rows(
        early, weights, warped, above, below, down, across, coefs, template, total, difference
    )
    coadd = sum_visits(total, jnp.sum(visit_weight).reshape(1))
    return difference, coadd


def solution(mesh):
    placed = (
        P("visit", "patch", None),
        P("visit", "patch"),
        P("visit", "patch", None, None),
        P("visit", "patch", None),
        P(),
        P(),
        P("visit", "patch", None, None),
        P("patch", None),
        P("patch", None),
        P(),
    )
    return jax.shard_map(
        on_device,
        mesh=mesh,
        in_specs=placed,
        out_specs=(P("visit", "patch", None), P(("patch", "visit"), None)),
        check_vma=False,
    )
```

```python
import functools

import jax
import jax.numpy as jnp
from jax import lax
from jax.experimental import pallas as pl
from jax.experimental.pallas import tpu as pltpu
from jax.sharding import PartitionSpec as P

lane = 128
half_lane = 64
step = 108
parts = 2
whole = 58 << 20
chunks = (4, 4)
bf16 = jnp.bfloat16


def pack_kernel(first, places_ref, rows_ref, sent_ref):
    tiles = sent_ref.shape[2] // 2
    patch_rows = places_ref.shape[1]
    visit = first + pl.program_id(0)

    def step(row, carry):
        place = places_ref[visit, row]
        start = (row // 8) * (8 * tiles) + row % 8
        cells = rows_ref[0, pl.ds(start, tiles, stride=8), :]
        at = pl.multiple_of((place % 2) * tiles, tiles)
        sent_ref[place // patch_rows, 0, pl.ds(at, tiles), :] = cells
        return carry

    lax.fori_loop(0, patch_rows, step, 0, unroll=True)


def pack_rows(first, count, tract_row, tiled_rows, patches):
    visits, cells, _ = tiled_rows.shape
    tiles = cells // tract_row.shape[1]
    shape = (patches, count, 2 * tiles, lane)
    return pl.pallas_call(
        functools.partial(pack_kernel, first),
        out_shape=jax.ShapeDtypeStruct(shape, jnp.float32),
        grid=(count,),
        in_specs=[
            pl.BlockSpec(memory_space=pltpu.SMEM),
            pl.BlockSpec((1, cells, lane), lambda q: (q + first, 0, 0)),
        ],
        out_specs=pl.BlockSpec((patches, 1, 2 * tiles, lane), lambda q: (0, q, 0, 0)),
        compiler_params=pltpu.CompilerParams(vmem_limit_bytes=whole),
        cost_estimate=pl.CostEstimate(flops=0, bytes_accessed=3 * count << 20, transcendentals=0),
        name="pack_rows",
    )(tract_row, tiled_rows)


def folded(tiles):
    return -(-tiles // 4)


def split(values):
    high = values.astype(bf16)
    low = (values - high.astype(jnp.float32)).astype(bf16)
    return high, low


def warp_kernel(
    first, turn_ref, got_ref, taps_ref, shift_ref, warped_ref, head_ref, tail_ref, rows, image, sems
):
    patches, _, depth = got_ref.shape[:3]
    tiles = depth // 2
    patch_rows = warped_ref.shape[1]
    groups = patch_rows // 8
    visit = pl.program_id(0)

    @pl.when(visit == 0)
    def _():
        def fetch(local, carry):
            for pair in range(patch_rows // 2):
                source = (turn_ref[0] + first + local - pair + 2 * patches) % patches
                pltpu.make_async_copy(
                    got_ref.at[source, local],
                    rows.at[local, pl.ds(pair * depth, depth), :],
                    sems.at[local],
                ).start()
            return carry

        lax.fori_loop(0, pl.num_programs(0), fetch, 0)
        blank = jnp.zeros((2 * patch_rows, lane), bf16)
        image[:, :lane] = blank
        image[:, (tiles + 1) * lane :] = blank

    pltpu.make_async_copy(rows.at[visit], rows.at[visit], sems.at[visit]).wait()

    def split_step(tile, carry):
        values = jnp.concatenate(
            [
                rows[visit, pl.ds(8 * g * tiles + tile, 8, stride=tiles), :]
                for g in range(groups)
            ],
            axis=0,
        )
        window = pl.ds(pl.multiple_of((tile + 1) * lane, lane), lane)
        image[:, window] = jnp.concatenate(split(values), axis=0)
        return carry

    lax.fori_loop(0, tiles, split_step, 0, unroll=4)
    columns = lax.broadcasted_iota(jnp.int32, (8, lane), 1) + half_lane
    sublanes = lax.broadcasted_iota(jnp.int32, (8, lane), 0)

    fold = folded(tiles + 1)
    for ref in (head_ref, tail_ref):
        ref[0, :, (tiles + 1) * lane :] = jnp.zeros((8, fold * lane), jnp.float32)
    for u in range(tiles + 1):
        window = slice(u * lane, (u + 1) * lane)
        spot = columns + jnp.broadcast_to(shift_ref[0, :, window], (8, lane))
        taps = taps_ref[0, :, window]
        turned = jnp.take_along_axis(
            taps, (sublanes - spot) & 7, axis=0, mode="promise_in_bounds"
        )
        block = (spot >> 3) + jnp.where(sublanes < (spot & 7), 1, 0)
        high = turned.astype(bf16).astype(jnp.float32)
        low = turned - high
        here = [block == i for i in range(2 * lane // 8)]
        matrix = jnp.concatenate(
            [
                jnp.concatenate([jnp.where(m, high, 0.0) for m in here], axis=0).astype(bf16),
                jnp.concatenate([jnp.where(m, low, 0.0) for m in here], axis=0).astype(bf16),
            ],
            axis=1,
        )
        both = slice(u * lane, (u + 2) * lane)
        out = jnp.dot(image[:, both], matrix, preferred_element_type=jnp.float32)
        cells = out[:patch_rows, :lane] + out[:patch_rows, lane:] + out[patch_rows:, :lane]
        warped_ref[0, :, window] = cells
        at = 2 * (u // fold)
        spare = slice((tiles + 1 + u % fold) * lane, (tiles + 2 + u % fold) * lane)
        head_ref[0, :, window] = cells[:8]
        head_ref[0, at : at + 2, spare] = cells[8:10]
        tail_ref[0, :, window] = cells[patch_rows - 8 :]
        tail_ref[0, at : at + 2, spare] = cells[patch_rows - 10 : patch_rows - 8]


def warp_rows(first, count, turn, got, taps, shift, patch_rows):
    depth = got.shape[2]
    width = (depth // 2 + 1) * lane
    span = width + folded(width // lane) * lane
    edge = jax.ShapeDtypeStruct((count, 8, span), jnp.float32)
    return pl.pallas_call(
        functools.partial(warp_kernel, first),
        out_shape=(jax.ShapeDtypeStruct((count, patch_rows, width), jnp.float32), edge, edge),
        grid=(count,),
        in_specs=[
            pl.BlockSpec(memory_space=pltpu.SMEM),
            pl.BlockSpec(memory_space=pl.ANY),
            pl.BlockSpec((1,) + taps.shape[1:], lambda q: (q + first, 0, 0)),
            pl.BlockSpec((1,) + shift.shape[1:], lambda q: (q + first, 0, 0)),
        ],
        out_specs=[
            pl.BlockSpec((1, patch_rows, width), lambda q: (q, 0, 0)),
            *[pl.BlockSpec((1, 8, span), lambda q: (q, 0, 0))] * 2,
        ],
        scratch_shapes=[
            pltpu.VMEM((count, patch_rows // 2 * depth, lane), jnp.float32),
            pltpu.VMEM((2 * patch_rows, width + lane), bf16),
            pltpu.SemaphoreType.DMA((count,)),
        ],
        compiler_params=pltpu.CompilerParams(vmem_limit_bytes=50 << 20),
        cost_estimate=pl.CostEstimate(flops=0, bytes_accessed=12 * count << 20, transcendentals=0),
        name="warp_rows",
    )(turn, got, taps, shift)


def match_kernel(
    first,
    fresh,
    weight_ref,
    warped_ref,
    above_ref,
    below_ref,
    down_ref,
    across_ref,
    coef_ref,
    template_ref,
    before_ref,
    _,
    difference_ref,
    total_ref,
    pieces,
    high_refs,
    low_refs,
    found,
):
    patch_rows, row_width = template_ref.shape
    bases = across_ref.shape[0]
    windows = pieces.shape[1] // lane
    part = high_refs.shape[2] // lane
    tiles = warped_ref.shape[2] // lane
    fold = folded(tiles)
    inside = lax.broadcasted_iota(jnp.int32, (16, lane), 1)
    quarter = lax.broadcasted_iota(jnp.int32, (16, lane), 0) % 8 // 2

    def columns(tile):
        own = warped_ref[0, :, tile * lane : (tile + 1) * lane]
        edges = []
        for at in (tile, tiles + tile % fold):
            here = slice(at * lane, (at + 1) * lane)
            edges.append(jnp.concatenate([above_ref[0, :, here], below_ref[0, :, here]], axis=0))
        edges[1] = jnp.where(quarter == tile // fold, edges[1], 0.0)
        return [own[:16], own[16:], *edges]


    @pl.when(pl.program_id(0) == 0)
    def _():
        total_ref[...] = jnp.zeros_like(total_ref) if fresh else before_ref[...]

    def cut_window(w):
        start = step * w + half_lane - (lane - step) // 2
        tile, turn = start // lane, start % lane
        here = slice(w * lane, (w + 1) * lane)
        blocks = columns(tile)
        if turn:
            blocks = [
                jnp.where(
                    inside < lane - turn,
                    pltpu.roll(before, lane - turn, 1),
                    pltpu.roll(after, lane - turn, 1),
                )
                for before, after in zip(blocks, columns(tile + 1))
            ]
        for i, values in enumerate(blocks):
            high, low = split(values)
            for j, value in enumerate((high, low, high)):
                at = (j * len(blocks) + i) * 16
                pieces[at : at + 16, here] = value

    def part_step(p):
        for w in range(p * part, (p + 1) * part):
            cut_window(w)
        wide = slice(p * part * lane, (p + 1) * part * lane)
        high_ref = high_refs.at[p]
        low_ref = low_refs.at[p]
        vertical = jnp.dot(down_ref[...], pieces[:, wide], preferred_element_type=jnp.float32)
        high_ref[...], low_ref[...] = split(vertical)

        def gathered(ref, b):
            rows = slice(b * patch_rows, (b + 1) * patch_rows)
            return jnp.concatenate(
                [ref[rows, lane * i : lane * (i + 1)] for i in range(part)], axis=0
            )

        matched = jnp.zeros((part * patch_rows, lane), jnp.float32)
        for b in range(bases):
            operand = jnp.concatenate([gathered(high_ref, b), gathered(low_ref, b)], axis=1)
            both = jnp.dot(operand, across_ref[b], preferred_element_type=jnp.float32)
            scales = coef_ref[0, b : b + 1, wide]
            scale = jnp.concatenate(
                [
                    jnp.broadcast_to(scales[:, lane * i : lane * (i + 1)], (patch_rows, lane))
                    for i in range(part)
                ],
                axis=0,
            )
            matched = matched + scale * (both[:, :lane] + both[:, lane:])
        found[p * part * patch_rows : (p + 1) * part * patch_rows, :] = matched

    for p in range(windows // part):
        part_step(p)
    weight = weight_ref[first + pl.program_id(0)]
    inside = lax.broadcasted_iota(jnp.int32, (patch_rows, lane), 1)
    for tile in range(row_width // lane):
        piece = None
        for w in range(tile * lane // step, ((tile + 1) * lane - 1) // step + 1):
            start = step * w - tile * lane
            values = found[w * patch_rows : (w + 1) * patch_rows, :]
            if start % lane:
                values = pltpu.roll(values, start % lane, 1)
            piece = values if piece is None else jnp.where(inside < start, piece, values)
        here = slice(lane * tile, lane * (tile + 1))
        difference_ref[0, :, here] = piece - template_ref[:, here]
        total_ref[:, here] = total_ref[:, here] + weight * piece


def spread_kernel(
    weight_ref,
    warped_ref,
    down_ref,
    across_ref,
    coef_ref,
    coef_up_ref,
    coef_dn_ref,
    template_ref,
    difference_ref,
    total_ref,
    up_ref,
    dn_ref,
    pieces,
    high_refs,
    low_refs,
    found,
):
    patch_rows, row_width = template_ref.shape
    rows_out = patch_rows + 32
    bases = across_ref.shape[0]
    windows = pieces.shape[1] // lane
    part = high_refs.shape[2] // lane
    inside = lax.broadcasted_iota(jnp.int32, (patch_rows, lane), 1)

    @pl.when(pl.program_id(0) == 0)
    def _():
        total_ref[...] = jnp.zeros_like(total_ref)

    for p in range(windows // part):
        for w in range(p * part, (p + 1) * part):
            start = step * w + half_lane - (lane - step) // 2
            tile, turn = start // lane, start % lane
            values = warped_ref[0, :, tile * lane : (tile + 1) * lane]
            if turn:
                after = warped_ref[0, :, (tile + 1) * lane : (tile + 2) * lane]
                values = jnp.where(
                    inside < lane - turn,
                    pltpu.roll(values, lane - turn, 1),
                    pltpu.roll(after, lane - turn, 1),
                )
            high, low = split(values)
            here = slice(w * lane, (w + 1) * lane)
            for j, value in enumerate((high, low, high)):
                pieces[j * patch_rows : (j + 1) * patch_rows, here] = value
        wide = slice(p * part * lane, (p + 1) * part * lane)
        vertical = jnp.dot(down_ref[...], pieces[:, wide], preferred_element_type=jnp.float32)
        high_refs[p], low_refs[p] = split(vertical)

        def gathered(refs, b):
            rows = slice(b * rows_out, (b + 1) * rows_out)
            return jnp.concatenate(
                [refs[p, rows, lane * i : lane * (i + 1)] for i in range(part)], axis=0
            )

        matched = jnp.zeros((part * rows_out, lane), jnp.float32)
        for b in range(bases):
            operand = jnp.concatenate([gathered(high_refs, b), gathered(low_refs, b)], axis=1)
            both = jnp.dot(operand, across_ref[b], preferred_element_type=jnp.float32)
            scales = []
            for w in range(p * part, (p + 1) * part):
                here = slice(w * lane, (w + 1) * lane)
                for ref, count in ((coef_ref, patch_rows), (coef_up_ref, 16), (coef_dn_ref, 16)):
                    scales.append(jnp.broadcast_to(ref[0, b : b + 1, here], (count, lane)))
            matched = matched + jnp.concatenate(scales, axis=0) * (both[:, :lane] + both[:, lane:])
        found[p * part * rows_out : (p + 1) * part * rows_out, :] = matched
    weight = weight_ref[pl.program_id(0)]
    inside = lax.broadcasted_iota(jnp.int32, (rows_out, lane), 1)
    tiles = row_width // lane
    fold = folded(tiles)
    for tile in range(tiles):
        piece = None
        for w in range(tile * lane // step, ((tile + 1) * lane - 1) // step + 1):
            start = step * w - tile * lane
            values = found[w * rows_out : (w + 1) * rows_out, :]
            if start % lane:
                values = pltpu.roll(values, start % lane, 1)
            piece = values if piece is None else jnp.where(inside < start, piece, values)
        here = slice(lane * tile, lane * (tile + 1))
        own, above, below = piece[:patch_rows], piece[patch_rows : patch_rows + 16], piece[-16:]
        difference_ref[0, :, here] = own - template_ref[:, here]
        total_ref[:, here] = total_ref[:, here] + weight * own
        at = 2 * (tile // fold)
        spare = slice((tiles + tile % fold) * lane, (tiles + tile % fold + 1) * lane)
        up_ref[0, :, here] = above[8:]
        up_ref[0, at : at + 2, spare] = above[6:8]
        dn_ref[0, :, here] = below[:8]
        dn_ref[0, at : at + 2, spare] = below[8:10]


def spread_rows(weights, warped, down, across, coefs, coefs_up, coefs_dn, template):
    count, patch_rows, width = warped.shape
    visits, bases, span = coefs.shape
    row_width = template.shape[1]
    part = span // lane // parts
    edge = row_width + folded(row_width // lane) * lane
    coef_spec = pl.BlockSpec((1, bases, span), lambda q: (q, 0, 0))
    edge_spec = pl.BlockSpec((1, 8, edge), lambda q: (q, 0, 0))
    return pl.pallas_call(
        spread_kernel,
        out_shape=(
            jax.ShapeDtypeStruct((visits, patch_rows, row_width), jnp.float32),
            jax.ShapeDtypeStruct(template.shape, jnp.float32),
            jax.ShapeDtypeStruct((count, 8, edge), jnp.float32),
            jax.ShapeDtypeStruct((count, 8, edge), jnp.float32),
        ),
        grid=(count,),
        in_specs=[
            pl.BlockSpec(memory_space=pltpu.SMEM),
            pl.BlockSpec((1, patch_rows, width), lambda q: (q, 0, 0)),
            pl.BlockSpec(down.shape, lambda q: (0, 0)),
            pl.BlockSpec(across.shape, lambda q: (0, 0, 0)),
            coef_spec,
            coef_spec,
            coef_spec,
            pl.BlockSpec(template.shape, lambda q: (0, 0)),
        ],
        out_specs=[
            pl.BlockSpec((1, patch_rows, row_width), lambda q: (q, 0, 0)),
            pl.BlockSpec(template.shape, lambda q: (0, 0)),
            edge_spec,
            edge_spec,
        ],
        scratch_shapes=[
            pltpu.VMEM((down.shape[1], span), bf16),
            pltpu.VMEM((parts, down.shape[0], part * lane), bf16),
            pltpu.VMEM((parts, down.shape[0], part * lane), bf16),
            pltpu.VMEM((span // lane * (patch_rows + 32), lane), jnp.float32),
        ],
        compiler_params=pltpu.CompilerParams(vmem_limit_bytes=58 << 20),
        cost_estimate=pl.CostEstimate(flops=0, bytes_accessed=24 * count << 20, transcendentals=0),
        name="spread_rows",
    )(weights, warped, down, across, coefs, coefs_up, coefs_dn, template)


def add_kernel(
    weight_ref, above_ref, below_ref, before_ref, sums_ref, difference_ref, total_ref
):
    _, patch_rows, row_width = before_ref.shape
    tiles = row_width // lane
    fold = folded(tiles)
    weight = weight_ref[pl.program_id(0)]

    @pl.when(pl.program_id(0) == 0)
    def _():
        total_ref[...] = sums_ref[...]

    difference_ref[0, 10 : patch_rows - 10, :] = before_ref[0, 10 : patch_rows - 10, :]
    for tile in range(tiles):
        here = slice(lane * tile, lane * (tile + 1))
        at = 2 * (tile // fold)
        spare = slice((tiles + tile % fold) * lane, (tiles + tile % fold + 1) * lane)
        for first, ref, rows, columns in (
            (0, above_ref, slice(0, 8), here),
            (8, above_ref, slice(at, at + 2), spare),
            (patch_rows - 10, below_ref, slice(at, at + 2), spare),
            (patch_rows - 8, below_ref, slice(0, 8), here),
        ):
            values = ref[0, rows, columns]
            to = slice(first, first + rows.stop - rows.start)
            difference_ref[0, to, here] = before_ref[0, to, here] + values
            total_ref[to, here] = total_ref[to, here] + weight * values


def add_edges(weights, above, below, difference, total):
    count, _, edge = above.shape
    _, patch_rows, row_width = difference.shape
    row_spec = pl.BlockSpec((1, patch_rows, row_width), lambda q: (q, 0, 0))
    edge_spec = pl.BlockSpec((1, 8, edge), lambda q: (q, 0, 0))
    total_spec = pl.BlockSpec(total.shape, lambda q: (0, 0))
    return pl.pallas_call(
        add_kernel,
        out_shape=(
            jax.ShapeDtypeStruct(difference.shape, jnp.float32),
            jax.ShapeDtypeStruct(total.shape, jnp.float32),
        ),
        grid=(count,),
        in_specs=[
            pl.BlockSpec(memory_space=pltpu.SMEM),
            edge_spec,
            edge_spec,
            row_spec,
            total_spec,
        ],
        out_specs=[row_spec, total_spec],
        input_output_aliases={3: 0},
        compiler_params=pltpu.CompilerParams(vmem_limit_bytes=52 << 20),
        cost_estimate=pl.CostEstimate(flops=0, bytes_accessed=3 * count << 20, transcendentals=0),
        name="add_edges",
    )(weights, above, below, difference, total)


def match_rows(
    first, weights, warped, above, below, down, across, coefs, template, before, difference
):
    count, _, width = warped.shape
    edge = above.shape[2]
    visits, bases, span = coefs.shape
    patch_rows, row_width = template.shape
    part = span // lane // parts
    fresh = before is None
    if fresh:
        before = template
    extra, aliases = [], {}
    if difference is not None:
        extra, aliases = [difference], {9: 0}
    kernel = functools.partial(match_kernel, first, fresh)
    if difference is None:

        def body(*refs):
            kernel(*refs[:9], None, *refs[9:])

    else:
        body = kernel
    rows_spec = pl.BlockSpec(template.shape, lambda q: (0, 0))
    return pl.pallas_call(
        body,
        out_shape=(
            jax.ShapeDtypeStruct((visits, patch_rows, row_width), jnp.float32),
            jax.ShapeDtypeStruct(template.shape, jnp.float32),
        ),
        grid=(count,),
        in_specs=[
            pl.BlockSpec(memory_space=pltpu.SMEM),
            pl.BlockSpec((1, patch_rows, width), lambda q: (q, 0, 0)),
            *[pl.BlockSpec((1, 8, edge), lambda q: (q, 0, 0))] * 2,
            pl.BlockSpec(down.shape, lambda q: (0, 0)),
            pl.BlockSpec(across.shape, lambda q: (0, 0, 0)),
            pl.BlockSpec((1, bases, span), lambda q: (q + first, 0, 0)),
            rows_spec,
            rows_spec,
        ]
        + [pl.BlockSpec(memory_space=pl.ANY)] * len(extra),
        out_specs=[
            pl.BlockSpec((1, patch_rows, row_width), lambda q: (q + first, 0, 0)),
            rows_spec,
        ],
        scratch_shapes=[
            pltpu.VMEM((down.shape[1], span), bf16),
            pltpu.VMEM((parts, down.shape[0], part * lane), bf16),
            pltpu.VMEM((parts, down.shape[0], part * lane), bf16),
            pltpu.VMEM((span // lane * patch_rows, lane), jnp.float32),
        ],
        input_output_aliases=aliases,
        compiler_params=pltpu.CompilerParams(vmem_limit_bytes=48 << 20),
        cost_estimate=pl.CostEstimate(flops=0, bytes_accessed=20 * count << 20, transcendentals=0),
        name="match_rows",
    )(weights, warped, above, below, down, across, coefs, template, before, *extra)


def sum_kernel(total_ref, scale_ref, out_ref, slots, send_sems, recv_sems):
    me = lax.axis_index("visit")
    slabs = lax.axis_size("visit")
    rows = out_ref.shape[0]
    mesh_ids = pl.DeviceIdType.MESH
    barrier = pltpu.get_barrier_semaphore()
    for i in range(1, slabs):
        to = lax.rem(me + i, slabs)
        pl.semaphore_signal(barrier, inc=1, device_id={"visit": to}, device_id_type=mesh_ids)
    pl.semaphore_wait(barrier, slabs - 1)
    copies = []
    for i in range(1, slabs):
        to = lax.rem(me + i, slabs)
        copy = pltpu.make_async_remote_copy(
            src_ref=total_ref.at[pl.ds(pl.multiple_of(rows * to, rows), rows), :],
            dst_ref=slots.at[i - 1],
            send_sem=send_sems.at[i - 1],
            recv_sem=recv_sems.at[i - 1],
            device_id={"visit": to},
            device_id_type=mesh_ids,
        )
        copy.start()
        copies.append(copy)
    for copy in copies:
        copy.wait()
    result = total_ref[pl.ds(pl.multiple_of(rows * me, rows), rows), :]
    for i in range(slabs - 1):
        result = result + slots[i]
    out_ref[...] = result / scale_ref[0]


def sum_visits(total, scale):
    slabs = lax.axis_size("visit")
    shape = (total.shape[0] // slabs, total.shape[1])
    return pl.pallas_call(
        sum_kernel,
        out_shape=jax.ShapeDtypeStruct(shape, jnp.float32),
        in_specs=[
            pl.BlockSpec(memory_space=pltpu.VMEM),
            pl.BlockSpec(memory_space=pltpu.SMEM),
        ],
        out_specs=pl.BlockSpec(memory_space=pltpu.VMEM),
        scratch_shapes=[
            pltpu.VMEM((slabs - 1,) + shape, jnp.float32),
            pltpu.SemaphoreType.DMA((slabs - 1,)),
            pltpu.SemaphoreType.DMA((slabs - 1,)),
        ],
        compiler_params=pltpu.CompilerParams(
            collective_id=0, has_side_effects=True, vmem_limit_bytes=16 << 20
        ),
        name="sum_visits",
    )(total, scale)


def split_table(values):
    high = lax.reduce_precision(values, 8, 7)
    return high.astype(bf16), (values - high).astype(bf16)


def taken(values, index):
    table = jnp.zeros((values.shape[0],) + index.shape, jnp.float32)
    for lag in range(values.shape[1]):
        table = jnp.where((index == lag)[None], values[:, lag].reshape(-1, 1, 1), table)
    return table


def on_device(
    ccd_rows,
    tract_row,
    warp_taps,
    warp_shift,
    basis_rows,
    basis_cols,
    coef_table,
    grid_index,
    template,
    visit_weight,
):
    visits, patch_rows, row_width = ccd_rows.shape
    patches = lax.axis_size("patch")
    here = lax.axis_index("patch")
    half = basis_rows.shape[1] // 2
    tiles = row_width // lane

    tiled_rows = ccd_rows.reshape(visits, patch_rows // 8, 8, tiles, lane).transpose(0, 1, 3, 2, 4)
    tiled_rows = tiled_rows.reshape(visits, patch_rows * tiles, lane)
    place = tract_row[0, 0]
    offset = place // patch_rows - here - (place % patch_rows) // 2
    turn = ((here - offset) % patches).astype(jnp.int32).reshape(1)
    taps = jnp.pad(warp_taps[:, 0], ((0, 0), (0, 0), (half_lane, half_lane)))
    shift = jnp.pad(warp_shift, ((0, 0), (0, 0), (half_lane, half_lane)))

    def windowed_coefs(table, grid):
        windows = -(-row_width // step)
        cells = jnp.pad(grid, (0, windows * step - row_width)).reshape(windows, step)
        cells = jnp.pad(cells, ((0, 0), (0, lane - step))).reshape(-1)
        one_hot = (cells[None, :] == jnp.arange(table.shape[2])[:, None]).astype(jnp.float32)
        return jnp.einsum("qbg,gx->qbx", table, one_hot, precision=lax.Precision.HIGHEST)

    down_pairs = [(i, i + 1) for i in range(patches - 1)]
    up_pairs = [(i + 1, i) for i in range(patches - 1)]
    table = coef_table[:, 0]
    coefs = windowed_coefs(table, grid_index[0])

    rows = jnp.arange(patch_rows)
    pair = jnp.arange(8)
    inner = jnp.concatenate(
        [rows, pair - 8, pair + patch_rows, pair % 2 - half, pair % 2 + patch_rows + half - 2]
    )
    down = taken(basis_rows, inner[None, :] - rows[:, None] + half).reshape(-1, inner.shape[0])
    down_high, down_low = split_table(down)
    down = jnp.concatenate([down_high, down_high, down_low], axis=1)
    outer = jnp.concatenate([rows, jnp.arange(16) - 16, jnp.arange(16) + patch_rows])
    wide = taken(basis_rows, rows[None, :] - outer[:, None] + half).reshape(-1, patch_rows)
    wide_high, wide_low = split_table(wide)
    wide = jnp.concatenate([wide_high, wide_high, wide_low], axis=1)
    out = jnp.arange(lane)[None, :]
    across = taken(
        basis_cols, jnp.where(out < step, jnp.arange(lane)[:, None] - out, basis_cols.shape[1])
    )
    high, low = split_table(across)
    across = jnp.concatenate(
        [
            jnp.concatenate([high, low], axis=2),
            jnp.concatenate([high, jnp.zeros_like(low)], axis=2),
        ],
        axis=1,
    )
    weights = lax.dynamic_slice_in_dim(
        visit_weight, lax.axis_index("visit") * visits, visits
    )

    early, late = chunks
    sent = [
        pack_rows(first, count, tract_row, tiled_rows, patches)
        for first, count in ((0, early), (early, late))
    ]
    packed = jnp.concatenate([table.reshape(-1), grid_index[0].astype(jnp.float32)])
    nearby = [lax.ppermute(packed, "patch", pairs) for pairs in (down_pairs, up_pairs)]
    sent[1], down, wide, across, coefs, taps, shift, weights, turn, nearby = (
        lax.optimization_barrier(
            (sent[1], down, wide, across, coefs, taps, shift, weights, turn, nearby)
        )
    )
    got = [lax.all_to_all(block, "patch", split_axis=0, concat_axis=0, tiled=True) for block in sent]

    def neighbour_coefs(values):
        cells = values[table.size :].astype(jnp.int32)
        return windowed_coefs(values[: table.size].reshape(table.shape), cells)

    warped, _, _ = warp_rows(0, early, turn, got[0], taps, shift, patch_rows)
    difference, total, up, dn = spread_rows(
        weights,
        warped,
        wide,
        across,
        coefs,
        *map(neighbour_coefs, nearby),
        template,
    )
    from_above = lax.ppermute(dn, "patch", down_pairs)
    from_below = lax.ppermute(up, "patch", up_pairs)
    turn, total = lax.optimization_barrier((turn, total))
    warped, head, tail = warp_rows(early, late, turn, got[1], taps, shift, patch_rows)
    head, tail, from_above, from_below = lax.optimization_barrier(
        (head, tail, from_above, from_below)
    )
    above = lax.ppermute(tail, "patch", down_pairs)
    below = lax.ppermute(head, "patch", up_pairs)
    difference, total = add_edges(weights, from_above, from_below, difference, total)
    difference, total = match_rows(
        early, weights, warped, above, below, down, across, coefs, template, total, difference
    )
    coadd = sum_visits(total, jnp.sum(visit_weight).reshape(1))
    return difference, coadd


def solution(mesh):
    placed = (
        P("visit", "patch", None),
        P("visit", "patch"),
        P("visit", "patch", None, None),
        P("visit", "patch", None),
        P(),
        P(),
        P("visit", "patch", None, None),
        P("patch", None),
        P("patch", None),
        P(),
    )
    return jax.shard_map(
        on_device,
        mesh=mesh,
        in_specs=placed,
        out_specs=(P("visit", "patch", None), P(("patch", "visit"), None)),
        check_vma=False,
    )
```
